128 devices in a mesh: ka: 16 (over y, z), cfg: 8 (over x, core).
Axes of the slice: x: 4, y: 4, z: 4, core: 2. Of those that a mesh axis runs over, the one named last changes fastest.
Arguments:
- medium_t: float32 [2, 2, 16, 16, 16], replicated, may hold values from -6 to 6
- structure: float32 [2, 2, 16, 16, 16384], P(None, None, None, None, ('ka', 'cfg')), may hold values from -0.12 to 0.12
- kmap: int32 [16384], P(('ka', 'cfg')), may hold values from 0 to 15, as said below
- occupation: int32 [128, 16], P(('ka', 'cfg')), may hold values from 0 to 1
- cfg_weight: float32 [128], P(('ka', 'cfg')), may hold values from 1 to 30
- shift_a: float32 [2, 2, 16, 16], replicated, may hold values from -0.18 to 0.18
- shift_b: float32 [2, 2, 16, 16], replicated, may hold values from -0.18 to 0.18
Outputs:
- coarse_tau: float32 [2, 2, 16, 16, 16], replicated
- avg_tau: float32 [2, 2, 256, 256], P(None, None, 'cfg')
- correction: float32 [2, 2, 16384], P(None, None, ('ka', 'cfg'))
The draws below stay inside these ranges and needn't reach their ends.
Inputs may be any that keep to these rules, and one draw needn't show every extreme that they name: `kmap`: every cluster momentum is named by exactly 16384 / 16 k-points.
All inputs are finite; a program needn't handle non-finite values.
Results may differ from the reference program's by a relative error of at most 0.00015.
Values sent between devices are 32-bit elements; how exact they have to be, the bound alone decides.
A program may use at most 128 MiB of HBM per device.

```python
import math
import jax
import jax.numpy as jnp
from jax import lax

NC = 16
LM = 16
ENERGIES = 2
TERMS = 3
CFD = 1
NK = 16
KPTS = 16384
NCFG = 128


def draw_kmap(key, part):
    order_k = jax.random.permutation(key, KPTS)
    return (order_k % NK).astype(jnp.int32)


def draw_cfg_weight(key, part):
    base = jax.random.uniform(key, (NCFG,), jnp.float32)
    ramp = 1.0 + 2.0 * jnp.arange(NCFG, dtype=jnp.float32) / max(NCFG - 1, 1)
    scaled = jnp.exp(base * math.log(3.0))
    return scaled * ramp


def touch_ends(array, stream_key, smallest, top_value):
    spot = [jax.random.randint(jax.random.fold_in(stream_key, axis), (), 0, length) for axis, length in enumerate(array.shape)]
    longest = array.shape.index(max(array.shape))
    next_to = spot[:longest] + [(spot[longest] + 1) % array.shape[longest]] + spot[longest + 1:]
    return array.at[tuple(spot)].set(smallest).at[tuple(next_to)].set(top_value)


def shard_levels(key, extent, split, low, largest):
    factor_of, own = 1.0, jax.random.fold_in(key, 6)
    for axis_at, parts in split:
        steps = jnp.exp(jax.random.uniform(jax.random.fold_in(own, axis_at), (parts,), jnp.float32, low / len(split), largest / len(split)))
        factor_of = factor_of * jnp.repeat(steps, extent[axis_at] // parts).reshape([-1 if axis == axis_at else 1 for axis in range(len(extent))])
    return factor_of


def scatter_about(rng, extent, width, reach, split=(), kind=jnp.bfloat16):
    values = width * jax.random.normal(rng, extent, jnp.float32)
    if split:
        values = values * shard_levels(rng, extent, split, -0.22, 0.18)
    return jnp.clip(values, -reach, reach).astype(kind)


def setup_inputs(seed: int = 0) -> dict:
    streams_of = jax.random.split(jax.random.key(seed), 8)
    return {
        "medium_t": scatter_about(streams_of[0], (ENERGIES, 2, LM, LM, NK), 1.0, 6.0, (), jnp.float32),
        "structure": scatter_about(streams_of[1], (ENERGIES, 2, LM, LM, KPTS), 0.02, 0.12, ((4, 128),), jnp.float32),
        "kmap": draw_kmap(jax.random.fold_in(streams_of[7], 71), 0),
        "occupation": touch_ends(jax.random.randint(streams_of[3], (NCFG, NC), 0, 2), jax.random.fold_in(streams_of[3], 1), 0, 1).astype(jnp.int32),
        "cfg_weight": draw_cfg_weight(jax.random.fold_in(streams_of[7], 71), 0),
        "shift_a": scatter_about(streams_of[5], (ENERGIES, 2, LM, LM), 0.03, 0.18, (), jnp.float32),
        "shift_b": scatter_about(streams_of[6], (ENERGIES, 2, LM, LM), 0.03, 0.18, (), jnp.float32),
    }


HIGH = lax.Precision.HIGHEST


def phase_tables(count_sites):
    places = jnp.arange(count_sites, dtype=jnp.int32)
    half_n = count_sites // 2
    cell = places % half_n
    site_xyz = jnp.stack([cell // 4, (cell // 2) % 2, cell % 2], axis=1).astype(jnp.float32)
    site_xyz = site_xyz + 0.5 * (places >= half_n).astype(jnp.float32)[:, None]
    mom_hkl = jnp.stack([places // 4, (places // 2) % 2, places % 2], axis=1).astype(jnp.float32)
    angles = math.pi * jnp.sum(mom_hkl[:, None, :] * site_xyz[None, :, :], axis=2)
    differ = angles[:, :, None] - angles[:, None, :]
    return jnp.cos(differ), jnp.sin(differ)


def batch_mul(first_m, second_m):
    def single(left_m, right_m):
        return jnp.einsum("abk,bck->ack", left_m, right_m, precision=HIGH)
    return jnp.stack([single(first_m[0], second_m[0]) - single(first_m[1], second_m[1]),
                      single(first_m[0], second_m[1]) + single(first_m[1], second_m[0])])


def batch_trace(first_m, second_m):
    def single(left_m, right_m):
        return jnp.einsum("abk,bak->k", left_m, right_m, precision=HIGH)
    return jnp.stack([single(first_m[0], second_m[0]) - single(first_m[1], second_m[1]),
                      single(first_m[0], second_m[1]) + single(first_m[1], second_m[0])])


def momentum_onehot(kmap, count_moms):
    return (kmap[None, :] == jnp.arange(count_moms, dtype=jnp.int32)[:, None]).astype(jnp.float32)


def kpoint_terms(medium, structure, onehot):
    spread_m = jnp.einsum("xabm,mk->xabk", medium, onehot, precision=HIGH)
    factor_m = batch_mul(spread_m, structure)
    second_t = batch_mul(factor_m, spread_m)
    third_t = batch_mul(factor_m, second_t)
    kpoint_tau = spread_m + second_t + third_t
    partial_sum = jnp.einsum("xabk,mk->xabm", kpoint_tau, onehot, precision=HIGH)
    return partial_sum, batch_mul(kpoint_tau, kpoint_tau)


def to_cluster(moment_tau, cosine, sine_tab):
    count_sites = cosine.shape[1]
    chans = moment_tau.shape[1]

    def apply_phase(table, block):
        return jnp.einsum("mij,abm->iajb", table, block, precision=HIGH)
    real_part = (apply_phase(cosine, moment_tau[0]) - apply_phase(sine_tab, moment_tau[1])) / count_sites
    imag_part = (apply_phase(cosine, moment_tau[1]) + apply_phase(sine_tab, moment_tau[0])) / count_sites
    order_n = count_sites * chans
    return jnp.stack([real_part.reshape(order_n, order_n), imag_part.reshape(order_n, order_n)])


def to_moment(cluster_rows, cosine_rows, sine_rows):
    count_sites = cosine_rows.shape[2]
    chans = cluster_rows.shape[2] // count_sites
    real_in = cluster_rows[0].reshape(-1, chans, count_sites, chans)
    imag_in = cluster_rows[1].reshape(-1, chans, count_sites, chans)

    def apply_phase(table, block):
        return jnp.einsum("mij,iajb->abm", table, block, precision=HIGH)
    real_part = (apply_phase(cosine_rows, real_in) + apply_phase(sine_rows, imag_in)) / count_sites
    imag_part = (apply_phase(cosine_rows, imag_in) - apply_phase(sine_rows, real_in)) / count_sites
    return jnp.stack([real_part, imag_part])


def impurity_sum(cluster, shift_first, shift_second, occupied, weights):
    count_cfg, count_sites = occupied.shape
    order_n = cluster.shape[1]
    chans = order_n // count_sites
    share = occupied.astype(jnp.float32)[None, :, :, None, None]
    delta = share * shift_first[:, None, None] + (1.0 - share) * shift_second[:, None, None]
    current = jnp.broadcast_to(cluster[:, None], (2, count_cfg, order_n, order_n))

    def site_mul(left_m, right_m):
        return jnp.einsum("gsab,gsbc->gsac", left_m, right_m, precision=HIGH)

    def left_mul(left_m, right_m):
        return jnp.einsum("ij,gjc->gic", left_m, right_m, precision=HIGH)
    for sweep_idx in range(TERMS):
        blocks = current.reshape(2, count_cfg, count_sites, chans, order_n)
        scattered = jnp.stack([site_mul(delta[0], blocks[0]) - site_mul(delta[1], blocks[1]),
                               site_mul(delta[0], blocks[1]) + site_mul(delta[1], blocks[0])])
        scattered = scattered.reshape(2, count_cfg, order_n, order_n)
        product = jnp.stack([left_mul(cluster[0], scattered[0]) - left_mul(cluster[1], scattered[1]),
                             left_mul(cluster[0], scattered[1]) + left_mul(cluster[1], scattered[0])])
        current = cluster[:, None] - product
    return jnp.einsum("g,xgij->xij", weights, current, precision=HIGH)


def reference(medium_t, structure, kmap, occupation, cfg_weight, shift_a, shift_b):
    cosine, sine_tab = phase_tables(NC)
    onehot = momentum_onehot(kmap, NK)
    per_moment = KPTS // NK
    weight_total = jnp.sum(cfg_weight)
    occ_blocks = occupation.reshape(-1, CFD, NC)
    weight_blocks = cfg_weight.reshape(-1, CFD)
    coarse_list = []
    average_list = []
    correct_list = []
    for energy in range(ENERGIES):
        partial_sum, squared = kpoint_terms(medium_t[energy], structure[energy], onehot)
        coarse = partial_sum / per_moment
        cluster = to_cluster(coarse, cosine, sine_tab)

        def one_block(block_pair):
            return impurity_sum(cluster, shift_a[energy], shift_b[energy], block_pair[0], block_pair[1])
        sums = lax.map(one_block, (occ_blocks, weight_blocks))
        average = jnp.sum(sums, axis=0) / weight_total
        diff_moment = to_moment(average, cosine, sine_tab) - coarse
        spread_d = jnp.einsum("xabm,mk->xabk", diff_moment, onehot, precision=HIGH)
        coarse_list.append(coarse)
        average_list.append(average)
        correct_list.append(batch_trace(spread_d, squared))
    return jnp.stack(coarse_list), jnp.stack(average_list), jnp.stack(correct_list)
```

```python
import functools

import jax
import jax.numpy as jnp
from jax import lax
from jax.experimental import pallas as pl
from jax.experimental.pallas import tpu as pltpu
from jax.sharding import PartitionSpec as P

MESH = pl.DeviceIdType.MESH
F32 = jnp.float32
BF16 = jnp.bfloat16
NN = (((1,), (0,)), ((), ()))
NT = (((1,), (1,)), ((), ()))

ENERGIES = 2
SITES = 16
CHANS = 16
MOMS = 16
WIDE = SITES * CHANS
LANES = 128
ALPHA = 24


def split(x):
    high = x.astype(BF16)
    return high, (x - high.astype(F32)).astype(BF16)


def dot(left, right, dims=NN):
    return lax.dot_general(left, right, dims, preferred_element_type=F32)


def dot_exact(x, right, dims=NN):
    high, low = split(x)
    return dot(high, right, dims) + dot(low, right, dims)


def dot3(x, right, dims=NN):
    high, low = split(x)
    return dot(high, right[0], dims) + (dot(low, right[0], dims) + dot(high, right[1], dims))


def cdot(x, right, dims=NN):
    rows = x[0].shape[0]
    both = jnp.concatenate([x[0], x[1]], axis=0)
    by_re = dot3(both, right[0], dims)
    by_im = dot3(both, right[1], dims)
    return by_re[:rows] - by_im[rows:], by_im[:rows] + by_re[rows:]


def csplit(x):
    return split(x[0]), split(x[1])


def iota(shape, axis):
    return lax.broadcasted_iota(jnp.int32, shape, axis)


def tile_rows(x, times):
    return jnp.concatenate([x] * times, axis=0)


def quarter_turns(mom, site):
    half = site >> 3
    x = 2 * ((site >> 2) & 1) + half
    y = 2 * ((site >> 1) & 1) + half
    z = 2 * (site & 1) + half
    return ((mom >> 2) * x + ((mom >> 1) & 1) * y + (mom & 1) * z) & 3


def cos_sin(turns):
    sign = (1 - (turns & 2)).astype(F32)
    odd = (turns & 1) == 1
    return jnp.where(odd, 0.0, sign), jnp.where(odd, sign, 0.0)


def site_sum(first, second):
    carry = (first & second) >> 3
    return (first ^ second) ^ (7 * carry)


class Tables:
    def __init__(self):
        rows, cols = iota((WIDE, WIDE), 0), iota((WIDE, WIDE), 1)
        self.row_block, self.col_block = rows >> 4, cols >> 4
        self.row_in, self.col_in = rows & 15, cols & 15
        self.same_block = self.row_block == self.col_block
        self.same_in = self.row_in == self.col_in
        self.cos, self.sin = cos_sin(quarter_turns(self.col_block, self.row_block))
        self.wave_cos = jnp.where(self.same_in, self.cos, 0.0).astype(BF16)
        self.wave_sin = jnp.where(self.same_in, self.sin, 0.0).astype(BF16)
        small_r, small_c = iota((SITES, WIDE), 0), iota((SITES, WIDE), 1)
        self.pick_in = (small_r == (small_c & 15)).astype(F32).astype(BF16)
        self.pick_block = (small_r == (small_c >> 4)).astype(F32).astype(BF16)


def block_diag(panel, tab):
    def spread(part):
        return jnp.where(tab.same_block, tile_rows(part.astype(F32), SITES), 0.0).astype(BF16)

    high, low = split(panel)
    return spread(high), spread(low)


def block_diag_c(panel, tab):
    return block_diag(panel[0], tab), block_diag(panel[1], tab)


def kpoint_mul(store, left, right, times=(1.0,)):
    def body(a, carry):
        re = jnp.zeros((CHANS, LANES), F32)
        im = jnp.zeros((CHANS, LANES), F32)
        for b in range(CHANS):
            lr = left[0, a, pl.ds(b, 1), :]
            li = left[1, a, pl.ds(b, 1), :]
            rr = right[0, b]
            ri = right[1, b]
            re = re + (lr * rr - li * ri)
            im = im + (lr * ri + li * rr)
        store(a, re, im)
        return carry

    lax.fori_loop(0, CHANS, body, 0)


def spread_medium(medium, kmap, spread):
    onehot = (iota((MOMS, LANES), 0) == kmap[...]).astype(F32).astype(BF16)
    for e in range(ENERGIES):
        for c in range(2):
            flat = medium[e, c].reshape(WIDE, MOMS)
            spread[e, c] = dot_exact(flat, onehot).reshape(CHANS, CHANS, LANES)


def kpoint_sums(structure, spread, factor, inner, kmap, write_tile):
    for e in range(ENERGIES):
        y, g, f, h = spread.at[e], structure.at[e], factor.at[e], inner.at[e]

        def put_f(a, re, im, f=f):
            f[0, a] = re
            f[1, a] = im

        def put_h(a, re, im, h=h, g=g):
            h[0, a] = g[0, a] + re
            h[1, a] = g[1, a] + im

        kpoint_mul(put_f, y, g)
        kpoint_mul(put_h, g, f)
    rows, lanes = iota((WIDE, LANES), 0), kmap[...]
    onehot_t = ((rows >> 4) == lanes).astype(F32).astype(BF16)
    row_block = iota((WIDE, WIDE), 0) >> 4
    col_in = iota((WIDE, WIDE), 1) & 15
    keep = row_block == col_in
    for e in range(ENERGIES):
        for c in range(2):
            flat = inner[e, c].reshape(WIDE, LANES)
            by_mom = jnp.where(keep, dot_exact(flat, onehot_t, NT), 0.0)
            panel = jnp.sum(by_mom.reshape(CHANS, CHANS, WIDE), axis=0)
            for half in range(2):
                for side in range(2):
                    write_tile(
                        ((e * 2 + c) * 2 + half) * 2 + side,
                        panel[half * 8 : half * 8 + 8, side * LANES : side * LANES + LANES],
                    )


def kpoint_squares(spread, factor, tau, square):
    for e in range(ENERGIES):
        y, f, t, s = spread.at[e], factor.at[e], tau.at[e], square.at[e]

        def put_q(a, re, im, s=s, f=f):
            s[0, a] = f[0, a] + re
            s[1, a] = f[1, a] + im

        def put_t(a, re, im, t=t, y=y):
            t[0, a] = y[0, a] + re
            t[1, a] = y[1, a] + im

        def put_s(a, re, im, s=s):
            s[0, a] = re
            s[1, a] = im

        kpoint_mul(put_q, f, f)
        kpoint_mul(put_t, s, y)
        kpoint_mul(put_s, t, t)


def config_row(occupation, weight, row):
    lane = iota((8, LANES), 1)
    row[...] = jnp.where(lane == SITES, 1.0, 0.0) + jnp.where(
        lane == SITES + 1, weight[0], 0.0
    )
    row[:, 0:SITES] = jnp.broadcast_to(occupation[...].astype(F32), (8, SITES))


def moment_tables(configs, tab, rows_tab, shift_tab):
    turned = jnp.transpose(configs)
    count = turned[0:ALPHA]
    weight = turned[SITES + 1 : SITES + 2]
    weight = weight / jnp.sum(weight, axis=1, keepdims=True)
    live = iota((ALPHA, LANES), 0) <= SITES
    count = jnp.where(live, count, 0.0)
    weighted = count * weight
    flat = configs.astype(BF16)
    lane_r, lane_c = iota((LANES, WIDE), 0), iota((LANES, WIDE), 1)
    pick = (lane_r == (lane_c >> 4)).astype(F32).astype(BF16)
    wide = dot(flat, pick).astype(BF16)
    ones = jnp.ones((LANES, LANES), BF16)
    for s in range(SITES + 1):
        product = weighted * count[s : s + 1]
        rows_tab[s, :, 0:WIDE] = dot_exact(product, wide)
        rows_tab[s, :, WIDE : WIDE + LANES] = dot_exact(product, ones)
    r, c = iota((WIDE, LANES), 0), iota((WIDE, LANES), 1)
    move = (site_sum(r >> 4, r & 15) == c).astype(F32).astype(BF16)
    moved = dot(move, flat, NT)
    moved_b = moved.astype(BF16)
    own = dot(((r >> 4) == c).astype(F32).astype(BF16), flat, NT)
    base = moved * (weight * (1.0 / SITES))
    fold = (tab.row_in == tab.col_block).astype(F32).astype(BF16)
    for which, left in ((0, base), (1, base * own)):
        full = dot_exact(left, moved_b, NT)
        kept = jnp.where(tab.same_block, full, 0.0)
        small = jnp.sum(kept.reshape(SITES, SITES, WIDE), axis=0)
        lanes = dot_exact(small, fold)
        shift_tab[which] = jnp.broadcast_to(
            lanes[:, None, :], (SITES, CHANS, WIDE)
        ).reshape(WIDE, WIDE)


def medium_panels(medium, tab, e):
    out = []
    for c in range(2):
        flat = medium[e, c].reshape(WIDE, MOMS)
        pick = ((iota((MOMS, WIDE), 1) >> 4) == iota((MOMS, WIDE), 0)).astype(F32).astype(BF16)
        by_mom = jnp.where(tab.same_in, dot_exact(flat, pick), 0.0)
        out.append(jnp.sum(by_mom.reshape(CHANS, CHANS, WIDE), axis=1))
    return tuple(out)


def shift_panels(shift_a, shift_b, tab, e):
    def wide(x):
        return dot_exact(x, tab.pick_in)

    b = (wide(shift_b[e, 0]), wide(shift_b[e, 1]))
    c = (
        wide(shift_a[e, 0] - shift_b[e, 0]),
        wide(shift_a[e, 1] - shift_b[e, 1]),
    )
    return b, c


def coarse_panel(y, sum_t, tab, per_moment):
    left = cdot(y, block_diag_c(sum_t, tab), NT)
    both = cdot(left, block_diag_c(y, tab))
    scale = 1.0 / per_moment
    return y[0] + scale * both[0], y[1] + scale * both[1]


def cluster_matrix(x, tab):
    re, im = tile_rows(x[0], SITES), tile_rows(x[1], SITES)
    scale = 1.0 / SITES
    left_r = (re * tab.cos - im * tab.sin) * scale
    left_i = (re * tab.sin + im * tab.cos) * scale
    real = dot_exact(left_r, tab.wave_cos, NT) + dot_exact(left_i, tab.wave_sin, NT)
    imag = dot_exact(left_i, tab.wave_cos, NT) - dot_exact(left_r, tab.wave_sin, NT)
    return real, imag


def rows_stage(cluster, t_parts, b_parts, c_parts, rows_tab, site0, chan):
    def own(ref):
        first = ref[pl.ds(site0 * CHANS + chan, 1), :]
        second = ref[pl.ds((site0 + 1) * CHANS + chan, 1), :]
        return jnp.concatenate(
            [jnp.broadcast_to(first, (8, WIDE)), jnp.broadcast_to(second, (8, WIDE))], axis=0
        )

    start = (own(cluster[0]), own(cluster[1]))
    with_b = cdot(start, b_parts)
    with_c = cdot(start, c_parts)
    row = iota((ALPHA, WIDE), 0)
    block = iota((ALPHA, WIDE), 1) >> 4

    def opened(c):
        out = []
        for at in (0, 8):
            ub = jnp.broadcast_to(with_b[c][at : at + 1], (ALPHA, WIDE))
            uc = jnp.broadcast_to(with_c[c][at : at + 1], (ALPHA, WIDE))
            out.append(jnp.where(row == block, uc, jnp.where(row == SITES, ub, 0.0)))
        return jnp.concatenate(out, axis=0)

    hop = cdot((opened(0), opened(1)), t_parts)
    plain, dressed = [[], []], [[], []]
    for c in range(2):
        for site in range(2):
            f = jnp.zeros((ALPHA, WIDE), F32)
            h = jnp.zeros((ALPHA, WIDE), F32)
            for s in range(SITES + 1):
                line = hop[c][site * ALPHA + s : site * ALPHA + s + 1]
                pair = rows_tab[s, :, WIDE : WIDE + LANES]
                f = f + jnp.concatenate([pair, pair], axis=1) * line
                h = h + rows_tab[s, :, 0:WIDE] * line
            plain[c].append(f)
            dressed[c].append(h)
    plain = tuple(jnp.concatenate(p, axis=0) for p in plain)
    dressed = tuple(jnp.concatenate(d, axis=0) for d in dressed)
    by_b = cdot(plain, b_parts)
    by_c = cdot(dressed, c_parts)
    inner = (by_b[0] + by_c[0], by_b[1] + by_c[1])
    second = cdot(inner, t_parts)
    mean = rows_tab[SITES, SITES : SITES + 1, 0:WIDE]

    def eight(parts):
        return jnp.concatenate([jnp.broadcast_to(p, (8, WIDE)) for p in parts], axis=0)

    for_b, for_c, rest = [], [], []
    for c in range(2):
        last_b, last_c, known = [], [], []
        for site in range(2):
            lines = second[c][site * ALPHA : site * ALPHA + ALPHA]
            picked = jnp.sum(jnp.where(row == block, lines, 0.0), axis=0, keepdims=True)
            last_b.append(lines[SITES : SITES + 1])
            last_c.append(picked)
            known.append(
                with_b[c][site * 8 : site * 8 + 1]
                + with_c[c][site * 8 : site * 8 + 1] * mean
                - inner[c][site * ALPHA + SITES : site * ALPHA + SITES + 1]
            )
        for_b.append(eight(last_b))
        for_c.append(eight(last_c))
        rest.append(eight(known))
    by_b = cdot(tuple(for_b), b_parts)
    by_c = cdot(tuple(for_c), c_parts)
    z = (rest[0] + by_b[0] + by_c[0], rest[1] + by_b[1] + by_c[1])
    last = cdot(z, t_parts)
    return start[0] - last[0], start[1] - last[1]


def moment_stage(cluster, t_parts, x, x_parts, b_wide, c_wide, b_parts, c_parts, shift_tab, tab):
    top = (cluster[0][0:CHANS, :], cluster[1][0:CHANS, :])
    top_parts = csplit(top)

    def head(wide):
        return wide[0][:, 0:CHANS], wide[1][:, 0:CHANS]

    b_in, c_in = head(b_wide), head(c_wide)
    small = (
        jnp.concatenate([b_in[0], c_in[0]], axis=0),
        jnp.concatenate([b_in[1], c_in[1]], axis=0),
    )
    lead = cdot(small, top_parts)
    lead_b = (lead[0][0:CHANS], lead[1][0:CHANS])
    lead_c = (lead[0][CHANS:], lead[1][CHANS:])
    then_b = cdot(lead, b_parts)
    then_c = cdot(lead, c_parts)
    two = shift_tab[1, 0:1, :]
    mean = shift_tab[1, 0:1, 0:1]

    def mix(c):
        bb, cb = then_b[c][0:CHANS], then_b[c][CHANS:]
        bc, cc = then_c[c][0:CHANS], then_c[c][CHANS:]
        return bb + mean * (bc + cb) + two * cc, bb, cb

    re, im = mix(0), mix(1)
    hop = cdot((jnp.concatenate(re, axis=0), jnp.concatenate(im, axis=0)), t_parts)

    def scaled(which):
        return (
            split(cluster[0][...] * shift_tab[which]),
            split(cluster[1][...] * shift_tab[which]),
        )

    pair = cdot((then_c[0][0:CHANS], then_c[1][0:CHANS]), scaled(0))
    triple = cdot((then_c[0][CHANS:], then_c[1][CHANS:]), scaled(1))
    for_b, for_c = [], []
    for c in range(2):
        h = hop[c]
        for_b.append(h[0:CHANS] - (lead_b[c] + mean * lead_c[c]))
        for_c.append(
            mean * h[CHANS : 2 * CHANS]
            + two * h[2 * CHANS : 3 * CHANS]
            + pair[c]
            + triple[c]
            - (mean * lead_b[c] + two * lead_c[c])
        )
    by_b = cdot(tuple(for_b), b_parts)
    by_c = cdot(tuple(for_c), c_parts)
    line_r, line_i = by_b[0] + by_c[0], by_b[1] + by_c[1]
    m_r = dot_exact(line_r, tab.wave_cos) - dot_exact(line_i, tab.wave_sin)
    m_i = dot_exact(line_r, tab.wave_sin) + dot_exact(line_i, tab.wave_cos)
    m_r = m_r + b_wide[0] + mean * c_wide[0]
    m_i = m_i + b_wide[1] + mean * c_wide[1]
    d = cdot(cdot(x, block_diag_c((m_r, m_i), tab)), x_parts)
    return -d[0], -d[1]


def correction_stage(d, square, e, kmap, tab):
    onehot = ((iota((WIDE, LANES), 0) >> 4) == kmap[...]).astype(F32).astype(BF16)
    keep = tab.row_block == tab.col_in

    def spread(panel):
        high, low = split(panel)

        def one(part):
            full = jnp.where(keep, tile_rows(part.astype(F32), CHANS), 0.0)
            return dot(full.astype(BF16), onehot)

        return one(high) + one(low)

    dr, di = spread(d[0]), spread(d[1])
    sr, si = square[e, 0].reshape(WIDE, LANES), square[e, 1].reshape(WIDE, LANES)
    re = jnp.sum(dr * sr - di * si, axis=0, keepdims=True)
    im = jnp.sum(dr * si + di * sr, axis=0, keepdims=True)
    return re, im


def coarse_out(x, tab, store):
    fold = (tab.col_block == tab.row_in)
    pick = (iota((WIDE, MOMS), 0) >> 4 == iota((WIDE, MOMS), 1)).astype(F32).astype(BF16)
    high = x.astype(BF16)
    rest = x - high.astype(F32)
    mid = rest.astype(BF16)
    low = (rest - mid.astype(F32)).astype(BF16)
    total = None
    for part in (low, mid, high):
        wide = jnp.broadcast_to(part.astype(F32)[:, None, :], (CHANS, CHANS, WIDE))
        wide = jnp.where(tab.same_in, wide.reshape(WIDE, WIDE), 0.0).astype(BF16)
        piece = dot(wide, pick)
        total = piece if total is None else total + piece
    store(total.reshape(CHANS, CHANS, MOMS))


def gathered_panel(tiles, at):
    top = jnp.concatenate([tiles[at], tiles[at + 1]], axis=1)
    low = jnp.concatenate([tiles[at + 2], tiles[at + 3]], axis=1)
    return jnp.concatenate([top, low], axis=0)


def kpoint_kernel(structure, medium, kmap, occupation, weight, sums, row, square, spread, factor, inner):
    spread_medium(medium, kmap, spread)

    def write(at, value):
        sums[at] = value

    kpoint_sums(structure, spread, factor, inner, kmap, write)
    config_row(occupation, weight, row)
    kpoint_squares(spread, factor, inner, square)


def reduce_kernel(
    n_ka, n_cfg, sums, row, total, configs,
    outgoing, first, own_rows, part, rows_send, rows_recv, a_send, a_recv, b_send, b_recv, c_send, c_recv,
):
    ka, cfg = lax.axis_index("ka"), lax.axis_index("cfg")
    barrier = pltpu.get_barrier_semaphore()
    for d in range(1, n_ka):
        pl.semaphore_signal(barrier, inc=1, device_id=(lax.rem(ka + d, n_ka), cfg), device_id_type=MESH)
    for d in range(1, n_cfg):
        pl.semaphore_signal(barrier, inc=1, device_id=(ka, lax.rem(cfg + d, n_cfg)), device_id_type=MESH)
    pl.semaphore_wait(barrier, n_ka + n_cfg - 2)

    def cfg_copy(src, slots, send, recv, d):
        return pltpu.make_async_remote_copy(
            src_ref=src, dst_ref=slots.at[cfg], send_sem=send.at[d], recv_sem=recv.at[cfg],
            device_id=(ka, lax.rem(cfg + d, n_cfg)), device_id_type=MESH,
        )

    def cfg_wait(src, slots, send, recv, d):
        at = lax.rem(cfg + d, n_cfg)
        pltpu.make_async_remote_copy(
            src_ref=src, dst_ref=slots.at[at], send_sem=send.at[d], recv_sem=recv.at[at],
            device_id=(ka, at), device_id_type=MESH,
        ).wait_recv()

    def ka_copy(src, slots, send, recv, d):
        return pltpu.make_async_remote_copy(
            src_ref=src, dst_ref=slots.at[ka], send_sem=send.at[d], recv_sem=recv.at[ka],
            device_id=(lax.rem(ka + d, n_ka), cfg), device_id_type=MESH,
        )

    def ka_wait(src, slots, send, recv, d):
        at = lax.rem(ka + d, n_ka)
        pltpu.make_async_remote_copy(
            src_ref=src, dst_ref=slots.at[at], send_sem=send.at[d], recv_sem=recv.at[at],
            device_id=(at, cfg), device_id_type=MESH,
        ).wait_recv()

    for d in range(1, n_cfg):
        cfg_copy(row, own_rows, rows_send, rows_recv, d).start()
    own_rows[cfg] = row[...]
    for d in range(1, n_cfg):
        cfg_wait(row, own_rows, rows_send, rows_recv, d)
    line = iota((8, LANES), 0)
    group = jnp.zeros((8, LANES), F32)
    for at in range(n_cfg):
        group = group + jnp.where(line == at, own_rows[at], 0.0)
    for at in range(n_ka):
        outgoing[at, 0] = sums[at]
        outgoing[at, 1] = group
    for d in range(1, n_ka):
        ka_copy(outgoing.at[lax.rem(ka + d, n_ka)], first, a_send, a_recv, d).start()
    first[ka] = outgoing[ka]
    for d in range(1, n_ka):
        ka_wait(outgoing.at[0], first, a_send, a_recv, d)
    value = first[0, 0]
    configs[0] = first[0, 1]
    for at in range(1, n_ka):
        value = value + first[at, 0]
        configs[at] = first[at, 1]
    part[cfg] = value
    for d in range(1, n_cfg):
        cfg_copy(part.at[cfg], part, b_send, b_recv, d).start()
    for d in range(1, n_cfg):
        cfg_wait(part.at[cfg], part, b_send, b_recv, d)
    value = part[0]
    for at in range(1, n_cfg):
        value = value + part[at]
    total[ka] = value
    for d in range(1, n_ka):
        ka_copy(total.at[ka], total, c_send, c_recv, d).start()
    for d in range(1, n_ka):
        ka_wait(total.at[ka], total, c_send, c_recv, d)
    for d in range(1, n_cfg):
        cfg_copy(row, own_rows, rows_send, rows_recv, d).wait_send()
        cfg_copy(part.at[cfg], part, b_send, b_recv, d).wait_send()
    for d in range(1, n_ka):
        ka_copy(outgoing.at[0], first, a_send, a_recv, d).wait_send()
        ka_copy(total.at[ka], total, c_send, c_recv, d).wait_send()


def cluster_kernel(
    per_moment, total, configs, medium, kmap, shift_a, shift_b, square, coarse, block, correction,
    cluster, rows_tab, shift_tab,
):
    ka, cfg = lax.axis_index("ka"), lax.axis_index("cfg")
    cluster_body(
        per_moment, ka, cfg, total, configs, medium, kmap, shift_a, shift_b, square, coarse, block,
        correction, cluster, rows_tab, shift_tab,
    )


def cluster_body(
    per_moment, ka, cfg, total, configs, medium, kmap, shift_a, shift_b, square, coarse, block, correction,
    cluster, rows_tab, shift_tab,
):
    tab = Tables()
    moment_tables(configs[...].reshape(LANES, LANES), tab, rows_tab, shift_tab)
    which = iota((8, WIDE), 0)
    out = jnp.zeros((8, WIDE), F32)
    for e in range(ENERGIES):
        y = medium_panels(medium, tab, e)
        b_wide, c_wide = shift_panels(shift_a, shift_b, tab, e)
        b_parts, c_parts = block_diag_c(b_wide, tab), block_diag_c(c_wide, tab)
        sum_t = (gathered_panel(total, e * 8), gathered_panel(total, e * 8 + 4))
        x = coarse_panel(y, sum_t, tab, per_moment)
        x_parts = block_diag_c(x, tab)
        real, imag = cluster_matrix(x, tab)
        cluster[e, 0] = real
        cluster[e, 1] = imag
        t_parts = split(real), split(imag)
        held = (cluster.at[e, 0], cluster.at[e, 1])
        avg = rows_stage(held, t_parts, b_parts, c_parts, rows_tab, cfg * 2, ka)
        for c in range(2):
            for site in range(2):
                at = e * 4 + c * 2 + site
                out = jnp.where(which == at, avg[c][site * 8 : site * 8 + 8], out)
        d = moment_stage(
            held, t_parts, x, x_parts, b_wide, c_wide, b_parts, c_parts, shift_tab, tab
        )
        re, im = correction_stage(d, square, e, kmap, tab)
        correction[e, 0:1, :] = re
        correction[e, 1:2, :] = im
        for c in range(2):
            def store(value, e=e, c=c):
                coarse[e, c] = value

            coarse_out(x[c], tab, store)
    block[...] = out


def gather_kernel(n_ka, block, average, slots, send, recv):
    ka, cfg = lax.axis_index("ka"), lax.axis_index("cfg")
    barrier = pltpu.get_barrier_semaphore()
    for d in range(1, n_ka):
        pl.semaphore_signal(barrier, inc=1, device_id=(lax.rem(ka + d, n_ka), cfg), device_id_type=MESH)
    pl.semaphore_wait(barrier, n_ka - 1)

    def copy(at, d):
        return pltpu.make_async_remote_copy(
            src_ref=block, dst_ref=slots.at[at], send_sem=send.at[d], recv_sem=recv.at[at],
            device_id=(lax.rem(ka + d, n_ka), cfg), device_id_type=MESH,
        )

    for d in range(1, n_ka):
        copy(ka, d).start()
    slots[ka] = block[...]
    for d in range(1, n_ka):
        copy(lax.rem(ka + d, n_ka), d).wait_recv()
    for at in range(n_ka):
        for e in range(ENERGIES):
            for c in range(2):
                for site in range(2):
                    line = e * 4 + c * 2 + site
                    row = site * CHANS + at
                    average[e, c, row : row + 1, :] = slots[at, line : line + 1, :]
    for d in range(1, n_ka):
        copy(ka, d).wait_send()


def shape(*dims):
    return jax.ShapeDtypeStruct(dims, F32)


VMEM_SPEC = pl.BlockSpec(memory_space=pltpu.VMEM)
SMEM_SPEC = pl.BlockSpec(memory_space=pltpu.SMEM)


def per_device(medium_t, structure, kmap, occupation, cfg_weight, shift_a, shift_b):
    n_ka, n_cfg = lax.axis_size("ka"), lax.axis_size("cfg")
    per_moment = kmap.shape[0] * n_ka * n_cfg // MOMS
    kmap = kmap.reshape(1, LANES)
    kdims = (ENERGIES, 2, CHANS, CHANS, LANES)
    params = functools.partial(pltpu.CompilerParams, vmem_limit_bytes=48 * 1024 * 1024)
    sums, row, square = pl.pallas_call(
        kpoint_kernel,
        out_shape=(shape(16, 8, LANES), shape(8, LANES), shape(*kdims)),
        in_specs=[VMEM_SPEC] * 4 + [SMEM_SPEC],
        out_specs=(VMEM_SPEC,) * 3,
        scratch_shapes=[pltpu.VMEM(kdims, F32)] * 3,
        compiler_params=params(),
    )(structure, medium_t, kmap, occupation, cfg_weight)
    dma = pltpu.SemaphoreType.DMA
    total, configs = pl.pallas_call(
        functools.partial(reduce_kernel, n_ka, n_cfg),
        out_shape=(shape(16, 8, LANES), shape(16, 8, LANES)),
        in_specs=[VMEM_SPEC] * 2,
        out_specs=(VMEM_SPEC,) * 2,
        scratch_shapes=[
            pltpu.VMEM((n_ka, 2, 8, LANES), F32),
            pltpu.VMEM((n_ka, 2, 8, LANES), F32),
            pltpu.VMEM((n_cfg, 8, LANES), F32),
            pltpu.VMEM((n_cfg, 8, LANES), F32),
            dma((n_cfg,)), dma((n_cfg,)),
            dma((n_ka,)), dma((n_ka,)),
            dma((n_cfg,)), dma((n_cfg,)),
            dma((n_ka,)), dma((n_ka,)),
        ],
        compiler_params=params(collective_id=0, has_side_effects=True),
    )(sums, row)
    coarse, block, correction = pl.pallas_call(
        functools.partial(cluster_kernel, per_moment),
        out_shape=(
            shape(ENERGIES, 2, CHANS, CHANS, MOMS),
            shape(8, WIDE),
            shape(ENERGIES, 2, LANES),
        ),
        in_specs=[VMEM_SPEC] * 7,
        out_specs=(VMEM_SPEC,) * 3,
        scratch_shapes=[
            pltpu.VMEM((ENERGIES, 2, WIDE, WIDE), F32),
            pltpu.VMEM((SITES + 1, ALPHA, WIDE + LANES), F32),
            pltpu.VMEM((2, WIDE, WIDE), F32),
        ],
        compiler_params=params(),
    )(total, configs, medium_t, kmap, shift_a, shift_b, square)
    average = pl.pallas_call(
        functools.partial(gather_kernel, n_ka),
        out_shape=shape(ENERGIES, 2, 2 * CHANS, WIDE),
        in_specs=[VMEM_SPEC],
        out_specs=VMEM_SPEC,
        scratch_shapes=[pltpu.VMEM((n_ka, 8, WIDE), F32), dma((n_ka,)), dma((n_ka,))],
        compiler_params=params(collective_id=1, has_side_effects=True),
    )(block)
    return coarse, average, correction


def solution(mesh):
    placed = (
        P(),
        P(None, None, None, None, ("ka", "cfg")),
        P(("ka", "cfg")),
        P(("ka", "cfg"), None),
        P(("ka", "cfg")),
        P(),
        P(),
    )
    return jax.shard_map(
        per_device,
        mesh=mesh,
        in_specs=placed,
        out_specs=(P(), P(None, None, "cfg", None), P(None, None, ("ka", "cfg"))),
        check_vma=False,
    )
```

```python
import functools

import jax
import jax.numpy as jnp
from jax import lax
from jax.experimental import pallas as pl
from jax.experimental.pallas import tpu as pltpu
from jax.sharding import PartitionSpec as P

MESH = pl.DeviceIdType.MESH
F32 = jnp.float32
BF16 = jnp.bfloat16
NN = (((1,), (0,)), ((), ()))
NT = (((1,), (1,)), ((), ()))

ENERGIES = 2
SITES = 16
CHANS = 16
MOMS = 16
WIDE = SITES * CHANS
LANES = 128
ALPHA = 24


def split(x):
    high = x.astype(BF16)
    return high, (x - high.astype(F32)).astype(BF16)


def dot(left, right, dims=NN):
    return lax.dot_general(left, right, dims, preferred_element_type=F32)


def dot_exact(x, right, dims=NN):
    high, low = split(x)
    return dot(high, right, dims) + dot(low, right, dims)


def dot3(x, right, dims=NN):
    high, low = split(x)
    return dot(high, right[0], dims) + (dot(low, right[0], dims) + dot(high, right[1], dims))


def cdot(x, right, dims=NN):
    rows = x[0].shape[0]
    both = jnp.concatenate([x[0], x[1]], axis=0)
    by_re = dot3(both, right[0], dims)
    by_im = dot3(both, right[1], dims)
    return by_re[:rows] - by_im[rows:], by_im[:rows] + by_re[rows:]


def csplit(x):
    return split(x[0]), split(x[1])


def iota(shape, axis):
    return lax.broadcasted_iota(jnp.int32, shape, axis)


def tile_rows(x, times):
    return jnp.concatenate([x] * times, axis=0)


def quarter_turns(mom, site):
    half = site >> 3
    x = 2 * ((site >> 2) & 1) + half
    y = 2 * ((site >> 1) & 1) + half
    z = 2 * (site & 1) + half
    return ((mom >> 2) * x + ((mom >> 1) & 1) * y + (mom & 1) * z) & 3


def cos_sin(turns):
    sign = (1 - (turns & 2)).astype(F32)
    odd = (turns & 1) == 1
    return jnp.where(odd, 0.0, sign), jnp.where(odd, sign, 0.0)


def site_sum(first, second):
    carry = (first & second) >> 3
    return (first ^ second) ^ (7 * carry)


class Tables:
    def __init__(self):
        rows, cols = iota((WIDE, WIDE), 0), iota((WIDE, WIDE), 1)
        self.row_block, self.col_block = rows >> 4, cols >> 4
        self.row_in, self.col_in = rows & 15, cols & 15
        self.same_block = self.row_block == self.col_block
        self.same_in = self.row_in == self.col_in
        self.cos, self.sin = cos_sin(quarter_turns(self.col_block, self.row_block))
        self.wave_cos = jnp.where(self.same_in, self.cos, 0.0).astype(BF16)
        self.wave_sin = jnp.where(self.same_in, self.sin, 0.0).astype(BF16)
        small_r, small_c = iota((SITES, WIDE), 0), iota((SITES, WIDE), 1)
        self.pick_in = (small_r == (small_c & 15)).astype(F32).astype(BF16)
        self.pick_block = (small_r == (small_c >> 4)).astype(F32).astype(BF16)


def block_diag(panel, tab):
    def spread(part):
        return jnp.where(tab.same_block, tile_rows(part.astype(F32), SITES), 0.0).astype(BF16)

    high, low = split(panel)
    return spread(high), spread(low)


def block_diag_c(panel, tab):
    return block_diag(panel[0], tab), block_diag(panel[1], tab)


def kpoint_mul(store, left, right):
    def body(a, carry):
        re = jnp.zeros((CHANS, LANES), F32)
        im = jnp.zeros((CHANS, LANES), F32)
        for b in range(CHANS):
            lr = left[0, a, pl.ds(b, 1), :]
            li = left[1, a, pl.ds(b, 1), :]
            rr = right[0, b]
            ri = right[1, b]
            re = re + (lr * rr - li * ri)
            im = im + (lr * ri + li * rr)
        store(a, re, im)
        return carry

    lax.fori_loop(0, CHANS, body, 0)


def spread_medium(medium, kmap, spread):
    onehot = (iota((MOMS, LANES), 0) == kmap[...]).astype(F32).astype(BF16)
    for e in range(ENERGIES):
        for c in range(2):
            flat = medium[e, c].reshape(WIDE, MOMS)
            spread[e, c] = dot_exact(flat, onehot).reshape(CHANS, CHANS, LANES)


def kpoint_inner(structure, spread, factor, inner, e):
    y, g, f, h = spread.at[e], structure.at[e], factor.at[e], inner.at[e]

    def put_f(a, re, im):
        f[0, a] = re
        f[1, a] = im

    def put_h(a, re, im):
        h[0, a] = g[0, a] + re
        h[1, a] = g[1, a] + im

    kpoint_mul(put_f, y, g)
    kpoint_mul(put_h, g, f)


def kpoint_sums(inner, kmap, write_tile):
    rows, lanes = iota((WIDE, LANES), 0), kmap[...]
    onehot_t = ((rows >> 4) == lanes).astype(F32).astype(BF16)
    row_block = iota((WIDE, WIDE), 0) >> 4
    col_in = iota((WIDE, WIDE), 1) & 15
    keep = row_block == col_in
    for e in range(ENERGIES):
        for c in range(2):
            flat = inner[e, c].reshape(WIDE, LANES)
            by_mom = jnp.where(keep, dot_exact(flat, onehot_t, NT), 0.0)
            panel = jnp.sum(by_mom.reshape(CHANS, CHANS, WIDE), axis=0)
            for half in range(2):
                for side in range(2):
                    write_tile(
                        ((e * 2 + c) * 2 + half) * 2 + side,
                        panel[half * 8 : half * 8 + 8, side * LANES : side * LANES + LANES],
                    )


def kpoint_squares(spread, factor, tau, square):
    for e in range(ENERGIES):
        y, f, t, s = spread.at[e], factor.at[e], tau.at[e], square.at[e]

        def put_q(a, re, im, s=s, f=f):
            s[0, a] = f[0, a] + re
            s[1, a] = f[1, a] + im

        def put_t(a, re, im, t=t, y=y):
            t[0, a] = y[0, a] + re
            t[1, a] = y[1, a] + im

        def put_s(a, re, im, s=s):
            s[0, a] = re
            s[1, a] = im

        kpoint_mul(put_q, f, f)
        kpoint_mul(put_t, s, y)
        kpoint_mul(put_s, t, t)


def config_row(occupation, weight, row):
    lane = iota((8, LANES), 1)
    row[...] = jnp.where(lane == SITES, 1.0, 0.0) + jnp.where(
        lane == SITES + 1, weight[0], 0.0
    )
    row[:, 0:SITES] = jnp.broadcast_to(occupation[...].astype(F32), (8, SITES))


def moment_tables(configs, tab, rows_tab, shift_tab):
    turned = jnp.transpose(configs)
    count = turned[0:ALPHA]
    weight = turned[SITES + 1 : SITES + 2]
    weight = weight / jnp.sum(weight, axis=1, keepdims=True)
    live = iota((ALPHA, LANES), 0) <= SITES
    count = jnp.where(live, count, 0.0)
    weighted = count * weight
    flat = configs.astype(BF16)
    lane_r, lane_c = iota((LANES, WIDE), 0), iota((LANES, WIDE), 1)
    pick = (lane_r == (lane_c >> 4)).astype(F32).astype(BF16)
    wide = dot(flat, pick).astype(BF16)
    ones = jnp.ones((LANES, LANES), BF16)
    for s in range(SITES + 1):
        product = weighted * count[s : s + 1]
        rows_tab[s, :, 0:WIDE] = dot_exact(product, wide)
        rows_tab[s, :, WIDE : WIDE + LANES] = dot_exact(product, ones)
    r, c = iota((WIDE, LANES), 0), iota((WIDE, LANES), 1)
    move = (site_sum(r >> 4, r & 15) == c).astype(F32).astype(BF16)
    moved = dot(move, flat, NT)
    moved_b = moved.astype(BF16)
    own = dot(((r >> 4) == c).astype(F32).astype(BF16), flat, NT)
    base = moved * (weight * (1.0 / SITES))
    fold = (tab.row_in == tab.col_block).astype(F32).astype(BF16)
    for which, left in ((0, base), (1, base * own)):
        full = dot_exact(left, moved_b, NT)
        kept = jnp.where(tab.same_block, full, 0.0)
        small = jnp.sum(kept.reshape(SITES, SITES, WIDE), axis=0)
        lanes = dot_exact(small, fold)
        shift_tab[which] = jnp.broadcast_to(
            lanes[:, None, :], (SITES, CHANS, WIDE)
        ).reshape(WIDE, WIDE)


def medium_panels(medium, tab, e):
    out = []
    for c in range(2):
        flat = medium[e, c].reshape(WIDE, MOMS)
        pick = ((iota((MOMS, WIDE), 1) >> 4) == iota((MOMS, WIDE), 0)).astype(F32).astype(BF16)
        by_mom = jnp.where(tab.same_in, dot_exact(flat, pick), 0.0)
        out.append(jnp.sum(by_mom.reshape(CHANS, CHANS, WIDE), axis=1))
    return tuple(out)


def shift_panels(shift_a, shift_b, tab, e):
    def wide(x):
        return dot_exact(x, tab.pick_in)

    b = (wide(shift_b[e, 0]), wide(shift_b[e, 1]))
    c = (
        wide(shift_a[e, 0] - shift_b[e, 0]),
        wide(shift_a[e, 1] - shift_b[e, 1]),
    )
    return b, c


def coarse_panel(y, y_parts, sum_t, tab, per_moment):
    left = cdot(y, block_diag_c(sum_t, tab), NT)
    both = cdot(left, y_parts)
    scale = 1.0 / per_moment
    return y[0] + scale * both[0], y[1] + scale * both[1]


def cluster_matrix(x, tab):
    re, im = tile_rows(x[0], SITES), tile_rows(x[1], SITES)
    scale = 1.0 / SITES
    left_r = (re * tab.cos - im * tab.sin) * scale
    left_i = (re * tab.sin + im * tab.cos) * scale
    real = dot_exact(left_r, tab.wave_cos, NT) + dot_exact(left_i, tab.wave_sin, NT)
    imag = dot_exact(left_i, tab.wave_cos, NT) - dot_exact(left_r, tab.wave_sin, NT)
    return real, imag


def rows_stage(cluster, t_parts, b_parts, c_parts, rows_tab, site0, chan):
    def own(ref):
        first = ref[pl.ds(site0 * CHANS + chan, 1), :]
        second = ref[pl.ds((site0 + 1) * CHANS + chan, 1), :]
        return jnp.concatenate(
            [jnp.broadcast_to(first, (8, WIDE)), jnp.broadcast_to(second, (8, WIDE))], axis=0
        )

    start = (own(cluster[0]), own(cluster[1]))
    with_b = cdot(start, b_parts)
    with_c = cdot(start, c_parts)
    row = iota((ALPHA, WIDE), 0)
    block = iota((ALPHA, WIDE), 1) >> 4

    def opened(c):
        out = []
        for at in (0, 8):
            ub = jnp.broadcast_to(with_b[c][at : at + 1], (ALPHA, WIDE))
            uc = jnp.broadcast_to(with_c[c][at : at + 1], (ALPHA, WIDE))
            out.append(jnp.where(row == block, uc, jnp.where(row == SITES, ub, 0.0)))
        return jnp.concatenate(out, axis=0)

    hop = cdot((opened(0), opened(1)), t_parts)
    plain, dressed = [[], []], [[], []]
    for c in range(2):
        for site in range(2):
            f = jnp.zeros((ALPHA, WIDE), F32)
            h = jnp.zeros((ALPHA, WIDE), F32)
            for s in range(SITES + 1):
                line = hop[c][site * ALPHA + s : site * ALPHA + s + 1]
                pair = rows_tab[s, :, WIDE : WIDE + LANES]
                f = f + jnp.concatenate([pair, pair], axis=1) * line
                h = h + rows_tab[s, :, 0:WIDE] * line
            plain[c].append(f)
            dressed[c].append(h)
    plain = tuple(jnp.concatenate(p, axis=0) for p in plain)
    dressed = tuple(jnp.concatenate(d, axis=0) for d in dressed)
    by_b = cdot(plain, b_parts)
    by_c = cdot(dressed, c_parts)
    inner = (by_b[0] + by_c[0], by_b[1] + by_c[1])
    second = cdot(inner, t_parts)
    mean = rows_tab[SITES, SITES : SITES + 1, 0:WIDE]

    def eight(parts):
        return jnp.concatenate([jnp.broadcast_to(p, (8, WIDE)) for p in parts], axis=0)

    for_b, for_c, rest = [], [], []
    for c in range(2):
        last_b, last_c, known = [], [], []
        for site in range(2):
            lines = second[c][site * ALPHA : site * ALPHA + ALPHA]
            picked = jnp.sum(jnp.where(row == block, lines, 0.0), axis=0, keepdims=True)
            last_b.append(lines[SITES : SITES + 1])
            last_c.append(picked)
            known.append(
                with_b[c][site * 8 : site * 8 + 1]
                + with_c[c][site * 8 : site * 8 + 1] * mean
                - inner[c][site * ALPHA + SITES : site * ALPHA + SITES + 1]
            )
        for_b.append(eight(last_b))
        for_c.append(eight(last_c))
        rest.append(eight(known))
    by_b = cdot(tuple(for_b), b_parts)
    by_c = cdot(tuple(for_c), c_parts)
    z = (rest[0] + by_b[0] + by_c[0], rest[1] + by_b[1] + by_c[1])
    last = cdot(z, t_parts)
    return start[0] - last[0], start[1] - last[1]


def moment_stage(cluster, t_parts, x, x_parts, b_wide, c_wide, b_parts, c_parts, shift_tab, tab):
    top = (cluster[0][0:CHANS, :], cluster[1][0:CHANS, :])
    top_parts = csplit(top)

    def head(wide):
        return wide[0][:, 0:CHANS], wide[1][:, 0:CHANS]

    b_in, c_in = head(b_wide), head(c_wide)
    small = (
        jnp.concatenate([b_in[0], c_in[0]], axis=0),
        jnp.concatenate([b_in[1], c_in[1]], axis=0),
    )
    lead = cdot(small, top_parts)
    lead_b = (lead[0][0:CHANS], lead[1][0:CHANS])
    lead_c = (lead[0][CHANS:], lead[1][CHANS:])
    then_b = cdot(lead, b_parts)
    then_c = cdot(lead, c_parts)
    two = shift_tab[1, 0:1, :]
    mean = shift_tab[1, 0:1, 0:1]

    def mix(c):
        bb, cb = then_b[c][0:CHANS], then_b[c][CHANS:]
        bc, cc = then_c[c][0:CHANS], then_c[c][CHANS:]
        return bb + mean * (bc + cb) + two * cc, bb, cb

    re, im = mix(0), mix(1)
    hop = cdot((jnp.concatenate(re, axis=0), jnp.concatenate(im, axis=0)), t_parts)

    def scaled(which):
        return (
            split(cluster[0][...] * shift_tab[which]),
            split(cluster[1][...] * shift_tab[which]),
        )

    pair = cdot((then_c[0][0:CHANS], then_c[1][0:CHANS]), scaled(0))
    triple = cdot((then_c[0][CHANS:], then_c[1][CHANS:]), scaled(1))
    for_b, for_c = [], []
    for c in range(2):
        h = hop[c]
        for_b.append(h[0:CHANS] - (lead_b[c] + mean * lead_c[c]))
        for_c.append(
            mean * h[CHANS : 2 * CHANS]
            + two * h[2 * CHANS : 3 * CHANS]
            + pair[c]
            + triple[c]
            - (mean * lead_b[c] + two * lead_c[c])
        )
    by_b = cdot(tuple(for_b), b_parts)
    by_c = cdot(tuple(for_c), c_parts)
    line_r, line_i = by_b[0] + by_c[0], by_b[1] + by_c[1]
    m_r = dot_exact(line_r, tab.wave_cos) - dot_exact(line_i, tab.wave_sin)
    m_i = dot_exact(line_r, tab.wave_sin) + dot_exact(line_i, tab.wave_cos)
    m_r = m_r + b_wide[0] + mean * c_wide[0]
    m_i = m_i + b_wide[1] + mean * c_wide[1]
    d = cdot(cdot(x, block_diag_c((m_r, m_i), tab)), x_parts)
    return -d[0], -d[1]


def correction_stage(d, square, e, kmap, tab):
    onehot = ((iota((WIDE, LANES), 0) >> 4) == kmap[...]).astype(F32).astype(BF16)
    keep = tab.row_block == tab.col_in

    def spread(panel):
        high, low = split(panel)

        def one(part):
            full = jnp.where(keep, tile_rows(part.astype(F32), CHANS), 0.0)
            return dot(full.astype(BF16), onehot)

        return one(high) + one(low)

    dr, di = spread(d[0]), spread(d[1])
    sr, si = square[e, 0].reshape(WIDE, LANES), square[e, 1].reshape(WIDE, LANES)
    re = jnp.sum(dr * sr - di * si, axis=0, keepdims=True)
    im = jnp.sum(dr * si + di * sr, axis=0, keepdims=True)
    return re, im


def coarse_out(x, tab, store):
    fold = (tab.col_block == tab.row_in)
    pick = (iota((WIDE, MOMS), 0) >> 4 == iota((WIDE, MOMS), 1)).astype(F32).astype(BF16)
    high = x.astype(BF16)
    rest = x - high.astype(F32)
    mid = rest.astype(BF16)
    low = (rest - mid.astype(F32)).astype(BF16)
    total = None
    for part in (low, mid, high):
        wide = jnp.broadcast_to(part.astype(F32)[:, None, :], (CHANS, CHANS, WIDE))
        wide = jnp.where(tab.same_in, wide.reshape(WIDE, WIDE), 0.0).astype(BF16)
        piece = dot(wide, pick)
        total = piece if total is None else total + piece
    store(total.reshape(CHANS, CHANS, MOMS))


def gathered_panel(tiles, at):
    top = jnp.concatenate([tiles[at], tiles[at + 1]], axis=1)
    low = jnp.concatenate([tiles[at + 2], tiles[at + 3]], axis=1)
    return jnp.concatenate([top, low], axis=0)


class Exchange:
    def __init__(self, axis, count, slots, send, recv):
        self.axis, self.count = axis, count
        self.slots, self.send, self.recv = slots, send, recv
        self.me = lax.axis_index(axis)

    def peer(self, d):
        return lax.rem(self.me + d, self.count)

    def copy(self, src, at, d):
        return pltpu.make_async_remote_copy(
            src_ref=src, dst_ref=self.slots.at[at], send_sem=self.send.at[d],
            recv_sem=self.recv.at[at], device_id={self.axis: self.peer(d)}, device_id_type=MESH,
        )

    def start(self, source):
        for d in range(1, self.count):
            self.copy(source(self.peer(d)), self.me, d).start()

    def wait(self, source):
        for d in range(1, self.count):
            self.copy(source(self.me), self.peer(d), d).wait_recv()

    def drain(self, source):
        for d in range(1, self.count):
            self.copy(source(self.me), self.me, d).wait_send()


def greet(n_ka, n_cfg):
    barrier = pltpu.get_barrier_semaphore()
    for axis, count in (("ka", n_ka), ("cfg", n_cfg)):
        me = lax.axis_index(axis)
        for d in range(1, count):
            pl.semaphore_signal(
                barrier, inc=1, device_id={axis: lax.rem(me + d, count)}, device_id_type=MESH
            )
    return barrier


def kernel(
    per_moment, n_ka, n_cfg,
    structure_hbm, medium_hbm, kmap, occupation, weight, shift_a, shift_b,
    coarse, average, correction,
    structure, medium, spread, factor, inner, square, cluster, rows_tab, shift_tab,
    row, own_rows, outgoing, first, part, total, block, slots,
    load_sem, row_send, row_recv, first_send, first_recv, part_send, part_recv,
    total_send, total_recv, slot_send, slot_recv,
):
    barrier = greet(n_ka, n_cfg)
    loads = [
        pltpu.make_async_copy(medium_hbm, medium, load_sem.at[0]),
        pltpu.make_async_copy(structure_hbm, structure, load_sem.at[1]),
    ]
    for load in loads:
        load.start()
    rows_x = Exchange("cfg", n_cfg, own_rows, row_send, row_recv)
    first_x = Exchange("ka", n_ka, first, first_send, first_recv)
    part_x = Exchange("cfg", n_cfg, part, part_send, part_recv)
    total_x = Exchange("ka", n_ka, total, total_send, total_recv)
    slot_x = Exchange("ka", n_ka, slots, slot_send, slot_recv)
    ka, cfg = first_x.me, rows_x.me
    config_row(occupation, weight, row)
    loads[0].wait()
    spread_medium(medium, kmap, spread)
    loads[1].wait()
    kpoint_inner(structure, spread, factor, inner, 0)
    pl.semaphore_wait(barrier, n_ka + n_cfg - 2)
    rows_x.start(lambda to: row)
    own_rows[cfg] = row[...]
    kpoint_inner(structure, spread, factor, inner, 1)

    def write(at, value):
        outgoing[at, 0] = value

    kpoint_sums(inner, kmap, write)
    rows_x.wait(lambda to: row)
    line = iota((8, LANES), 0)
    group = jnp.zeros((8, LANES), F32)
    for at in range(n_cfg):
        group = group + jnp.where(line == at, own_rows[at], 0.0)
    for at in range(n_ka):
        outgoing[at, 1] = group
    first_x.start(lambda to: outgoing.at[to])
    first[ka] = outgoing[ka]
    kpoint_squares(spread, factor, inner, square)
    first_x.wait(lambda to: outgoing.at[to])
    value = first[0, 0]
    for at in range(1, n_ka):
        value = value + first[at, 0]
    part[cfg] = value
    part_x.start(lambda to: part.at[cfg])
    tab = Tables()
    y = [medium_panels(medium, tab, e) for e in range(ENERGIES)]
    y_parts = [block_diag_c(y[e], tab) for e in range(ENERGIES)]
    wide = [shift_panels(shift_a, shift_b, tab, e) for e in range(ENERGIES)]
    b_parts = [block_diag_c(wide[e][0], tab) for e in range(ENERGIES)]
    c_parts = [block_diag_c(wide[e][1], tab) for e in range(ENERGIES)]
    part_x.wait(lambda to: part.at[cfg])
    value = part[0]
    for at in range(1, n_cfg):
        value = value + part[at]
    total[ka] = value
    total_x.start(lambda to: total.at[ka])
    configs = jnp.concatenate([first[at, 1] for at in range(n_ka)], axis=0)
    moment_tables(configs, tab, rows_tab, shift_tab)
    total_x.wait(lambda to: total.at[ka])
    which = iota((8, WIDE), 0)
    out = jnp.zeros((8, WIDE), F32)
    x, x_parts, t_parts, held = [], [], [], []
    for e in range(ENERGIES):
        sum_t = (gathered_panel(total, e * 8), gathered_panel(total, e * 8 + 4))
        x.append(coarse_panel(y[e], y_parts[e], sum_t, tab, per_moment))
        real, imag = cluster_matrix(x[e], tab)
        cluster[e, 0] = real
        cluster[e, 1] = imag
        t_parts.append((split(real), split(imag)))
        held.append((cluster.at[e, 0], cluster.at[e, 1]))
        avg = rows_stage(held[e], t_parts[e], b_parts[e], c_parts[e], rows_tab, cfg * 2, ka)
        for c in range(2):
            for site in range(2):
                at = e * 4 + c * 2 + site
                out = jnp.where(which == at, avg[c][site * 8 : site * 8 + 8], out)
    block[...] = out
    slot_x.start(lambda to: block)
    slots[ka] = out
    for e in range(ENERGIES):
        x_parts = block_diag_c(x[e], tab)
        d = moment_stage(
            held[e], t_parts[e], x[e], x_parts, wide[e][0], wide[e][1], b_parts[e], c_parts[e],
            shift_tab, tab,
        )
        re, im = correction_stage(d, square, e, kmap, tab)
        correction[e, 0:1, :] = re
        correction[e, 1:2, :] = im
        for c in range(2):

            def store(value, e=e, c=c):
                coarse[e, c] = value

            coarse_out(x[e][c], tab, store)
    slot_x.wait(lambda to: block)
    for at in range(n_ka):
        for e in range(ENERGIES):
            for c in range(2):
                for site in range(2):
                    line = e * 4 + c * 2 + site
                    to = site * CHANS + at
                    average[e, c, to : to + 1, :] = slots[at, line : line + 1, :]
    rows_x.drain(lambda to: row)
    first_x.drain(lambda to: outgoing.at[to])
    part_x.drain(lambda to: part.at[cfg])
    total_x.drain(lambda to: total.at[ka])
    slot_x.drain(lambda to: block)


def shape(*dims):
    return jax.ShapeDtypeStruct(dims, F32)


VMEM_SPEC = pl.BlockSpec(memory_space=pltpu.VMEM)
SMEM_SPEC = pl.BlockSpec(memory_space=pltpu.SMEM)


def per_device(medium_t, structure, kmap, occupation, cfg_weight, shift_a, shift_b):
    n_ka, n_cfg = lax.axis_size("ka"), lax.axis_size("cfg")
    per_moment = kmap.shape[0] * n_ka * n_cfg // MOMS
    kmap = kmap.reshape(1, LANES)
    kdims = (ENERGIES, 2, CHANS, CHANS, LANES)
    dma = pltpu.SemaphoreType.DMA

    def vmem(*dims):
        return pltpu.VMEM(dims, F32)

    hbm_spec = pl.BlockSpec(memory_space=pltpu.HBM)
    return pl.pallas_call(
        functools.partial(kernel, per_moment, n_ka, n_cfg),
        out_shape=(
            shape(ENERGIES, 2, CHANS, CHANS, MOMS),
            shape(ENERGIES, 2, 2 * CHANS, WIDE),
            shape(ENERGIES, 2, LANES),
        ),
        in_specs=[hbm_spec] * 2 + [VMEM_SPEC] * 2 + [SMEM_SPEC] + [VMEM_SPEC] * 2,
        out_specs=(VMEM_SPEC,) * 3,
        scratch_shapes=[
            vmem(*kdims), vmem(ENERGIES, 2, CHANS, CHANS, MOMS),
            vmem(*kdims), vmem(*kdims), vmem(*kdims), vmem(*kdims),
            vmem(ENERGIES, 2, WIDE, WIDE),
            vmem(SITES + 1, ALPHA, WIDE + LANES),
            vmem(2, WIDE, WIDE),
            vmem(8, LANES), vmem(n_cfg, 8, LANES),
            vmem(n_ka, 2, 8, LANES), vmem(n_ka, 2, 8, LANES),
            vmem(n_cfg, 8, LANES), vmem(n_ka, 8, LANES),
            vmem(8, WIDE), vmem(n_ka, 8, WIDE),
            dma((2,)),
            dma((n_cfg,)), dma((n_cfg,)),
            dma((n_ka,)), dma((n_ka,)),
            dma((n_cfg,)), dma((n_cfg,)),
            dma((n_ka,)), dma((n_ka,)),
            dma((n_ka,)), dma((n_ka,)),
        ],
        compiler_params=pltpu.CompilerParams(
            collective_id=0, has_side_effects=True, vmem_limit_bytes=48 * 1024 * 1024
        ),
    )(structure, medium_t, kmap, occupation, cfg_weight, shift_a, shift_b)


def solution(mesh):
    placed = (
        P(),
        P(None, None, None, None, ("ka", "cfg")),
        P(("ka", "cfg")),
        P(("ka", "cfg"), None),
        P(("ka", "cfg")),
        P(),
        P(),
    )
    return jax.shard_map(
        per_device,
        mesh=mesh,
        in_specs=placed,
        out_specs=(P(), P(None, None, "cfg", None), P(None, None, ("ka", "cfg"))),
        check_vma=False,
    )
```

```python
import functools

import jax
import jax.numpy as jnp
from jax import lax
from jax.experimental import pallas as pl
from jax.experimental.pallas import tpu as pltpu
from jax.sharding import PartitionSpec as P

MESH = pl.DeviceIdType.MESH
F32 = jnp.float32
BF16 = jnp.bfloat16
NN = (((1,), (0,)), ((), ()))
NT = (((1,), (1,)), ((), ()))

ENERGIES = 2
SITES = 16
CHANS = 16
MOMS = 16
WIDE = SITES * CHANS
LANES = 128
ALPHA = 24


def split(x):
    high = x.astype(BF16)
    return high, (x - high.astype(F32)).astype(BF16)


def dot(left, right, dims=NN):
    return lax.dot_general(left, right, dims, preferred_element_type=F32)


def dot_exact(x, right, dims=NN):
    high, low = split(x)
    rows = x.shape[0]
    both = dot(jnp.concatenate([high, low], axis=0), right, dims)
    return both[:rows] + both[rows:]


def dot3(x, right, dims=NN):
    high, low = split(x)
    rows = x.shape[0]
    both = dot(jnp.concatenate([high, low], axis=0), right[0], dims)
    return both[:rows] + (both[rows:] + dot(high, right[1], dims))


def cdot(x, right, dims=NN):
    rows = x[0].shape[0]
    both = jnp.concatenate([x[0], x[1]], axis=0)
    by_re = dot3(both, right[0], dims)
    by_im = dot3(both, right[1], dims)
    return by_re[:rows] - by_im[rows:], by_im[:rows] + by_re[rows:]


def csplit(x):
    return split(x[0]), split(x[1])


def iota(shape, axis):
    return lax.broadcasted_iota(jnp.int32, shape, axis)


def tile_rows(x, times):
    return jnp.concatenate([x] * times, axis=0)


def quarter_turns(mom, site):
    half = site >> 3
    x = 2 * ((site >> 2) & 1) + half
    y = 2 * ((site >> 1) & 1) + half
    z = 2 * (site & 1) + half
    return ((mom >> 2) * x + ((mom >> 1) & 1) * y + (mom & 1) * z) & 3


def cos_sin(turns):
    sign = (1 - (turns & 2)).astype(F32)
    odd = (turns & 1) == 1
    return jnp.where(odd, 0.0, sign), jnp.where(odd, sign, 0.0)


def site_sum(first, second):
    carry = (first & second) >> 3
    return (first ^ second) ^ (7 * carry)


class Tables:
    def __init__(self):
        rows, cols = iota((WIDE, WIDE), 0), iota((WIDE, WIDE), 1)
        self.row_block, self.col_block = rows >> 4, cols >> 4
        self.row_in, self.col_in = rows & 15, cols & 15
        self.same_block = self.row_block == self.col_block
        self.same_in = self.row_in == self.col_in
        self.cos, self.sin = cos_sin(quarter_turns(self.col_block, self.row_block))
        self.wave_cos = jnp.where(self.same_in, self.cos, 0.0).astype(BF16)
        self.wave_sin = jnp.where(self.same_in, self.sin, 0.0).astype(BF16)
        small_r, small_c = iota((SITES, WIDE), 0), iota((SITES, WIDE), 1)
        self.pick_in = (small_r == (small_c & 15)).astype(F32).astype(BF16)
        self.pick_block = (small_r == (small_c >> 4)).astype(F32).astype(BF16)


def block_diag(panel, tab):
    def spread(part):
        return jnp.where(tab.same_block, tile_rows(part.astype(F32), SITES), 0.0).astype(BF16)

    high, low = split(panel)
    return spread(high), spread(low)


def block_diag_c(panel, tab):
    return block_diag(panel[0], tab), block_diag(panel[1], tab)


def kpoint_mul(store, left, right):
    def body(a, carry):
        re = jnp.zeros((CHANS, LANES), F32)
        im = jnp.zeros((CHANS, LANES), F32)
        for b in range(CHANS):
            lr = left[0, a, pl.ds(b, 1), :]
            li = left[1, a, pl.ds(b, 1), :]
            rr = right[0, b]
            ri = right[1, b]
            re = re + (lr * rr - li * ri)
            im = im + (lr * ri + li * rr)
        store(a, re, im)
        return carry

    lax.fori_loop(0, CHANS, body, 0)


def spread_medium(medium, kmap, spread):
    onehot = (iota((MOMS, LANES), 0) == kmap[...]).astype(F32).astype(BF16)
    for e in range(ENERGIES):
        for c in range(2):
            flat = medium[e, c].reshape(WIDE, MOMS)
            spread[e, c] = dot_exact(flat, onehot).reshape(CHANS, CHANS, LANES)


def kpoint_inner(structure, spread, factor, inner, e):
    y, g, f, h = spread.at[e], structure.at[e], factor.at[e], inner.at[e]

    def put_f(a, re, im):
        f[0, a] = re
        f[1, a] = im

    def put_h(a, re, im):
        h[0, a] = g[0, a] + re
        h[1, a] = g[1, a] + im

    kpoint_mul(put_f, y, g)
    kpoint_mul(put_h, g, f)


def kpoint_sums(inner, kmap, write_tile):
    rows, lanes = iota((WIDE, LANES), 0), kmap[...]
    onehot = jnp.transpose(((rows >> 4) == lanes).astype(F32)).astype(BF16)
    onehot = jnp.concatenate([onehot, onehot], axis=0)
    row_block = iota((WIDE, WIDE), 0) >> 4
    col_in = iota((WIDE, WIDE), 1) & 15
    keep = row_block == col_in
    for e in range(ENERGIES):
        for c in range(2):
            flat = inner[e, c].reshape(WIDE, LANES)
            parts = jnp.concatenate(split(flat), axis=1)
            by_mom = jnp.where(keep, dot(parts, onehot), 0.0)
            panel = jnp.sum(by_mom.reshape(CHANS, CHANS, WIDE), axis=0)
            for half in range(2):
                for side in range(2):
                    write_tile(
                        ((e * 2 + c) * 2 + half) * 2 + side,
                        panel[half * 8 : half * 8 + 8, side * LANES : side * LANES + LANES],
                    )


def kpoint_squares(spread, factor, tau, square, e):
    y, f, t, s = spread.at[e], factor.at[e], tau.at[e], square.at[e]

    def put_q(a, re, im):
        s[0, a] = f[0, a] + re
        s[1, a] = f[1, a] + im

    def put_t(a, re, im):
        t[0, a] = y[0, a] + re
        t[1, a] = y[1, a] + im

    def put_s(a, re, im):
        s[0, a] = re
        s[1, a] = im

    kpoint_mul(put_q, f, f)
    kpoint_mul(put_t, s, y)
    kpoint_mul(put_s, t, t)


def config_row(occupation, weight, row):
    lane = iota((8, LANES), 1)
    row[...] = jnp.where(lane == SITES, 1.0, 0.0) + jnp.where(
        lane == SITES + 1, weight[0], 0.0
    )
    row[:, 0:SITES] = jnp.broadcast_to(occupation[...].astype(F32), (8, SITES))


def moment_tables(configs, tab, rows_tab, shift_tab):
    turned = jnp.transpose(configs)
    count = turned[0:ALPHA]
    weight = turned[SITES + 1 : SITES + 2]
    weight = weight / jnp.sum(weight, axis=1, keepdims=True)
    live = iota((ALPHA, LANES), 0) <= SITES
    count = jnp.where(live, count, 0.0)
    weighted = count * weight
    flat = configs.astype(BF16)
    lane_r, lane_c = iota((LANES, WIDE), 0), iota((LANES, WIDE), 1)
    pick = (lane_r == (lane_c >> 4)).astype(F32).astype(BF16)
    wide = dot(flat, pick).astype(BF16)
    ones = jnp.ones((LANES, LANES), BF16)
    for s in range(SITES + 1):
        product = weighted * count[s : s + 1]
        rows_tab[s, :, 0:WIDE] = dot_exact(product, wide)
        rows_tab[s, :, WIDE : WIDE + LANES] = dot_exact(product, ones)
    r, c = iota((WIDE, LANES), 0), iota((WIDE, LANES), 1)
    move = (site_sum(r >> 4, r & 15) == c).astype(F32).astype(BF16)
    moved = dot(move, flat, NT)
    moved_b = moved.astype(BF16)
    own = dot(((r >> 4) == c).astype(F32).astype(BF16), flat, NT)
    base = moved * (weight * (1.0 / SITES))
    fold = (tab.row_in == tab.col_block).astype(F32).astype(BF16)
    for which, left in ((0, base), (1, base * own)):
        full = dot_exact(left, moved_b, NT)
        kept = jnp.where(tab.same_block, full, 0.0)
        small = jnp.sum(kept.reshape(SITES, SITES, WIDE), axis=0)
        lanes = dot_exact(small, fold)
        shift_tab[which] = jnp.broadcast_to(
            lanes[:, None, :], (SITES, CHANS, WIDE)
        ).reshape(WIDE, WIDE)


def medium_panels(medium, tab, e):
    out = []
    for c in range(2):
        flat = medium[e, c].reshape(WIDE, MOMS)
        pick = ((iota((MOMS, WIDE), 1) >> 4) == iota((MOMS, WIDE), 0)).astype(F32).astype(BF16)
        by_mom = jnp.where(tab.same_in, dot_exact(flat, pick), 0.0)
        out.append(jnp.sum(by_mom.reshape(CHANS, CHANS, WIDE), axis=1))
    return tuple(out)


def shift_panels(shift_a, shift_b, tab, e):
    def wide(x):
        return dot_exact(x, tab.pick_in)

    b = (wide(shift_b[e, 0]), wide(shift_b[e, 1]))
    c = (
        wide(shift_a[e, 0] - shift_b[e, 0]),
        wide(shift_a[e, 1] - shift_b[e, 1]),
    )
    return b, c


def coarse_panels(y, y_b, y_c, y_all, sum_t, tab, per_moment):
    left = cdot(y, block_diag_c(sum_t, tab), NT)
    scale = 1.0 / per_moment
    left = (left[0] * scale, left[1] * scale)
    out = []
    for base, parts in zip((y, y_b, y_c), y_all):
        step = cdot(left, parts)
        out.append((base[0] + step[0], base[1] + step[1]))
    return out


def first_rows(panels, lines, tab, site0):
    mom = iota((16, WIDE), 1) >> 4
    second = (iota((16, WIDE), 0) >> 3).astype(jnp.int32)
    cos, sin = cos_sin(quarter_turns(mom, site0 + second))
    left_r, left_i = [], []
    for panel, line in zip(panels, lines):
        lr, li = jnp.broadcast_to(line[0], (16, WIDE)), jnp.broadcast_to(line[1], (16, WIDE))
        left_r += [panel[0], lr * cos - li * sin]
        left_i += [panel[1], lr * sin + li * cos]
    rows = 32 * len(panels)
    both = jnp.concatenate(left_r + left_i, axis=0) * (1.0 / SITES)
    by_cos = dot_exact(both, tab.wave_cos, NT)
    by_sin = dot_exact(both, tab.wave_sin, NT)
    real = by_cos[:rows] + by_sin[rows:]
    imag = by_cos[rows:] - by_sin[:rows]
    out = []
    for at in range(0, rows, 32):
        out.append(
            (
                (real[at : at + 16], imag[at : at + 16]),
                (real[at + 16 : at + 32], imag[at + 16 : at + 32]),
            )
        )
    return out


def swap_blocks(x, bit):
    step = 16 * bit
    up = pltpu.roll(x, LANES - step, axis=1)
    if bit == 4:
        return up
    down = pltpu.roll(x, step, axis=1)
    high = ((iota(x.shape, 1) >> 4) & bit) != 0
    return jnp.where(high, down, up)


def all_swaps(x):
    out = {0: x}
    out[4] = swap_blocks(x, 4)
    for at in (0, 4):
        out[at | 2] = swap_blocks(out[at], 2)
    for at in (0, 2, 4, 6):
        out[at | 1] = swap_blocks(out[at], 1)
    return out


def translated(panel):
    low = all_swaps(panel[:, 0:LANES])
    top = all_swaps(panel[:, LANES:WIDE])

    def whole(a, b):
        rows = [jnp.concatenate([a[q], b[q]], axis=1) for q in range(8)]
        rows += [jnp.concatenate([b[q ^ 7], a[q]], axis=1) for q in range(8)]
        return jnp.concatenate(rows, axis=0)

    low_parts = {q: split(v) for q, v in low.items()}
    top_parts = {q: split(v) for q, v in top.items()}
    parts = tuple(
        whole({q: v[p] for q, v in low_parts.items()}, {q: v[p] for q, v in top_parts.items()})
        for p in range(2)
    )
    return whole(low, top), parts


def translated_c(panel):
    real, imag = translated(panel[0]), translated(panel[1])
    return (real[0], imag[0]), (real[1], imag[1])


def rows_stage(start, with_b, with_c, t_parts, tb_parts, tc_parts, rows_tab):
    row = iota((ALPHA, WIDE), 0)
    block = iota((ALPHA, WIDE), 1) >> 4

    def opened(c):
        out = []
        for at in (0, 8):
            ub = jnp.broadcast_to(with_b[c][at : at + 1], (ALPHA, WIDE))
            uc = jnp.broadcast_to(with_c[c][at : at + 1], (ALPHA, WIDE))
            out.append(jnp.where(row == block, uc, jnp.where(row == SITES, ub, 0.0)))
        return jnp.concatenate(out, axis=0)

    begin = (opened(0), opened(1))
    hop_b = cdot(begin, tb_parts)
    hop_c = cdot(begin, tc_parts)
    inner = []
    for c in range(2):
        out = []
        for site in range(2):
            g = jnp.zeros((ALPHA, WIDE), F32)
            for s in range(SITES + 1):
                at = site * ALPHA + s
                pair = rows_tab[s, :, WIDE : WIDE + LANES]
                g = g + jnp.concatenate([pair, pair], axis=1) * hop_b[c][at : at + 1]
                g = g + rows_tab[s, :, 0:WIDE] * hop_c[c][at : at + 1]
            out.append(g)
        inner.append(jnp.concatenate(out, axis=0))
    mean = rows_tab[SITES, SITES : SITES + 1, 0:WIDE]

    def eight(parts):
        return jnp.concatenate([jnp.broadcast_to(p, (8, WIDE)) for p in parts], axis=0)

    ends = tuple(
        eight([inner[c][site * ALPHA + SITES : site * ALPHA + SITES + 1] for site in range(2)])
        for c in range(2)
    )
    by_b = cdot(ends, tb_parts)
    by_c = cdot(tuple(inner), tc_parts)
    z = []
    for c in range(2):
        picked = []
        for site in range(2):
            lines = by_c[c][site * ALPHA : site * ALPHA + ALPHA]
            picked.append(jnp.sum(jnp.where(row == block, lines, 0.0), axis=0, keepdims=True))
        z.append(with_b[c] + with_c[c] * mean - ends[c] + by_b[c] + eight(picked))
    last = cdot(tuple(z), t_parts)
    return start[0] - last[0], start[1] - last[1]


def moment_stage(top_b, top_c, tc_full, tb_parts, tc_parts, x, x_parts, b_wide, c_wide, shift_tab, tab):
    def head(wide):
        return wide[0][:, 0:CHANS], wide[1][:, 0:CHANS]

    b_in, c_in = head(b_wide), head(c_wide)
    small = (
        jnp.concatenate([b_in[0], c_in[0]], axis=0),
        jnp.concatenate([b_in[1], c_in[1]], axis=0),
    )
    lead_b = cdot(small, csplit(top_b))
    lead_c = cdot(small, csplit(top_c))
    bb, cb = [v[0:CHANS] for v in lead_b], [v[CHANS:] for v in lead_b]
    bc, cc = [v[0:CHANS] for v in lead_c], [v[CHANS:] for v in lead_c]
    two = shift_tab[1, 0:1, :]
    mean = shift_tab[1, 0:1, 0:1]
    zero = [bb[c] + mean * (bc[c] + cb[c]) + two * cc[c] for c in range(2)]
    by_b = cdot(tuple(zero), tb_parts)
    by_c = cdot(tuple(jnp.concatenate([bb[c], cb[c]], axis=0) for c in range(2)), tc_parts)

    def scaled(which):
        return split(tc_full[0] * shift_tab[which]), split(tc_full[1] * shift_tab[which])

    pair = cdot(tuple(bc), scaled(0))
    triple = cdot(tuple(cc), scaled(1))
    line = []
    for c in range(2):
        third = by_b[c] + mean * by_c[c][0:CHANS] + two * by_c[c][CHANS:] + pair[c] + triple[c]
        line.append(third - (bb[c] + mean * (cb[c] + bc[c]) + two * cc[c]))
    m_cos = dot_exact(jnp.concatenate(line, axis=0), tab.wave_cos)
    m_sin = dot_exact(jnp.concatenate(line, axis=0), tab.wave_sin)
    m_r = m_cos[:CHANS] - m_sin[CHANS:] + b_wide[0] + mean * c_wide[0]
    m_i = m_sin[:CHANS] + m_cos[CHANS:] + b_wide[1] + mean * c_wide[1]
    d = cdot(cdot(x, block_diag_c((m_r, m_i), tab)), x_parts)
    return -d[0], -d[1]


def correction_stage(d, square, e, kmap, tab):
    onehot = ((iota((WIDE, LANES), 0) >> 4) == kmap[...]).astype(F32).astype(BF16)
    keep = tab.row_block == tab.col_in

    def spread(panel):
        high, low = split(panel)

        def one(part):
            full = jnp.where(keep, tile_rows(part.astype(F32), CHANS), 0.0)
            return dot(full.astype(BF16), onehot)

        return one(high) + one(low)

    dr, di = spread(d[0]), spread(d[1])
    sr, si = square[e, 0].reshape(WIDE, LANES), square[e, 1].reshape(WIDE, LANES)
    re = jnp.sum(dr * sr - di * si, axis=0, keepdims=True)
    im = jnp.sum(dr * si + di * sr, axis=0, keepdims=True)
    return re, im


def coarse_out(x, tab, store):
    fold = (tab.col_block == tab.row_in)
    pick = (iota((WIDE, MOMS), 0) >> 4 == iota((WIDE, MOMS), 1)).astype(F32).astype(BF16)
    high = x.astype(BF16)
    rest = x - high.astype(F32)
    mid = rest.astype(BF16)
    low = (rest - mid.astype(F32)).astype(BF16)
    total = None
    for part in (low, mid, high):
        wide = jnp.broadcast_to(part.astype(F32)[:, None, :], (CHANS, CHANS, WIDE))
        wide = jnp.where(tab.same_in, wide.reshape(WIDE, WIDE), 0.0).astype(BF16)
        piece = dot(wide, pick)
        total = piece if total is None else total + piece
    store(total.reshape(CHANS, CHANS, MOMS))


def gathered_panel(tiles, at):
    top = jnp.concatenate([tiles[at // 2, 0], tiles[at // 2, 1]], axis=1)
    low = jnp.concatenate([tiles[at // 2 + 1, 0], tiles[at // 2 + 1, 1]], axis=1)
    return jnp.concatenate([top, low], axis=0)


class Exchange:
    def __init__(self, axis, count, slots, send, recv):
        self.axis, self.count = axis, count
        self.slots, self.send, self.recv = slots, send, recv
        self.me = lax.axis_index(axis)

    def peer(self, d):
        return lax.rem(self.me + d, self.count)

    def copy(self, src, at, d):
        return pltpu.make_async_remote_copy(
            src_ref=src, dst_ref=self.slots.at[at], send_sem=self.send.at[d],
            recv_sem=self.recv.at[at], device_id={self.axis: self.peer(d)}, device_id_type=MESH,
        )

    def start(self, source):
        for d in range(1, self.count):
            self.copy(source(self.peer(d)), self.me, d).start()

    def wait(self, source):
        for d in range(1, self.count):
            self.copy(source(self.me), self.peer(d), d).wait_recv()

    def drain(self, source):
        for d in range(1, self.count):
            self.copy(source(self.me), self.me, d).wait_send()


def greet(n_ka, n_cfg):
    barrier = pltpu.get_barrier_semaphore()
    for axis, count in (("ka", n_ka), ("cfg", n_cfg)):
        me = lax.axis_index(axis)
        for d in range(1, count):
            pl.semaphore_signal(
                barrier, inc=1, device_id={axis: lax.rem(me + d, count)}, device_id_type=MESH
            )
    return barrier


def kernel(
    per_moment, n_ka, n_cfg,
    structure_hbm, medium_hbm, kmap_hbm, occupation_hbm, weight, shift_a_hbm, shift_b_hbm,
    coarse, average, correction,
    structure, medium, kmap, occupation, shift_a, shift_b,
    spread, factor, inner, square, panels, rows_tab, shift_tab,
    row, own_rows, outgoing, first, part, total, block, slots,
    load_sem, row_send, row_recv, first_send, first_recv, part_send, part_recv,
    total_send, total_recv, slot_send, slot_recv,
):
    pairs = (
        (medium_hbm, medium), (kmap_hbm, kmap), (structure_hbm, structure),
        (occupation_hbm, occupation), (shift_a_hbm, shift_a), (shift_b_hbm, shift_b),
    )
    loads = [
        pltpu.make_async_copy(source, to, load_sem.at[at]) for at, (source, to) in enumerate(pairs)
    ]
    for load in loads:
        load.start()
    barrier = greet(n_ka, n_cfg)
    rows_x = Exchange("cfg", n_cfg, own_rows, row_send, row_recv)
    first_x = Exchange("cfg", n_cfg, first, first_send, first_recv)
    part_x = Exchange("ka", n_ka, part, part_send, part_recv)
    total_x = Exchange("cfg", n_cfg, total, total_send, total_recv)
    slot_x = Exchange("ka", n_ka, slots, slot_send, slot_recv)
    ka, cfg = part_x.me, rows_x.me
    loads[0].wait()
    loads[1].wait()
    spread_medium(medium, kmap, spread)
    loads[2].wait()
    kpoint_inner(structure, spread, factor, inner, 0)
    for load in loads[3:]:
        load.wait()
    config_row(occupation, weight, row)
    pl.semaphore_wait(barrier, n_ka + n_cfg - 2)
    rows_x.start(lambda to: row)
    own_rows[cfg] = row[...]
    kpoint_inner(structure, spread, factor, inner, 1)

    def write(at, value):
        outgoing[at // 2, at % 2] = value

    kpoint_sums(inner, kmap, write)
    first_x.start(lambda to: outgoing.at[to])
    first[cfg] = outgoing[cfg]
    kpoint_squares(spread, factor, inner, square, 0)
    rows_x.wait(lambda to: row)
    line = iota((8, LANES), 0)
    group = jnp.zeros((8, LANES), F32)
    for at in range(n_cfg):
        group = group + jnp.where(line == at, own_rows[at], 0.0)
    first_x.wait(lambda to: outgoing.at[to])
    value = [first[0, 0], first[0, 1]]
    for at in range(1, n_cfg):
        value = [value[0] + first[at, 0], value[1] + first[at, 1]]
    part[ka, 0] = value[0]
    part[ka, 1] = value[1]
    part[ka, 2] = group
    part_x.start(lambda to: part.at[ka])
    kpoint_squares(spread, factor, inner, square, 1)
    tab = Tables()
    energies = range(ENERGIES)
    y = [medium_panels(medium, tab, e) for e in energies]
    wide = [shift_panels(shift_a, shift_b, tab, e) for e in energies]
    y_b = [cdot(y[e], block_diag_c(wide[e][0], tab)) for e in energies]
    y_c = [cdot(y[e], block_diag_c(wide[e][1], tab)) for e in energies]
    y_all = [
        (block_diag_c(y[e], tab), block_diag_c(y_b[e], tab), block_diag_c(y_c[e], tab))
        for e in energies
    ]
    part_x.wait(lambda to: part.at[ka])
    value = [part[0, 0], part[0, 1]]
    for at in range(1, n_ka):
        value = [value[0] + part[at, 0], value[1] + part[at, 1]]
    total[cfg, 0] = value[0]
    total[cfg, 1] = value[1]
    total_x.start(lambda to: total.at[cfg])
    configs = jnp.concatenate([part[at, 2] for at in range(n_ka)], axis=0)
    moment_tables(configs, tab, rows_tab, shift_tab)
    total_x.wait(lambda to: total.at[cfg])
    which = iota((8, WIDE), 0)
    out = jnp.zeros((8, WIDE), F32)
    kept = []
    for e in energies:
        sum_t = (gathered_panel(total, e * 8), gathered_panel(total, e * 8 + 4))
        x, x_b, x_c = coarse_panels(y[e], y_b[e], y_c[e], y_all[e], sum_t, tab, per_moment)
        lines = []
        for at, panel in enumerate((x, x_b, x_c)):
            panels[e, at, 0] = panel[0]
            panels[e, at, 1] = panel[1]
            lines.append(
                (panels[e, at, 0, pl.ds(ka, 1), :], panels[e, at, 1, pl.ds(ka, 1), :])
            )
        (top, start), (top_b, with_b), (top_c, with_c) = first_rows(
            (x, x_b, x_c), lines, tab, cfg * 2
        )
        t_parts = translated_c(top)[1]
        tb_parts = translated_c(top_b)[1]
        tc_full, tc_parts = translated_c(top_c)
        avg = rows_stage(start, with_b, with_c, t_parts, tb_parts, tc_parts, rows_tab)
        for c in range(2):
            for site in range(2):
                at = e * 4 + c * 2 + site
                out = jnp.where(which == at, avg[c][site * 8 : site * 8 + 8], out)
        kept.append((top_b, top_c, tc_full, tb_parts, tc_parts, x))
    block[...] = out
    slot_x.start(lambda to: block)
    slots[ka] = out
    for e in energies:
        x = kept[e][5]
        d = moment_stage(
            *kept[e], block_diag_c(x, tab), wide[e][0], wide[e][1], shift_tab, tab
        )
        re, im = correction_stage(d, square, e, kmap, tab)
        correction[e, 0:1, :] = re
        correction[e, 1:2, :] = im
        for c in range(2):

            def store(value, e=e, c=c):
                coarse[e, c] = value

            coarse_out(x[c], tab, store)
    slot_x.wait(lambda to: block)
    for at in range(n_ka):
        for e in energies:
            for c in range(2):
                for site in range(2):
                    line = e * 4 + c * 2 + site
                    to = site * CHANS + at
                    average[e, c, to : to + 1, :] = slots[at, line : line + 1, :]
    rows_x.drain(lambda to: row)
    first_x.drain(lambda to: outgoing.at[to])
    part_x.drain(lambda to: part.at[ka])
    total_x.drain(lambda to: total.at[cfg])
    slot_x.drain(lambda to: block)


def output_kernel(coarse, average, correction, coarse_out_ref, average_out, correction_out, sem):
    pairs = ((coarse, coarse_out_ref), (average, average_out), (correction, correction_out))
    copies = [pltpu.make_async_copy(a, b, sem.at[at]) for at, (a, b) in enumerate(pairs)]
    for copy in copies:
        copy.start()
    for copy in copies:
        copy.wait()


def shape(*dims):
    return jax.ShapeDtypeStruct(dims, F32)


VMEM_SPEC = pl.BlockSpec(memory_space=pltpu.VMEM)
SMEM_SPEC = pl.BlockSpec(memory_space=pltpu.SMEM)


def per_device(medium_t, structure, kmap, occupation, cfg_weight, shift_a, shift_b):
    n_ka, n_cfg = lax.axis_size("ka"), lax.axis_size("cfg")
    per_moment = kmap.shape[0] * n_ka * n_cfg // MOMS
    kmap = kmap.reshape(1, LANES)
    kdims = (ENERGIES, 2, CHANS, CHANS, LANES)
    dma = pltpu.SemaphoreType.DMA

    def vmem(*dims):
        return pltpu.VMEM(dims, F32)

    any_spec = pl.BlockSpec(memory_space=pl.ANY)
    shapes = (
        shape(ENERGIES, 2, CHANS, CHANS, MOMS),
        shape(ENERGIES, 2, 2 * CHANS, WIDE),
        shape(ENERGIES, 2, LANES),
    )
    results = pl.pallas_call(
        functools.partial(kernel, per_moment, n_ka, n_cfg),
        out_shape=shapes,
        in_specs=[any_spec] * 4 + [SMEM_SPEC] + [any_spec] * 2,
        out_specs=(VMEM_SPEC,) * 3,
        scratch_shapes=[
            vmem(*kdims), vmem(ENERGIES, 2, CHANS, CHANS, MOMS),
            pltpu.VMEM((1, LANES), jnp.int32), pltpu.VMEM((1, SITES), jnp.int32),
            vmem(ENERGIES, 2, CHANS, CHANS), vmem(ENERGIES, 2, CHANS, CHANS),
            vmem(*kdims), vmem(*kdims), vmem(*kdims), vmem(*kdims),
            vmem(ENERGIES, 3, 2, CHANS, WIDE),
            vmem(SITES + 1, ALPHA, WIDE + LANES),
            vmem(2, WIDE, WIDE),
            vmem(8, LANES), vmem(n_cfg, 8, LANES),
            vmem(n_cfg, 2, 8, LANES), vmem(n_cfg, 2, 8, LANES),
            vmem(n_ka, 3, 8, LANES), vmem(n_cfg, 2, 8, LANES),
            vmem(8, WIDE), vmem(n_ka, 8, WIDE),
            dma((6,)),
            dma((n_cfg,)), dma((n_cfg,)),
            dma((n_cfg,)), dma((n_cfg,)),
            dma((n_ka,)), dma((n_ka,)),
            dma((n_cfg,)), dma((n_cfg,)),
            dma((n_ka,)), dma((n_ka,)),
        ],
        compiler_params=pltpu.CompilerParams(
            collective_id=0, has_side_effects=True, vmem_limit_bytes=56 * 1024 * 1024
        ),
    )(structure, medium_t, kmap, occupation, cfg_weight, shift_a, shift_b)
    return pl.pallas_call(
        output_kernel,
        out_shape=shapes,
        in_specs=[any_spec] * 3,
        out_specs=(any_spec,) * 3,
        scratch_shapes=[dma((3,))],
    )(*results)


def solution(mesh):
    placed = (
        P(),
        P(None, None, None, None, ("ka", "cfg")),
        P(("ka", "cfg")),
        P(("ka", "cfg"), None),
        P(("ka", "cfg")),
        P(),
        P(),
    )
    return jax.shard_map(
        per_device,
        mesh=mesh,
        in_specs=placed,
        out_specs=(P(), P(None, None, "cfg", None), P(None, None, ("ka", "cfg"))),
        check_vma=False,
    )
```

```python
import functools

import jax
import jax.numpy as jnp
from jax import lax
from jax.experimental import pallas as pl
from jax.experimental.pallas import tpu as pltpu
from jax.sharding import PartitionSpec as P

MESH = pl.DeviceIdType.MESH
F32 = jnp.float32
BF16 = jnp.bfloat16
NN = (((1,), (0,)), ((), ()))
NT = (((1,), (1,)), ((), ()))

ENERGIES = 2
SITES = 16
CHANS = 16
MOMS = 16
WIDE = SITES * CHANS
LANES = 128
ALPHA = 24


def split(x):
    high = x.astype(BF16)
    return high, (x - high.astype(F32)).astype(BF16)


def dot(left, right, dims=NN):
    return lax.dot_general(left, right, dims, preferred_element_type=F32)


def dot_exact(x, right, dims=NN):
    high, low = split(x)
    rows = x.shape[0]
    both = dot(jnp.concatenate([high, low], axis=0), right, dims)
    return both[:rows] + both[rows:]


def dot3(x, right, dims=NN):
    high, low = split(x)
    rows = x.shape[0]
    both = dot(jnp.concatenate([high, low], axis=0), right[0], dims)
    return both[:rows] + (both[rows:] + dot(high, right[1], dims))


def cdot(x, right, dims=NN):
    rows = x[0].shape[0]
    both = jnp.concatenate([x[0], x[1]], axis=0)
    by_re = dot3(both, right[0], dims)
    by_im = dot3(both, right[1], dims)
    return by_re[:rows] - by_im[rows:], by_im[:rows] + by_re[rows:]


def csplit(x):
    return split(x[0]), split(x[1])


def iota(shape, axis):
    return lax.broadcasted_iota(jnp.int32, shape, axis)


def tile_rows(x, times):
    return jnp.concatenate([x] * times, axis=0)


def quarter_turns(mom, site):
    half = site >> 3
    x = 2 * ((site >> 2) & 1) + half
    y = 2 * ((site >> 1) & 1) + half
    z = 2 * (site & 1) + half
    return ((mom >> 2) * x + ((mom >> 1) & 1) * y + (mom & 1) * z) & 3


def cos_sin(turns):
    sign = (1 - (turns & 2)).astype(F32)
    odd = (turns & 1) == 1
    return jnp.where(odd, 0.0, sign), jnp.where(odd, sign, 0.0)


def site_sum(first, second):
    carry = (first & second) >> 3
    return (first ^ second) ^ (7 * carry)


class Tables:
    def __init__(self):
        rows, cols = iota((WIDE, WIDE), 0), iota((WIDE, WIDE), 1)
        self.row_block, self.col_block = rows >> 4, cols >> 4
        self.row_in, self.col_in = rows & 15, cols & 15
        self.same_block = self.row_block == self.col_block
        self.same_in = self.row_in == self.col_in
        self.cos, self.sin = cos_sin(quarter_turns(self.col_block, self.row_block))
        self.wave_cos = jnp.where(self.same_in, self.cos, 0.0).astype(BF16)
        self.wave_sin = jnp.where(self.same_in, self.sin, 0.0).astype(BF16)
        small_r, small_c = iota((SITES, WIDE), 0), iota((SITES, WIDE), 1)
        self.pick_in = (small_r == (small_c & 15)).astype(F32).astype(BF16)
        self.pick_block = (small_r == (small_c >> 4)).astype(F32).astype(BF16)


def block_diag(panel, tab):
    def spread(part):
        return jnp.where(tab.same_block, tile_rows(part.astype(F32), SITES), 0.0).astype(BF16)

    high, low = split(panel)
    return spread(high), spread(low)


def block_diag_c(panel, tab):
    return block_diag(panel[0], tab), block_diag(panel[1], tab)


def kpoint_mul(store, left, right):
    def body(a, carry):
        re = jnp.zeros((CHANS, LANES), F32)
        im = jnp.zeros((CHANS, LANES), F32)
        for b in range(CHANS):
            lr = left[0, a, pl.ds(b, 1), :]
            li = left[1, a, pl.ds(b, 1), :]
            rr = right[0, b]
            ri = right[1, b]
            re = re + (lr * rr - li * ri)
            im = im + (lr * ri + li * rr)
        store(a, re, im)
        return carry

    lax.fori_loop(0, CHANS, body, 0)


def spread_medium(medium, kmap, spread):
    onehot = (iota((MOMS, LANES), 0) == kmap[...]).astype(F32).astype(BF16)
    for e in range(ENERGIES):
        for c in range(2):
            flat = medium[e, c].reshape(WIDE, MOMS)
            spread[e, c] = dot_exact(flat, onehot).reshape(CHANS, CHANS, LANES)


def kpoint_inner(structure, spread, factor, inner, e):
    y, g, f, h = spread.at[e], structure.at[e], factor.at[e], inner.at[e]

    def put_f(a, re, im):
        f[0, a] = re
        f[1, a] = im

    def put_h(a, re, im):
        h[0, a] = g[0, a] + re
        h[1, a] = g[1, a] + im

    kpoint_mul(put_f, y, g)
    kpoint_mul(put_h, g, f)


def kpoint_sums(inner, kmap, write_tile):
    rows, lanes = iota((WIDE, LANES), 0), kmap[...]
    onehot = jnp.transpose(((rows >> 4) == lanes).astype(F32)).astype(BF16)
    onehot = jnp.concatenate([onehot, onehot], axis=0)
    row_block = iota((WIDE, WIDE), 0) >> 4
    col_in = iota((WIDE, WIDE), 1) & 15
    keep = row_block == col_in
    for e in range(ENERGIES):
        for c in range(2):
            flat = inner[e, c].reshape(WIDE, LANES)
            parts = jnp.concatenate(split(flat), axis=1)
            by_mom = jnp.where(keep, dot(parts, onehot), 0.0)
            panel = jnp.sum(by_mom.reshape(CHANS, CHANS, WIDE), axis=0)
            for half in range(2):
                for side in range(2):
                    write_tile(
                        ((e * 2 + c) * 2 + half) * 2 + side,
                        panel[half * 8 : half * 8 + 8, side * LANES : side * LANES + LANES],
                    )


def kpoint_squares(spread, factor, tau, square, e):
    y, f, t, s = spread.at[e], factor.at[e], tau.at[e], square.at[e]

    def put_q(a, re, im):
        s[0, a] = f[0, a] + re
        s[1, a] = f[1, a] + im

    def put_t(a, re, im):
        t[0, a] = y[0, a] + re
        t[1, a] = y[1, a] + im

    def put_s(a, re, im):
        s[0, a] = re
        s[1, a] = im

    kpoint_mul(put_q, f, f)
    kpoint_mul(put_t, s, y)
    kpoint_mul(put_s, t, t)


def config_row(occupation, weight, row):
    lane = iota((8, LANES), 1)
    row[...] = jnp.where(lane == SITES, 1.0, 0.0) + jnp.where(
        lane == SITES + 1, weight[0], 0.0
    )
    row[:, 0:SITES] = jnp.broadcast_to(occupation[...].astype(F32), (8, SITES))


def moment_tables(configs, tab, rows_tab, shift_tab):
    turned = jnp.transpose(configs)
    count = turned[0:ALPHA]
    weight = turned[SITES + 1 : SITES + 2]
    weight = weight / jnp.sum(weight, axis=1, keepdims=True)
    live = iota((ALPHA, LANES), 0) <= SITES
    count = jnp.where(live, count, 0.0)
    weighted = count * weight
    flat = configs.astype(BF16)
    lane_r, lane_c = iota((LANES, WIDE), 0), iota((LANES, WIDE), 1)
    pick = (lane_r == (lane_c >> 4)).astype(F32).astype(BF16)
    wide = dot(flat, pick).astype(BF16)
    ones = jnp.ones((LANES, LANES), BF16)
    for s in range(SITES + 1):
        product = weighted * count[s : s + 1]
        rows_tab[s, :, 0:WIDE] = dot_exact(product, wide)
        rows_tab[s, :, WIDE : WIDE + LANES] = dot_exact(product, ones)
    r, c = iota((WIDE, LANES), 0), iota((WIDE, LANES), 1)
    move = (site_sum(r >> 4, r & 15) == c).astype(F32).astype(BF16)
    moved = dot(move, flat, NT)
    moved_b = moved.astype(BF16)
    own = dot(((r >> 4) == c).astype(F32).astype(BF16), flat, NT)
    base = moved * (weight * (1.0 / SITES))
    fold = (tab.row_in == tab.col_block).astype(F32).astype(BF16)
    for which, left in ((0, base), (1, base * own)):
        full = dot_exact(left, moved_b, NT)
        kept = jnp.where(tab.same_block, full, 0.0)
        small = jnp.sum(kept.reshape(SITES, SITES, WIDE), axis=0)
        lanes = dot_exact(small, fold)
        shift_tab[which] = jnp.broadcast_to(
            lanes[:, None, :], (SITES, CHANS, WIDE)
        ).reshape(WIDE, WIDE)


def medium_panels(medium, tab, e):
    out = []
    for c in range(2):
        flat = medium[e, c].reshape(WIDE, MOMS)
        pick = ((iota((MOMS, WIDE), 1) >> 4) == iota((MOMS, WIDE), 0)).astype(F32).astype(BF16)
        by_mom = jnp.where(tab.same_in, dot_exact(flat, pick), 0.0)
        out.append(jnp.sum(by_mom.reshape(CHANS, CHANS, WIDE), axis=1))
    return tuple(out)


def shift_panels(shift_a, shift_b, tab, e):
    def wide(x):
        return dot_exact(x, tab.pick_in)

    b = (wide(shift_b[e, 0]), wide(shift_b[e, 1]))
    c = (
        wide(shift_a[e, 0] - shift_b[e, 0]),
        wide(shift_a[e, 1] - shift_b[e, 1]),
    )
    return b, c


def coarse_panels(y, y_b, y_c, y_all, sum_t, tab, per_moment):
    left = cdot(y, block_diag_c(sum_t, tab), NT)
    scale = 1.0 / per_moment
    left = (left[0] * scale, left[1] * scale)
    out = []
    for base, parts in zip((y, y_b, y_c), y_all):
        step = cdot(left, parts)
        out.append((base[0] + step[0], base[1] + step[1]))
    return out


def first_rows(panels, lines, tab, site0):
    mom = iota((16, WIDE), 1) >> 4
    second = (iota((16, WIDE), 0) >> 3).astype(jnp.int32)
    cos, sin = cos_sin(quarter_turns(mom, site0 + second))
    left_r, left_i = [], []
    for panel, line in zip(panels, lines):
        lr, li = jnp.broadcast_to(line[0], (16, WIDE)), jnp.broadcast_to(line[1], (16, WIDE))
        left_r += [panel[0], lr * cos - li * sin]
        left_i += [panel[1], lr * sin + li * cos]
    rows = 32 * len(panels)
    both = jnp.concatenate(left_r + left_i, axis=0) * (1.0 / SITES)
    by_cos = dot_exact(both, tab.wave_cos, NT)
    by_sin = dot_exact(both, tab.wave_sin, NT)
    real = by_cos[:rows] + by_sin[rows:]
    imag = by_cos[rows:] - by_sin[:rows]
    out = []
    for at in range(0, rows, 32):
        out.append(
            (
                (real[at : at + 16], imag[at : at + 16]),
                (real[at + 16 : at + 32], imag[at + 16 : at + 32]),
            )
        )
    return out


def swap_blocks(x, bit):
    step = 16 * bit
    up = pltpu.roll(x, LANES - step, axis=1)
    if bit == 4:
        return up
    down = pltpu.roll(x, step, axis=1)
    high = ((iota(x.shape, 1) >> 4) & bit) != 0
    return jnp.where(high, down, up)


def all_swaps(x):
    out = {0: x}
    out[4] = swap_blocks(x, 4)
    for at in (0, 4):
        out[at | 2] = swap_blocks(out[at], 2)
    for at in (0, 2, 4, 6):
        out[at | 1] = swap_blocks(out[at], 1)
    return out


def translated(panel):
    low = all_swaps(panel[:, 0:LANES])
    top = all_swaps(panel[:, LANES:WIDE])

    def whole(a, b):
        rows = [jnp.concatenate([a[q], b[q]], axis=1) for q in range(8)]
        rows += [jnp.concatenate([b[q ^ 7], a[q]], axis=1) for q in range(8)]
        return jnp.concatenate(rows, axis=0)

    low_parts = {q: split(v) for q, v in low.items()}
    top_parts = {q: split(v) for q, v in top.items()}
    parts = tuple(
        whole({q: v[p] for q, v in low_parts.items()}, {q: v[p] for q, v in top_parts.items()})
        for p in range(2)
    )
    return whole(low, top), parts


def translated_c(panel):
    real, imag = translated(panel[0]), translated(panel[1])
    return (real[0], imag[0]), (real[1], imag[1])


def rows_stage(start, with_b, with_c, t_parts, tb_parts, tc_parts, rows_tab):
    row = iota((ALPHA, WIDE), 0)
    block = iota((ALPHA, WIDE), 1) >> 4

    def opened(c):
        out = []
        for at in (0, 8):
            ub = jnp.broadcast_to(with_b[c][at : at + 1], (ALPHA, WIDE))
            uc = jnp.broadcast_to(with_c[c][at : at + 1], (ALPHA, WIDE))
            out.append(jnp.where(row == block, uc, jnp.where(row == SITES, ub, 0.0)))
        return jnp.concatenate(out, axis=0)

    begin = (opened(0), opened(1))
    hop_b = cdot(begin, tb_parts)
    hop_c = cdot(begin, tc_parts)
    inner = []
    for c in range(2):
        out = []
        for site in range(2):
            g = jnp.zeros((ALPHA, WIDE), F32)
            for s in range(SITES + 1):
                at = site * ALPHA + s
                pair = rows_tab[s, :, WIDE : WIDE + LANES]
                g = g + jnp.concatenate([pair, pair], axis=1) * hop_b[c][at : at + 1]
                g = g + rows_tab[s, :, 0:WIDE] * hop_c[c][at : at + 1]
            out.append(g)
        inner.append(jnp.concatenate(out, axis=0))
    mean = rows_tab[SITES, SITES : SITES + 1, 0:WIDE]

    def eight(parts):
        return jnp.concatenate([jnp.broadcast_to(p, (8, WIDE)) for p in parts], axis=0)

    ends = tuple(
        eight([inner[c][site * ALPHA + SITES : site * ALPHA + SITES + 1] for site in range(2)])
        for c in range(2)
    )
    by_b = cdot(ends, tb_parts)
    by_c = cdot(tuple(inner), tc_parts)
    z = []
    for c in range(2):
        picked = []
        for site in range(2):
            lines = by_c[c][site * ALPHA : site * ALPHA + ALPHA]
            picked.append(jnp.sum(jnp.where(row == block, lines, 0.0), axis=0, keepdims=True))
        z.append(with_b[c] + with_c[c] * mean - ends[c] + by_b[c] + eight(picked))
    last = cdot(tuple(z), t_parts)
    return start[0] - last[0], start[1] - last[1]


def moment_stage(top_b, top_c, tc_full, tb_parts, tc_parts, x, x_parts, b_wide, c_wide, shift_tab, tab):
    def head(wide):
        return wide[0][:, 0:CHANS], wide[1][:, 0:CHANS]

    b_in, c_in = head(b_wide), head(c_wide)
    small = (
        jnp.concatenate([b_in[0], c_in[0]], axis=0),
        jnp.concatenate([b_in[1], c_in[1]], axis=0),
    )
    lead_b = cdot(small, csplit(top_b))
    lead_c = cdot(small, csplit(top_c))
    bb, cb = [v[0:CHANS] for v in lead_b], [v[CHANS:] for v in lead_b]
    bc, cc = [v[0:CHANS] for v in lead_c], [v[CHANS:] for v in lead_c]
    two = shift_tab[1, 0:1, :]
    mean = shift_tab[1, 0:1, 0:1]
    zero = [bb[c] + mean * (bc[c] + cb[c]) + two * cc[c] for c in range(2)]
    by_b = cdot(tuple(zero), tb_parts)
    by_c = cdot(tuple(jnp.concatenate([bb[c], cb[c]], axis=0) for c in range(2)), tc_parts)

    def scaled(which):
        return split(tc_full[0] * shift_tab[which]), split(tc_full[1] * shift_tab[which])

    pair = cdot(tuple(bc), scaled(0))
    triple = cdot(tuple(cc), scaled(1))
    line = []
    for c in range(2):
        third = by_b[c] + mean * by_c[c][0:CHANS] + two * by_c[c][CHANS:] + pair[c] + triple[c]
        line.append(third - (bb[c] + mean * (cb[c] + bc[c]) + two * cc[c]))
    m_cos = dot_exact(jnp.concatenate(line, axis=0), tab.wave_cos)
    m_sin = dot_exact(jnp.concatenate(line, axis=0), tab.wave_sin)
    m_r = m_cos[:CHANS] - m_sin[CHANS:] + b_wide[0] + mean * c_wide[0]
    m_i = m_sin[:CHANS] + m_cos[CHANS:] + b_wide[1] + mean * c_wide[1]
    d = cdot(cdot(x, block_diag_c((m_r, m_i), tab)), x_parts)
    return -d[0], -d[1]


def correction_stage(d, square, e, kmap, tab):
    onehot = ((iota((WIDE, LANES), 0) >> 4) == kmap[...]).astype(F32).astype(BF16)
    keep = tab.row_block == tab.col_in

    def spread(panel):
        high, low = split(panel)

        def one(part):
            full = jnp.where(keep, tile_rows(part.astype(F32), CHANS), 0.0)
            return dot(full.astype(BF16), onehot)

        return one(high) + one(low)

    dr, di = spread(d[0]), spread(d[1])
    sr, si = square[e, 0].reshape(WIDE, LANES), square[e, 1].reshape(WIDE, LANES)
    re = jnp.sum(dr * sr - di * si, axis=0, keepdims=True)
    im = jnp.sum(dr * si + di * sr, axis=0, keepdims=True)
    return re, im


def coarse_out(x, tab, store):
    fold = (tab.col_block == tab.row_in)
    pick = (iota((WIDE, MOMS), 0) >> 4 == iota((WIDE, MOMS), 1)).astype(F32).astype(BF16)
    high = x.astype(BF16)
    rest = x - high.astype(F32)
    mid = rest.astype(BF16)
    low = (rest - mid.astype(F32)).astype(BF16)
    total = None
    for part in (low, mid, high):
        wide = jnp.broadcast_to(part.astype(F32)[:, None, :], (CHANS, CHANS, WIDE))
        wide = jnp.where(tab.same_in, wide.reshape(WIDE, WIDE), 0.0).astype(BF16)
        piece = dot(wide, pick)
        total = piece if total is None else total + piece
    store(total.reshape(CHANS, CHANS, MOMS))


def gathered_panel(tiles, at):
    top = jnp.concatenate([tiles[at // 2, 0], tiles[at // 2, 1]], axis=1)
    low = jnp.concatenate([tiles[at // 2 + 1, 0], tiles[at // 2 + 1, 1]], axis=1)
    return jnp.concatenate([top, low], axis=0)


class Exchange:
    def __init__(self, axis, count, slots, send, recv):
        self.axis, self.count = axis, count
        self.slots, self.send, self.recv = slots, send, recv
        self.me = lax.axis_index(axis)

    def peer(self, d):
        return lax.rem(self.me + d, self.count)

    def copy(self, src, at, d):
        return pltpu.make_async_remote_copy(
            src_ref=src, dst_ref=self.slots.at[at], send_sem=self.send.at[d],
            recv_sem=self.recv.at[at], device_id={self.axis: self.peer(d)}, device_id_type=MESH,
        )

    def start(self, source):
        for d in range(1, self.count):
            self.copy(source(self.peer(d)), self.me, d).start()

    def wait(self, source):
        for d in range(1, self.count):
            self.copy(source(self.me), self.peer(d), d).wait_recv()

    def drain(self, source):
        for d in range(1, self.count):
            self.copy(source(self.me), self.me, d).wait_send()


def greet(n_ka, n_cfg):
    barrier = pltpu.get_barrier_semaphore()
    for axis, count in (("ka", n_ka), ("cfg", n_cfg)):
        me = lax.axis_index(axis)
        for d in range(1, count):
            pl.semaphore_signal(
                barrier, inc=1, device_id={axis: lax.rem(me + d, count)}, device_id_type=MESH
            )
    return barrier


def kernel(
    per_moment, n_ka, n_cfg,
    structure_hbm, medium_hbm, kmap_hbm, occupation_hbm, weight, shift_a_hbm, shift_b_hbm,
    coarse, average, correction,
    structure, medium, kmap, occupation, shift_a, shift_b,
    spread, factor, inner, square, panels, rows_tab, shift_tab,
    row, own_rows, outgoing, first, part, total, block, slots,
    load_sem, row_send, row_recv, first_send, first_recv, part_send, part_recv,
    total_send, total_recv, slot_send, slot_recv,
):
    pairs = (
        (medium_hbm, medium), (kmap_hbm, kmap), (structure_hbm, structure),
        (occupation_hbm, occupation), (shift_a_hbm, shift_a), (shift_b_hbm, shift_b),
    )
    loads = [
        pltpu.make_async_copy(source, to, load_sem.at[at]) for at, (source, to) in enumerate(pairs)
    ]
    for load in loads:
        load.start()
    barrier = greet(n_ka, n_cfg)
    rows_x = Exchange("cfg", n_cfg, own_rows, row_send, row_recv)
    first_x = Exchange("cfg", n_cfg, first, first_send, first_recv)
    part_x = Exchange("ka", n_ka, part, part_send, part_recv)
    total_x = Exchange("cfg", n_cfg, total, total_send, total_recv)
    slot_x = Exchange("ka", n_ka, slots, slot_send, slot_recv)
    ka, cfg = part_x.me, rows_x.me
    loads[0].wait()
    loads[1].wait()
    spread_medium(medium, kmap, spread)
    loads[2].wait()
    kpoint_inner(structure, spread, factor, inner, 0)
    for load in loads[3:]:
        load.wait()
    config_row(occupation, weight, row)
    pl.semaphore_wait(barrier, n_ka + n_cfg - 2)
    rows_x.start(lambda to: row)
    own_rows[cfg] = row[...]
    kpoint_inner(structure, spread, factor, inner, 1)

    def write(at, value):
        outgoing[at // 2, at % 2] = value

    kpoint_sums(inner, kmap, write)
    first_x.start(lambda to: outgoing.at[to])
    first[cfg] = outgoing[cfg]
    kpoint_squares(spread, factor, inner, square, 0)
    rows_x.wait(lambda to: row)
    line = iota((8, LANES), 0)
    group = jnp.zeros((8, LANES), F32)
    for at in range(n_cfg):
        group = group + jnp.where(line == at, own_rows[at], 0.0)
    first_x.wait(lambda to: outgoing.at[to])
    value = [first[0, 0], first[0, 1]]
    for at in range(1, n_cfg):
        value = [value[0] + first[at, 0], value[1] + first[at, 1]]
    part[ka, 0] = value[0]
    part[ka, 1] = value[1]
    part[ka, 2] = group
    part_x.start(lambda to: part.at[ka])
    kpoint_squares(spread, factor, inner, square, 1)
    tab = Tables()
    energies = range(ENERGIES)
    y = [medium_panels(medium, tab, e) for e in energies]
    wide = [shift_panels(shift_a, shift_b, tab, e) for e in energies]
    y_b = [cdot(y[e], block_diag_c(wide[e][0], tab)) for e in energies]
    y_c = [cdot(y[e], block_diag_c(wide[e][1], tab)) for e in energies]
    y_all = [
        (block_diag_c(y[e], tab), block_diag_c(y_b[e], tab), block_diag_c(y_c[e], tab))
        for e in energies
    ]
    part_x.wait(lambda to: part.at[ka])
    value = [part[0, 0], part[0, 1]]
    for at in range(1, n_ka):
        value = [value[0] + part[at, 0], value[1] + part[at, 1]]
    total[cfg, 0] = value[0]
    total[cfg, 1] = value[1]
    total_x.start(lambda to: total.at[cfg])
    configs = jnp.concatenate([part[at, 2] for at in range(n_ka)], axis=0)
    moment_tables(configs, tab, rows_tab, shift_tab)
    total_x.wait(lambda to: total.at[cfg])
    which = iota((8, WIDE), 0)
    out = jnp.zeros((8, WIDE), F32)
    kept = []
    for e in energies:
        sum_t = (gathered_panel(total, e * 8), gathered_panel(total, e * 8 + 4))
        x, x_b, x_c = coarse_panels(y[e], y_b[e], y_c[e], y_all[e], sum_t, tab, per_moment)
        lines = []
        for at, panel in enumerate((x, x_b, x_c)):
            panels[e, at, 0] = panel[0]
            panels[e, at, 1] = panel[1]
            lines.append(
                (panels[e, at, 0, pl.ds(ka, 1), :], panels[e, at, 1, pl.ds(ka, 1), :])
            )
        (top, start), (top_b, with_b), (top_c, with_c) = first_rows(
            (x, x_b, x_c), lines, tab, cfg * 2
        )
        t_parts = translated_c(top)[1]
        tb_parts = translated_c(top_b)[1]
        tc_full, tc_parts = translated_c(top_c)
        avg = rows_stage(start, with_b, with_c, t_parts, tb_parts, tc_parts, rows_tab)
        for c in range(2):
            for site in range(2):
                at = e * 4 + c * 2 + site
                out = jnp.where(which == at, avg[c][site * 8 : site * 8 + 8], out)
        kept.append((top_b, top_c, tc_full, tb_parts, tc_parts, x))
    block[...] = out
    slot_x.start(lambda to: block)
    slots[ka] = out
    for e in energies:
        x = kept[e][5]
        d = moment_stage(
            *kept[e], block_diag_c(x, tab), wide[e][0], wide[e][1], shift_tab, tab
        )
        re, im = correction_stage(d, square, e, kmap, tab)
        correction[e, 0:1, :] = re
        correction[e, 1:2, :] = im
        for c in range(2):

            def store(value, e=e, c=c):
                coarse[e, c] = value

            coarse_out(x[c], tab, store)
    slot_x.wait(lambda to: block)
    for at in range(n_ka):
        for e in energies:
            for c in range(2):
                for site in range(2):
                    line = e * 4 + c * 2 + site
                    to = site * CHANS + at
                    average[e, c, to : to + 1, :] = slots[at, line : line + 1, :]
    rows_x.drain(lambda to: row)
    first_x.drain(lambda to: outgoing.at[to])
    part_x.drain(lambda to: part.at[ka])
    total_x.drain(lambda to: total.at[cfg])
    slot_x.drain(lambda to: block)


def output_kernel(coarse, average, correction, coarse_to, average_to, correction_to):
    coarse_to[...] = coarse[...]
    average_to[...] = average[...]
    correction_to[...] = correction[...]


def shape(*dims):
    return jax.ShapeDtypeStruct(dims, F32)


VMEM_SPEC = pl.BlockSpec(memory_space=pltpu.VMEM)
SMEM_SPEC = pl.BlockSpec(memory_space=pltpu.SMEM)


def per_device(medium_t, structure, kmap, occupation, cfg_weight, shift_a, shift_b):
    n_ka, n_cfg = lax.axis_size("ka"), lax.axis_size("cfg")
    per_moment = kmap.shape[0] * n_ka * n_cfg // MOMS
    kmap = kmap.reshape(1, LANES)
    kdims = (ENERGIES, 2, CHANS, CHANS, LANES)
    dma = pltpu.SemaphoreType.DMA

    def vmem(*dims):
        return pltpu.VMEM(dims, F32)

    any_spec = pl.BlockSpec(memory_space=pl.ANY)
    shapes = (
        shape(ENERGIES, 2, CHANS, CHANS, MOMS),
        shape(ENERGIES, 2, 2 * CHANS, WIDE),
        shape(ENERGIES, 2, LANES),
    )
    results = pl.pallas_call(
        functools.partial(kernel, per_moment, n_ka, n_cfg),
        out_shape=shapes,
        in_specs=[any_spec] * 4 + [SMEM_SPEC] + [any_spec] * 2,
        out_specs=(VMEM_SPEC,) * 3,
        scratch_shapes=[
            vmem(*kdims), vmem(ENERGIES, 2, CHANS, CHANS, MOMS),
            pltpu.VMEM((1, LANES), jnp.int32), pltpu.VMEM((1, SITES), jnp.int32),
            vmem(ENERGIES, 2, CHANS, CHANS), vmem(ENERGIES, 2, CHANS, CHANS),
            vmem(*kdims), vmem(*kdims), vmem(*kdims), vmem(*kdims),
            vmem(ENERGIES, 3, 2, CHANS, WIDE),
            vmem(SITES + 1, ALPHA, WIDE + LANES),
            vmem(2, WIDE, WIDE),
            vmem(8, LANES), vmem(n_cfg, 8, LANES),
            vmem(n_cfg, 2, 8, LANES), vmem(n_cfg, 2, 8, LANES),
            vmem(n_ka, 3, 8, LANES), vmem(n_cfg, 2, 8, LANES),
            vmem(8, WIDE), vmem(n_ka, 8, WIDE),
            dma((6,)),
            dma((n_cfg,)), dma((n_cfg,)),
            dma((n_cfg,)), dma((n_cfg,)),
            dma((n_ka,)), dma((n_ka,)),
            dma((n_cfg,)), dma((n_cfg,)),
            dma((n_ka,)), dma((n_ka,)),
        ],
        compiler_params=pltpu.CompilerParams(
            collective_id=0, has_side_effects=True, vmem_limit_bytes=56 * 1024 * 1024
        ),
    )(structure, medium_t, kmap, occupation, cfg_weight, shift_a, shift_b)
    return pl.pallas_call(
        output_kernel,
        out_shape=shapes,
        in_specs=[VMEM_SPEC] * 3,
        out_specs=(VMEM_SPEC,) * 3,
    )(*results)


def solution(mesh):
    placed = (
        P(),
        P(None, None, None, None, ("ka", "cfg")),
        P(("ka", "cfg")),
        P(("ka", "cfg"), None),
        P(("ka", "cfg")),
        P(),
        P(),
    )
    return jax.shard_map(
        per_device,
        mesh=mesh,
        in_specs=placed,
        out_specs=(P(), P(None, None, "cfg", None), P(None, None, ("ka", "cfg"))),
        check_vma=False,
    )
```

```python
import functools

import jax
import jax.numpy as jnp
from jax import lax
from jax.experimental import pallas as pl
from jax.experimental.pallas import tpu as pltpu
from jax.sharding import PartitionSpec as P

MESH = pl.DeviceIdType.MESH
F32 = jnp.float32
BF16 = jnp.bfloat16
NN = (((1,), (0,)), ((), ()))
NT = (((1,), (1,)), ((), ()))

ENERGIES = 2
SITES = 16
CHANS = 16
MOMS = 16
WIDE = SITES * CHANS
LANES = 128
ALPHA = 24


def split(x):
    high = x.astype(BF16)
    return high, (x - high.astype(F32)).astype(BF16)


def dot(left, right, dims=NN):
    return lax.dot_general(left, right, dims, preferred_element_type=F32)


def dot_exact(x, right, dims=NN):
    high, low = split(x)
    rows = x.shape[0]
    both = dot(jnp.concatenate([high, low], axis=0), right, dims)
    return both[:rows] + both[rows:]


def dot3(x, right, dims=NN):
    high, low = split(x)
    rows = x.shape[0]
    both = dot(jnp.concatenate([high, low], axis=0), right[0], dims)
    return both[:rows] + (both[rows:] + dot(high, right[1], dims))


def cdot(x, right, dims=NN):
    rows = x[0].shape[0]
    both = jnp.concatenate([x[0], x[1]], axis=0)
    by_re = dot3(both, right[0], dims)
    by_im = dot3(both, right[1], dims)
    return by_re[:rows] - by_im[rows:], by_im[:rows] + by_re[rows:]


def csplit(x):
    return split(x[0]), split(x[1])


def iota(shape, axis):
    return lax.broadcasted_iota(jnp.int32, shape, axis)


def tile_rows(x, times):
    return jnp.concatenate([x] * times, axis=0)


def quarter_turns(mom, site):
    half = site >> 3
    x = 2 * ((site >> 2) & 1) + half
    y = 2 * ((site >> 1) & 1) + half
    z = 2 * (site & 1) + half
    return ((mom >> 2) * x + ((mom >> 1) & 1) * y + (mom & 1) * z) & 3


def cos_sin(turns):
    sign = (1 - (turns & 2)).astype(F32)
    odd = (turns & 1) == 1
    return jnp.where(odd, 0.0, sign), jnp.where(odd, sign, 0.0)


def site_sum(first, second):
    carry = (first & second) >> 3
    return (first ^ second) ^ (7 * carry)


class Tables:
    def __init__(self):
        rows, cols = iota((WIDE, WIDE), 0), iota((WIDE, WIDE), 1)
        self.row_block, self.col_block = rows >> 4, cols >> 4
        self.row_in, self.col_in = rows & 15, cols & 15
        self.same_block = self.row_block == self.col_block
        self.same_in = self.row_in == self.col_in
        self.cos, self.sin = cos_sin(quarter_turns(self.col_block, self.row_block))
        self.wave_cos = jnp.where(self.same_in, self.cos, 0.0).astype(BF16)
        self.wave_sin = jnp.where(self.same_in, self.sin, 0.0).astype(BF16)
        small_r, small_c = iota((SITES, WIDE), 0), iota((SITES, WIDE), 1)
        self.pick_in = (small_r == (small_c & 15)).astype(F32).astype(BF16)
        self.pick_block = (small_r == (small_c >> 4)).astype(F32).astype(BF16)


def block_diag(panel, tab):
    def spread(part):
        return jnp.where(tab.same_block, tile_rows(part.astype(F32), SITES), 0.0).astype(BF16)

    high, low = split(panel)
    return spread(high), spread(low)


def block_diag_c(panel, tab):
    return block_diag(panel[0], tab), block_diag(panel[1], tab)


HELD_ROWS = 8


def kpoint_mul(store, left, right):
    def body(step, carry):
        start = step * HELD_ROWS
        zero = jnp.zeros((CHANS, LANES), F32)
        p, q, t = [zero] * HELD_ROWS, [zero] * HELD_ROWS, [zero] * HELD_ROWS
        for b in range(CHANS):
            rr, ri = right[0, b], right[1, b]
            less, more = ri - rr, rr + ri
            for j in range(HELD_ROWS):
                lr = left[0, start + j, pl.ds(b, 1), :]
                li = left[1, start + j, pl.ds(b, 1), :]
                p[j] = p[j] + (lr + li) * rr
                q[j] = q[j] + lr * less
                t[j] = t[j] + li * more
        for j in range(HELD_ROWS):
            store(start + j, p[j] - t[j], p[j] + q[j])
        return carry

    lax.fori_loop(0, CHANS // HELD_ROWS, body, 0)


def spread_medium(medium, kmap, spread):
    onehot = (iota((MOMS, LANES), 0) == kmap[...]).astype(F32).astype(BF16)
    for e in range(ENERGIES):
        for c in range(2):
            flat = medium[e, c].reshape(WIDE, MOMS)
            spread[e, c] = dot_exact(flat, onehot).reshape(CHANS, CHANS, LANES)


def kpoint_inner(structure, spread, factor, inner, e):
    y, g, f, h = spread.at[e], structure.at[e], factor.at[e], inner.at[e]

    def put_f(a, re, im):
        f[0, a] = re
        f[1, a] = im

    def put_h(a, re, im):
        h[0, a] = g[0, a] + re
        h[1, a] = g[1, a] + im

    kpoint_mul(put_f, y, g)
    kpoint_mul(put_h, g, f)


def momentum_matrix(kmap):
    onehot = jnp.transpose(((iota((WIDE, LANES), 0) >> 4) == kmap[...]).astype(F32)).astype(BF16)
    return jnp.concatenate([onehot, onehot], axis=0)


def kpoint_sums(inner, onehot, e, write_tile):
    keep = (iota((WIDE, WIDE), 0) >> 4) == (iota((WIDE, WIDE), 1) & 15)
    for c in range(2):
        flat = inner[e, c].reshape(WIDE, LANES)
        parts = jnp.concatenate(split(flat), axis=1)
        by_mom = jnp.where(keep, dot(parts, onehot), 0.0)
        panel = jnp.sum(by_mom.reshape(CHANS, CHANS, WIDE), axis=0)
        for half in range(2):
            for side in range(2):
                write_tile(
                    c * 4 + half * 2 + side,
                    panel[half * 8 : half * 8 + 8, side * LANES : side * LANES + LANES],
                )


def kpoint_squares(spread, factor, tau, square, e):
    y, f, t, s = spread.at[e], factor.at[e], tau.at[e], square.at[e]

    def put_q(a, re, im):
        s[0, a] = f[0, a] + re
        s[1, a] = f[1, a] + im

    def put_t(a, re, im):
        t[0, a] = y[0, a] + re
        t[1, a] = y[1, a] + im

    def put_s(a, re, im):
        s[0, a] = re
        s[1, a] = im

    kpoint_mul(put_q, f, f)
    kpoint_mul(put_t, s, y)
    kpoint_mul(put_s, t, t)


def config_row(occupation, weight, row):
    lane = iota((8, LANES), 1)
    row[...] = jnp.where(lane == SITES, 1.0, 0.0) + jnp.where(
        lane == SITES + 1, weight[0], 0.0
    )
    row[:, 0:SITES] = jnp.broadcast_to(occupation[...].astype(F32), (8, SITES))


def moment_tables(configs, tab, rows_tab, shift_tab):
    turned = jnp.transpose(configs)
    count = turned[0:ALPHA]
    weight = turned[SITES + 1 : SITES + 2]
    weight = weight / jnp.sum(weight, axis=1, keepdims=True)
    live = iota((ALPHA, LANES), 0) <= SITES
    count = jnp.where(live, count, 0.0)
    weighted = count * weight
    flat = configs.astype(BF16)
    lane_r, lane_c = iota((LANES, WIDE), 0), iota((LANES, WIDE), 1)
    pick = (lane_r == (lane_c >> 4)).astype(F32).astype(BF16)
    wide = dot(flat, pick).astype(BF16)
    ones = jnp.ones((LANES, LANES), BF16)
    for s in range(SITES + 1):
        product = weighted * count[s : s + 1]
        rows_tab[s, :, 0:WIDE] = dot_exact(product, wide)
        rows_tab[s, :, WIDE : WIDE + LANES] = dot_exact(product, ones)
    r, c = iota((WIDE, LANES), 0), iota((WIDE, LANES), 1)
    move = (site_sum(r >> 4, r & 15) == c).astype(F32).astype(BF16)
    moved = dot(move, flat, NT)
    moved_b = moved.astype(BF16)
    own = dot(((r >> 4) == c).astype(F32).astype(BF16), flat, NT)
    base = moved * (weight * (1.0 / SITES))
    fold = (tab.row_in == tab.col_block).astype(F32).astype(BF16)
    for which, left in ((0, base), (1, base * own)):
        full = dot_exact(left, moved_b, NT)
        kept = jnp.where(tab.same_block, full, 0.0)
        small = jnp.sum(kept.reshape(SITES, SITES, WIDE), axis=0)
        lanes = dot_exact(small, fold)
        shift_tab[which] = jnp.broadcast_to(
            lanes[:, None, :], (SITES, CHANS, WIDE)
        ).reshape(WIDE, WIDE)


def medium_panels(medium, tab, e):
    out = []
    for c in range(2):
        flat = medium[e, c].reshape(WIDE, MOMS)
        pick = ((iota((MOMS, WIDE), 1) >> 4) == iota((MOMS, WIDE), 0)).astype(F32).astype(BF16)
        by_mom = jnp.where(tab.same_in, dot_exact(flat, pick), 0.0)
        out.append(jnp.sum(by_mom.reshape(CHANS, CHANS, WIDE), axis=1))
    return tuple(out)


def shift_panels(shift_a, shift_b, tab, e):
    def wide(x):
        return dot_exact(x, tab.pick_in)

    b = (wide(shift_b[e, 0]), wide(shift_b[e, 1]))
    c = (
        wide(shift_a[e, 0] - shift_b[e, 0]),
        wide(shift_a[e, 1] - shift_b[e, 1]),
    )
    return b, c


def coarse_panels(y, y_b, y_c, y_all, sum_t, tab, per_moment):
    left = cdot(y, block_diag_c(sum_t, tab), NT)
    scale = 1.0 / per_moment
    left = (left[0] * scale, left[1] * scale)
    out = []
    for base, parts in zip((y, y_b, y_c), y_all):
        step = cdot(left, parts)
        out.append((base[0] + step[0], base[1] + step[1]))
    return out


def first_rows(panels, lines, tab, site0):
    mom = iota((16, WIDE), 1) >> 4
    second = (iota((16, WIDE), 0) >> 3).astype(jnp.int32)
    cos, sin = cos_sin(quarter_turns(mom, site0 + second))
    left_r, left_i = [], []
    for panel, line in zip(panels, lines):
        lr, li = jnp.broadcast_to(line[0], (16, WIDE)), jnp.broadcast_to(line[1], (16, WIDE))
        left_r += [panel[0], lr * cos - li * sin]
        left_i += [panel[1], lr * sin + li * cos]
    rows = 32 * len(panels)
    both = jnp.concatenate(left_r + left_i, axis=0) * (1.0 / SITES)
    by_cos = dot_exact(both, tab.wave_cos, NT)
    by_sin = dot_exact(both, tab.wave_sin, NT)
    real = by_cos[:rows] + by_sin[rows:]
    imag = by_cos[rows:] - by_sin[:rows]
    out = []
    for at in range(0, rows, 32):
        out.append(
            (
                (real[at : at + 16], imag[at : at + 16]),
                (real[at + 16 : at + 32], imag[at + 16 : at + 32]),
            )
        )
    return out


def swap_blocks(x, bit):
    step = 16 * bit
    up = pltpu.roll(x, LANES - step, axis=1)
    if bit == 4:
        return up
    down = pltpu.roll(x, step, axis=1)
    high = ((iota(x.shape, 1) >> 4) & bit) != 0
    return jnp.where(high, down, up)


def all_swaps(x):
    out = {0: x}
    out[4] = swap_blocks(x, 4)
    for at in (0, 4):
        out[at | 2] = swap_blocks(out[at], 2)
    for at in (0, 2, 4, 6):
        out[at | 1] = swap_blocks(out[at], 1)
    return out


def translated(panel):
    low = all_swaps(panel[:, 0:LANES])
    top = all_swaps(panel[:, LANES:WIDE])

    def whole(a, b):
        rows = [jnp.concatenate([a[q], b[q]], axis=1) for q in range(8)]
        rows += [jnp.concatenate([b[q ^ 7], a[q]], axis=1) for q in range(8)]
        return jnp.concatenate(rows, axis=0)

    low_parts = {q: split(v) for q, v in low.items()}
    top_parts = {q: split(v) for q, v in top.items()}
    parts = tuple(
        whole({q: v[p] for q, v in low_parts.items()}, {q: v[p] for q, v in top_parts.items()})
        for p in range(2)
    )
    return whole(low, top), parts


def translated_c(panel):
    real, imag = translated(panel[0]), translated(panel[1])
    return (real[0], imag[0]), (real[1], imag[1])


def rows_stage(start, with_b, with_c, t_parts, tb_parts, tc_parts, rows_tab):
    row = iota((ALPHA, WIDE), 0)
    block = iota((ALPHA, WIDE), 1) >> 4

    def opened(c):
        out = []
        for at in (0, 8):
            ub = jnp.broadcast_to(with_b[c][at : at + 1], (ALPHA, WIDE))
            uc = jnp.broadcast_to(with_c[c][at : at + 1], (ALPHA, WIDE))
            out.append(jnp.where(row == block, uc, jnp.where(row == SITES, ub, 0.0)))
        return jnp.concatenate(out, axis=0)

    begin = (opened(0), opened(1))
    hop_b = cdot(begin, tb_parts)
    hop_c = cdot(begin, tc_parts)
    inner = []
    for c in range(2):
        out = []
        for site in range(2):
            g = jnp.zeros((ALPHA, WIDE), F32)
            for s in range(SITES + 1):
                at = site * ALPHA + s
                pair = rows_tab[s, :, WIDE : WIDE + LANES]
                g = g + jnp.concatenate([pair, pair], axis=1) * hop_b[c][at : at + 1]
                g = g + rows_tab[s, :, 0:WIDE] * hop_c[c][at : at + 1]
            out.append(g)
        inner.append(jnp.concatenate(out, axis=0))
    mean = rows_tab[SITES, SITES : SITES + 1, 0:WIDE]

    def eight(parts):
        return jnp.concatenate([jnp.broadcast_to(p, (8, WIDE)) for p in parts], axis=0)

    ends = tuple(
        eight([inner[c][site * ALPHA + SITES : site * ALPHA + SITES + 1] for site in range(2)])
        for c in range(2)
    )
    by_b = cdot(ends, tb_parts)
    by_c = cdot(tuple(inner), tc_parts)
    z = []
    for c in range(2):
        picked = []
        for site in range(2):
            lines = by_c[c][site * ALPHA : site * ALPHA + ALPHA]
            picked.append(jnp.sum(jnp.where(row == block, lines, 0.0), axis=0, keepdims=True))
        z.append(with_b[c] + with_c[c] * mean - ends[c] + by_b[c] + eight(picked))
    last = cdot(tuple(z), t_parts)
    return start[0] - last[0], start[1] - last[1]


def moment_stage(top_b, top_c, tc_full, tb_parts, tc_parts, x, x_parts, b_wide, c_wide, shift_tab, tab):
    def head(wide):
        return wide[0][:, 0:CHANS], wide[1][:, 0:CHANS]

    b_in, c_in = head(b_wide), head(c_wide)
    small = (
        jnp.concatenate([b_in[0], c_in[0]], axis=0),
        jnp.concatenate([b_in[1], c_in[1]], axis=0),
    )
    lead_b = cdot(small, csplit(top_b))
    lead_c = cdot(small, csplit(top_c))
    bb, cb = [v[0:CHANS] for v in lead_b], [v[CHANS:] for v in lead_b]
    bc, cc = [v[0:CHANS] for v in lead_c], [v[CHANS:] for v in lead_c]
    two = shift_tab[1, 0:1, :]
    mean = shift_tab[1, 0:1, 0:1]
    zero = [bb[c] + mean * (bc[c] + cb[c]) + two * cc[c] for c in range(2)]
    by_b = cdot(tuple(zero), tb_parts)
    by_c = cdot(tuple(jnp.concatenate([bb[c], cb[c]], axis=0) for c in range(2)), tc_parts)

    def scaled(which):
        return split(tc_full[0] * shift_tab[which]), split(tc_full[1] * shift_tab[which])

    pair = cdot(tuple(bc), scaled(0))
    triple = cdot(tuple(cc), scaled(1))
    line = []
    for c in range(2):
        third = by_b[c] + mean * by_c[c][0:CHANS] + two * by_c[c][CHANS:] + pair[c] + triple[c]
        line.append(third - (bb[c] + mean * (cb[c] + bc[c]) + two * cc[c]))
    m_cos = dot_exact(jnp.concatenate(line, axis=0), tab.wave_cos)
    m_sin = dot_exact(jnp.concatenate(line, axis=0), tab.wave_sin)
    m_r = m_cos[:CHANS] - m_sin[CHANS:] + b_wide[0] + mean * c_wide[0]
    m_i = m_sin[:CHANS] + m_cos[CHANS:] + b_wide[1] + mean * c_wide[1]
    d = cdot(cdot(x, block_diag_c((m_r, m_i), tab)), x_parts)
    return -d[0], -d[1]


def correction_stage(d, square, e, kmap, tab):
    onehot = ((iota((WIDE, LANES), 0) >> 4) == kmap[...]).astype(F32).astype(BF16)
    keep = tab.row_block == tab.col_in

    def spread(panel):
        high, low = split(panel)

        def one(part):
            full = jnp.where(keep, tile_rows(part.astype(F32), CHANS), 0.0)
            return dot(full.astype(BF16), onehot)

        return one(high) + one(low)

    dr, di = spread(d[0]), spread(d[1])
    sr, si = square[e, 0].reshape(WIDE, LANES), square[e, 1].reshape(WIDE, LANES)
    re = jnp.sum(dr * sr - di * si, axis=0, keepdims=True)
    im = jnp.sum(dr * si + di * sr, axis=0, keepdims=True)
    return re, im


def coarse_out(x, tab, store):
    fold = (tab.col_block == tab.row_in)
    pick = (iota((WIDE, MOMS), 0) >> 4 == iota((WIDE, MOMS), 1)).astype(F32).astype(BF16)
    high = x.astype(BF16)
    rest = x - high.astype(F32)
    mid = rest.astype(BF16)
    low = (rest - mid.astype(F32)).astype(BF16)
    total = None
    for part in (low, mid, high):
        wide = jnp.broadcast_to(part.astype(F32)[:, None, :], (CHANS, CHANS, WIDE))
        wide = jnp.where(tab.same_in, wide.reshape(WIDE, WIDE), 0.0).astype(BF16)
        piece = dot(wide, pick)
        total = piece if total is None else total + piece
    store(total.reshape(CHANS, CHANS, MOMS))


def gathered_panel(tiles, at):
    top = jnp.concatenate([tiles[at], tiles[at + 1]], axis=1)
    low = jnp.concatenate([tiles[at + 2], tiles[at + 3]], axis=1)
    return jnp.concatenate([top, low], axis=0)


class Exchange:
    def __init__(self, axis, count, slots, send, recv):
        self.axis, self.count = axis, count
        self.slots, self.send, self.recv = slots, send, recv
        self.me = lax.axis_index(axis)

    def peer(self, d):
        return lax.rem(self.me + d, self.count)

    def copy(self, src, at, d):
        return pltpu.make_async_remote_copy(
            src_ref=src, dst_ref=self.slots.at[at], send_sem=self.send.at[d],
            recv_sem=self.recv.at[at], device_id={self.axis: self.peer(d)}, device_id_type=MESH,
        )

    def start(self, source):
        for d in range(1, self.count):
            self.copy(source(self.peer(d)), self.me, d).start()

    def wait(self, source):
        for d in range(1, self.count):
            self.copy(source(self.me), self.peer(d), d).wait_recv()

    def drain(self, source):
        for d in range(1, self.count):
            self.copy(source(self.me), self.me, d).wait_send()


def greet(n_ka, n_cfg):
    barrier = pltpu.get_barrier_semaphore()
    for axis, count in (("ka", n_ka), ("cfg", n_cfg)):
        me = lax.axis_index(axis)
        for d in range(1, count):
            pl.semaphore_signal(
                barrier, inc=1, device_id={axis: lax.rem(me + d, count)}, device_id_type=MESH
            )
    return barrier


def kernel(
    per_moment, n_ka, n_cfg,
    structure_hbm, medium_hbm, kmap_hbm, occupation_hbm, weight, shift_a_hbm, shift_b_hbm,
    coarse, average, correction,
    structure, medium, kmap, occupation, shift_a, shift_b,
    spread, factor, inner, square, panels, rows_tab, shift_tab,
    row, own_rows, outgoing, first, part_a, part_b, total, block, slots,
    load_sem, row_send, row_recv, first_send, first_recv, part_send, part_recv,
    total_send, total_recv, slot_send, slot_recv,
):
    pairs = (
        (kmap_hbm, kmap), (medium_hbm, medium), (structure_hbm, structure),
        (occupation_hbm, occupation), (shift_a_hbm, shift_a), (shift_b_hbm, shift_b),
    )
    loads = [
        pltpu.make_async_copy(source, to, load_sem.at[at]) for at, (source, to) in enumerate(pairs)
    ]
    for load in loads:
        load.start()
    barrier = greet(n_ka, n_cfg)
    energies = range(ENERGIES)
    parts = (part_a, part_b)
    rows_x = Exchange("cfg", n_cfg, own_rows, row_send, row_recv)
    first_x = [
        Exchange("cfg", n_cfg, first.at[e], first_send.at[e], first_recv.at[e]) for e in energies
    ]
    part_x = [Exchange("ka", n_ka, parts[e], part_send.at[e], part_recv.at[e]) for e in energies]
    total_x = [
        Exchange("cfg", n_cfg, total.at[e], total_send.at[e], total_recv.at[e]) for e in energies
    ]
    slot_x = [Exchange("ka", n_ka, slots.at[e], slot_send.at[e], slot_recv.at[e]) for e in energies]
    ka, cfg = lax.axis_index("ka"), lax.axis_index("cfg")

    def own_row(to):
        return row

    def own_sums(e):
        return lambda to: outgoing.at[e, to]

    def own_part(e):
        return lambda to: parts[e].at[ka]

    def own_total(e):
        return lambda to: total.at[e, cfg]

    def own_block(e):
        return lambda to: block.at[e]

    def send_sums(e):
        def write(at, value):
            outgoing[e, at] = value

        kpoint_sums(inner, onehot, e, write)
        first_x[e].start(own_sums(e))
        first[e, cfg] = outgoing[e, cfg]

    def send_part(e):
        first_x[e].wait(own_sums(e))
        value = first[e, 0]
        for at in range(1, n_cfg):
            value = value + first[e, at]
        parts[e][ka, 0] = value
        part_x[e].start(own_part(e))

    def send_total(e):
        part_x[e].wait(own_part(e))
        value = parts[e][0, 0]
        for at in range(1, n_ka):
            value = value + parts[e][at, 0]
        total[e, cfg] = value
        total_x[e].start(own_total(e))

    loads[0].wait()
    onehot = momentum_matrix(kmap)
    loads[1].wait()
    spread_medium(medium, kmap, spread)
    loads[2].wait()
    kpoint_inner(structure, spread, factor, inner, 0)
    for load in loads[3:]:
        load.wait()
    config_row(occupation, weight, row)
    pl.semaphore_wait(barrier, n_ka + n_cfg - 2)
    rows_x.start(own_row)
    own_rows[cfg] = row[...]
    send_sums(0)
    kpoint_inner(structure, spread, factor, inner, 1)
    send_sums(1)
    kpoint_squares(spread, factor, inner, square, 0)
    rows_x.wait(own_row)
    line = iota((8, LANES), 0)
    group = jnp.zeros((8, LANES), F32)
    for at in range(n_cfg):
        group = group + jnp.where(line == at, own_rows[at], 0.0)
    part_a[ka, 1] = group
    send_part(0)
    tab = Tables()
    y = [medium_panels(medium, tab, e) for e in energies]
    wide = [shift_panels(shift_a, shift_b, tab, e) for e in energies]
    y_b = [cdot(y[e], block_diag_c(wide[e][0], tab)) for e in energies]
    y_c = [cdot(y[e], block_diag_c(wide[e][1], tab)) for e in energies]
    y_all = [
        (block_diag_c(y[e], tab), block_diag_c(y_b[e], tab), block_diag_c(y_c[e], tab))
        for e in energies
    ]
    send_part(1)
    kpoint_squares(spread, factor, inner, square, 1)
    send_total(0)
    configs = jnp.concatenate([part_a[at, 1] for at in range(n_ka)], axis=0)
    moment_tables(configs, tab, rows_tab, shift_tab)
    send_total(1)
    kept = []
    for e in energies:
        total_x[e].wait(own_total(e))
        sum_t = (gathered_panel(total.at[e], 0), gathered_panel(total.at[e], 4))
        x, x_b, x_c = coarse_panels(y[e], y_b[e], y_c[e], y_all[e], sum_t, tab, per_moment)
        lines = []
        for at, panel in enumerate((x, x_b, x_c)):
            panels[e, at, 0] = panel[0]
            panels[e, at, 1] = panel[1]
            lines.append(
                (panels[e, at, 0, pl.ds(ka, 1), :], panels[e, at, 1, pl.ds(ka, 1), :])
            )
        (top, start), (top_b, with_b), (top_c, with_c) = first_rows(
            (x, x_b, x_c), lines, tab, cfg * 2
        )
        t_parts = translated_c(top)[1]
        tb_parts = translated_c(top_b)[1]
        tc_full, tc_parts = translated_c(top_c)
        avg = rows_stage(start, with_b, with_c, t_parts, tb_parts, tc_parts, rows_tab)
        out = jnp.zeros((8, LANES), F32)
        for c in range(2):
            for site in range(2):
                for side in range(2):
                    at = c * 4 + site * 2 + side
                    lanes = avg[c][site * 8 : site * 8 + 8, side * LANES : side * LANES + LANES]
                    out = jnp.where(line == at, lanes, out)
        block[e] = out
        slot_x[e].start(own_block(e))
        slots[e, ka] = out
        kept.append((top_b, top_c, tc_full, tb_parts, tc_parts, x))
    for e in energies:
        x = kept[e][5]
        d = moment_stage(
            *kept[e], block_diag_c(x, tab), wide[e][0], wide[e][1], shift_tab, tab
        )
        re, im = correction_stage(d, square, e, kmap, tab)
        correction[e, 0:1, :] = re
        correction[e, 1:2, :] = im
        for c in range(2):

            def store(value, e=e, c=c):
                coarse[e, c] = value

            coarse_out(x[c], tab, store)
    for e in energies:
        slot_x[e].wait(own_block(e))
        for at in range(n_ka):
            for c in range(2):
                for site in range(2):
                    for side in range(2):
                        of = c * 4 + site * 2 + side
                        to = site * CHANS + at
                        average[e, c, to : to + 1, side * LANES : side * LANES + LANES] = slots[
                            e, at, of : of + 1, :
                        ]
    rows_x.drain(own_row)
    for e in energies:
        first_x[e].drain(own_sums(e))
        part_x[e].drain(own_part(e))
        total_x[e].drain(own_total(e))
        slot_x[e].drain(own_block(e))


def output_kernel(coarse, average, correction, coarse_to, average_to, correction_to):
    coarse_to[...] = coarse[...]
    average_to[...] = average[...]
    correction_to[...] = correction[...]


def shape(*dims):
    return jax.ShapeDtypeStruct(dims, F32)


VMEM_SPEC = pl.BlockSpec(memory_space=pltpu.VMEM)
SMEM_SPEC = pl.BlockSpec(memory_space=pltpu.SMEM)


def per_device(medium_t, structure, kmap, occupation, cfg_weight, shift_a, shift_b):
    n_ka, n_cfg = lax.axis_size("ka"), lax.axis_size("cfg")
    per_moment = kmap.shape[0] * n_ka * n_cfg // MOMS
    kmap = kmap.reshape(1, LANES)
    kdims = (ENERGIES, 2, CHANS, CHANS, LANES)
    dma = pltpu.SemaphoreType.DMA

    def vmem(*dims):
        return pltpu.VMEM(dims, F32)

    any_spec = pl.BlockSpec(memory_space=pl.ANY)
    shapes = (
        shape(ENERGIES, 2, CHANS, CHANS, MOMS),
        shape(ENERGIES, 2, 2 * CHANS, WIDE),
        shape(ENERGIES, 2, LANES),
    )
    results = pl.pallas_call(
        functools.partial(kernel, per_moment, n_ka, n_cfg),
        out_shape=shapes,
        in_specs=[any_spec] * 4 + [SMEM_SPEC] + [any_spec] * 2,
        out_specs=(VMEM_SPEC,) * 3,
        scratch_shapes=[
            vmem(*kdims), vmem(ENERGIES, 2, CHANS, CHANS, MOMS),
            pltpu.VMEM((1, LANES), jnp.int32), pltpu.VMEM((1, SITES), jnp.int32),
            vmem(ENERGIES, 2, CHANS, CHANS), vmem(ENERGIES, 2, CHANS, CHANS),
            vmem(*kdims), vmem(*kdims), vmem(*kdims), vmem(*kdims),
            vmem(ENERGIES, 3, 2, CHANS, WIDE),
            vmem(SITES + 1, ALPHA, WIDE + LANES),
            vmem(2, WIDE, WIDE),
            vmem(8, LANES), vmem(n_cfg, 8, LANES),
            vmem(ENERGIES, n_cfg, 8, LANES), vmem(ENERGIES, n_cfg, 8, LANES),
            vmem(n_ka, 2, 8, LANES), vmem(n_ka, 1, 8, LANES),
            vmem(ENERGIES, n_cfg, 8, LANES),
            vmem(ENERGIES, 8, LANES), vmem(ENERGIES, n_ka, 8, LANES),
            dma((6,)),
            dma((n_cfg,)), dma((n_cfg,)),
            dma((ENERGIES, n_cfg)), dma((ENERGIES, n_cfg)),
            dma((ENERGIES, n_ka)), dma((ENERGIES, n_ka)),
            dma((ENERGIES, n_cfg)), dma((ENERGIES, n_cfg)),
            dma((ENERGIES, n_ka)), dma((ENERGIES, n_ka)),
        ],
        compiler_params=pltpu.CompilerParams(
            collective_id=0, has_side_effects=True, vmem_limit_bytes=56 * 1024 * 1024
        ),
    )(structure, medium_t, kmap, occupation, cfg_weight, shift_a, shift_b)
    return pl.pallas_call(
        output_kernel,
        out_shape=shapes,
        in_specs=[VMEM_SPEC] * 3,
        out_specs=(VMEM_SPEC,) * 3,
    )(*results)


def solution(mesh):
    placed = (
        P(),
        P(None, None, None, None, ("ka", "cfg")),
        P(("ka", "cfg")),
        P(("ka", "cfg"), None),
        P(("ka", "cfg")),
        P(),
        P(),
    )
    return jax.shard_map(
        per_device,
        mesh=mesh,
        in_specs=placed,
        out_specs=(P(), P(None, None, "cfg", None), P(None, None, ("ka", "cfg"))),
        check_vma=False,
    )
```

```python
import functools

import jax
import jax.numpy as jnp
from jax import lax
from jax.experimental import pallas as pl
from jax.experimental.pallas import tpu as pltpu
from jax.sharding import PartitionSpec as P

MESH = pl.DeviceIdType.MESH
F32 = jnp.float32
BF16 = jnp.bfloat16
NN = (((1,), (0,)), ((), ()))
NT = (((1,), (1,)), ((), ()))

ENERGIES = 2
SITES = 16
CHANS = 16
MOMS = 16
WIDE = SITES * CHANS
LANES = 128
ALPHA = 24


def split(x):
    high = x.astype(BF16)
    return high, (x - high.astype(F32)).astype(BF16)


def dot(left, right, dims=NN):
    return lax.dot_general(left, right, dims, preferred_element_type=F32)


def dot_exact(x, right, dims=NN):
    high, low = split(x)
    rows = x.shape[0]
    both = dot(jnp.concatenate([high, low], axis=0), right, dims)
    return both[:rows] + both[rows:]


def dot3(x, right, dims=NN):
    high, low = split(x)
    rows = x.shape[0]
    both = dot(jnp.concatenate([high, low], axis=0), right[0], dims)
    return both[:rows] + (both[rows:] + dot(high, right[1], dims))


def cdot(x, right, dims=NN):
    rows = x[0].shape[0]
    both = jnp.concatenate([x[0], x[1]], axis=0)
    by_re = dot3(both, right[0], dims)
    by_im = dot3(both, right[1], dims)
    return by_re[:rows] - by_im[rows:], by_im[:rows] + by_re[rows:]


def csplit(x):
    return split(x[0]), split(x[1])


def iota(shape, axis):
    return lax.broadcasted_iota(jnp.int32, shape, axis)


def tile_rows(x, times):
    return jnp.concatenate([x] * times, axis=0)


def quarter_turns(mom, site):
    half = site >> 3
    x = 2 * ((site >> 2) & 1) + half
    y = 2 * ((site >> 1) & 1) + half
    z = 2 * (site & 1) + half
    return ((mom >> 2) * x + ((mom >> 1) & 1) * y + (mom & 1) * z) & 3


def cos_sin(turns):
    sign = (1 - (turns & 2)).astype(F32)
    odd = (turns & 1) == 1
    return jnp.where(odd, 0.0, sign), jnp.where(odd, sign, 0.0)


def site_sum(first, second):
    carry = (first & second) >> 3
    return (first ^ second) ^ (7 * carry)


class Tables:
    def __init__(self):
        rows, cols = iota((WIDE, WIDE), 0), iota((WIDE, WIDE), 1)
        self.row_block, self.col_block = rows >> 4, cols >> 4
        self.row_in, self.col_in = rows & 15, cols & 15
        self.same_block = self.row_block == self.col_block
        self.same_in = self.row_in == self.col_in
        self.cos, self.sin = cos_sin(quarter_turns(self.col_block, self.row_block))
        self.wave_cos = jnp.where(self.same_in, self.cos, 0.0).astype(BF16)
        self.wave_sin = jnp.where(self.same_in, self.sin, 0.0).astype(BF16)
        small_r, small_c = iota((SITES, WIDE), 0), iota((SITES, WIDE), 1)
        self.pick_in = (small_r == (small_c & 15)).astype(F32).astype(BF16)
        self.pick_block = (small_r == (small_c >> 4)).astype(F32).astype(BF16)


def block_diag(panel, tab):
    def spread(part):
        return jnp.where(tab.same_block, tile_rows(part.astype(F32), SITES), 0.0).astype(BF16)

    high, low = split(panel)
    return spread(high), spread(low)


def block_diag_c(panel, tab):
    return block_diag(panel[0], tab), block_diag(panel[1], tab)


HELD_ROWS = 8


def kpoint_mul(store, left, right):
    def body(step, carry):
        start = step * HELD_ROWS
        zero = jnp.zeros((CHANS, LANES), F32)
        p, q, t = [zero] * HELD_ROWS, [zero] * HELD_ROWS, [zero] * HELD_ROWS
        for b in range(CHANS):
            rr, ri = right[0, b], right[1, b]
            less, more = ri - rr, rr + ri
            for j in range(HELD_ROWS):
                lr = left[0, start + j, pl.ds(b, 1), :]
                li = left[1, start + j, pl.ds(b, 1), :]
                p[j] = p[j] + (lr + li) * rr
                q[j] = q[j] + lr * less
                t[j] = t[j] + li * more
        for j in range(HELD_ROWS):
            store(start + j, p[j] - t[j], p[j] + q[j])
        return carry

    lax.fori_loop(0, CHANS // HELD_ROWS, body, 0)


def spread_medium(medium, kmap, spread):
    onehot = (iota((MOMS, LANES), 0) == kmap[...]).astype(F32).astype(BF16)
    for e in range(ENERGIES):
        for c in range(2):
            flat = medium[e, c].reshape(WIDE, MOMS)
            spread[e, c] = dot_exact(flat, onehot).reshape(CHANS, CHANS, LANES)


def kpoint_factor(structure, spread, factor, e):
    f = factor.at[e]

    def put(a, re, im):
        f[0, a] = re
        f[1, a] = im

    kpoint_mul(put, spread.at[e], structure.at[e])


def kpoint_inner(structure, factor, inner, e):
    g, h = structure.at[e], inner.at[e]

    def put(a, re, im):
        h[0, a] = g[0, a] + re
        h[1, a] = g[1, a] + im

    kpoint_mul(put, g, factor.at[e])


def momentum_matrix(kmap):
    onehot = jnp.transpose(((iota((WIDE, LANES), 0) >> 4) == kmap[...]).astype(F32)).astype(BF16)
    return jnp.concatenate([onehot, onehot], axis=0)


def kpoint_sums(inner, onehot, e, write_tile):
    keep = (iota((WIDE, WIDE), 0) >> 4) == (iota((WIDE, WIDE), 1) & 15)
    for c in range(2):
        flat = inner[e, c].reshape(WIDE, LANES)
        parts = jnp.concatenate(split(flat), axis=1)
        by_mom = jnp.where(keep, dot(parts, onehot), 0.0)
        panel = jnp.sum(by_mom.reshape(CHANS, CHANS, WIDE), axis=0)
        for half in range(2):
            for side in range(2):
                write_tile(
                    c * 4 + half * 2 + side,
                    panel[half * 8 : half * 8 + 8, side * LANES : side * LANES + LANES],
                )


def kpoint_squares(spread, factor, tau, square, e):
    y, f, t, s = spread.at[e], factor.at[e], tau.at[e], square.at[e]

    def put_q(a, re, im):
        s[0, a] = f[0, a] + re
        s[1, a] = f[1, a] + im

    def put_t(a, re, im):
        t[0, a] = y[0, a] + re
        t[1, a] = y[1, a] + im

    def put_s(a, re, im):
        s[0, a] = re
        s[1, a] = im

    kpoint_mul(put_q, f, f)
    kpoint_mul(put_t, s, y)
    kpoint_mul(put_s, t, t)


def config_row(occupation, weight, row):
    lane = iota((8, LANES), 1)
    row[...] = jnp.where(lane == SITES, 1.0, 0.0) + jnp.where(
        lane == SITES + 1, weight[0], 0.0
    )
    row[:, 0:SITES] = jnp.broadcast_to(occupation[...].astype(F32), (8, SITES))


def moment_tables(configs, tab, rows_tab, shift_tab):
    turned = jnp.transpose(configs)
    count = turned[0:ALPHA]
    weight = turned[SITES + 1 : SITES + 2]
    weight = weight / jnp.sum(weight, axis=1, keepdims=True)
    live = iota((ALPHA, LANES), 0) <= SITES
    count = jnp.where(live, count, 0.0)
    weighted = count * weight
    flat = configs.astype(BF16)
    lane_r, lane_c = iota((LANES, WIDE), 0), iota((LANES, WIDE), 1)
    pick = (lane_r == (lane_c >> 4)).astype(F32).astype(BF16)
    wide = dot(flat, pick).astype(BF16)
    ones = jnp.ones((LANES, LANES), BF16)
    for s in range(SITES + 1):
        product = weighted * count[s : s + 1]
        rows_tab[s, :, 0:WIDE] = dot_exact(product, wide)
        rows_tab[s, :, WIDE : WIDE + LANES] = dot_exact(product, ones)
    r, c = iota((WIDE, LANES), 0), iota((WIDE, LANES), 1)
    move = (site_sum(r >> 4, r & 15) == c).astype(F32).astype(BF16)
    moved = dot(move, flat, NT)
    moved_b = moved.astype(BF16)
    own = dot(((r >> 4) == c).astype(F32).astype(BF16), flat, NT)
    base = moved * (weight * (1.0 / SITES))
    fold = (tab.row_in == tab.col_block).astype(F32).astype(BF16)
    for which, left in ((0, base), (1, base * own)):
        full = dot_exact(left, moved_b, NT)
        kept = jnp.where(tab.same_block, full, 0.0)
        small = jnp.sum(kept.reshape(SITES, SITES, WIDE), axis=0)
        lanes = dot_exact(small, fold)
        shift_tab[which] = jnp.broadcast_to(
            lanes[:, None, :], (SITES, CHANS, WIDE)
        ).reshape(WIDE, WIDE)


def medium_panels(medium, tab, e):
    out = []
    for c in range(2):
        flat = medium[e, c].reshape(WIDE, MOMS)
        pick = ((iota((MOMS, WIDE), 1) >> 4) == iota((MOMS, WIDE), 0)).astype(F32).astype(BF16)
        by_mom = jnp.where(tab.same_in, dot_exact(flat, pick), 0.0)
        out.append(jnp.sum(by_mom.reshape(CHANS, CHANS, WIDE), axis=1))
    return tuple(out)


def shift_panels(shift_a, shift_b, tab, e):
    def wide(x):
        return dot_exact(x, tab.pick_in)

    b = (wide(shift_b[e, 0]), wide(shift_b[e, 1]))
    c = (
        wide(shift_a[e, 0] - shift_b[e, 0]),
        wide(shift_a[e, 1] - shift_b[e, 1]),
    )
    return b, c


def coarse_panels(y, y_b, y_c, y_all, sum_t, tab, per_moment):
    left = cdot(y, block_diag_c(sum_t, tab), NT)
    scale = 1.0 / per_moment
    left = (left[0] * scale, left[1] * scale)
    out = []
    for base, parts in zip((y, y_b, y_c), y_all):
        step = cdot(left, parts)
        out.append((base[0] + step[0], base[1] + step[1]))
    return out


def first_rows(panels, lines, tab, site0):
    mom = iota((16, WIDE), 1) >> 4
    second = (iota((16, WIDE), 0) >> 3).astype(jnp.int32)
    cos, sin = cos_sin(quarter_turns(mom, site0 + second))
    left_r, left_i = [], []
    for panel, line in zip(panels, lines):
        lr, li = jnp.broadcast_to(line[0], (16, WIDE)), jnp.broadcast_to(line[1], (16, WIDE))
        left_r += [panel[0], lr * cos - li * sin]
        left_i += [panel[1], lr * sin + li * cos]
    rows = 32 * len(panels)
    both = jnp.concatenate(left_r + left_i, axis=0) * (1.0 / SITES)
    by_cos = dot_exact(both, tab.wave_cos, NT)
    by_sin = dot_exact(both, tab.wave_sin, NT)
    real = by_cos[:rows] + by_sin[rows:]
    imag = by_cos[rows:] - by_sin[:rows]
    out = []
    for at in range(0, rows, 32):
        out.append(
            (
                (real[at : at + 16], imag[at : at + 16]),
                (real[at + 16 : at + 32], imag[at + 16 : at + 32]),
            )
        )
    return out


def swap_blocks(x, bit):
    step = 16 * bit
    up = pltpu.roll(x, LANES - step, axis=1)
    if bit == 4:
        return up
    down = pltpu.roll(x, step, axis=1)
    high = ((iota(x.shape, 1) >> 4) & bit) != 0
    return jnp.where(high, down, up)


def all_swaps(x):
    out = {0: x}
    out[4] = swap_blocks(x, 4)
    for at in (0, 4):
        out[at | 2] = swap_blocks(out[at], 2)
    for at in (0, 2, 4, 6):
        out[at | 1] = swap_blocks(out[at], 1)
    return out


def translated(panel):
    low = all_swaps(panel[:, 0:LANES])
    top = all_swaps(panel[:, LANES:WIDE])

    def whole(a, b):
        rows = [jnp.concatenate([a[q], b[q]], axis=1) for q in range(8)]
        rows += [jnp.concatenate([b[q ^ 7], a[q]], axis=1) for q in range(8)]
        return jnp.concatenate(rows, axis=0)

    low_parts = {q: split(v) for q, v in low.items()}
    top_parts = {q: split(v) for q, v in top.items()}
    parts = tuple(
        whole({q: v[p] for q, v in low_parts.items()}, {q: v[p] for q, v in top_parts.items()})
        for p in range(2)
    )
    return whole(low, top), parts


def translated_c(panel):
    real, imag = translated(panel[0]), translated(panel[1])
    return (real[0], imag[0]), (real[1], imag[1])


def rows_stage(start, with_b, with_c, t_parts, tb_parts, tc_parts, rows_tab):
    row = iota((ALPHA, WIDE), 0)
    block = iota((ALPHA, WIDE), 1) >> 4

    def opened(c):
        out = []
        for at in (0, 8):
            ub = jnp.broadcast_to(with_b[c][at : at + 1], (ALPHA, WIDE))
            uc = jnp.broadcast_to(with_c[c][at : at + 1], (ALPHA, WIDE))
            out.append(jnp.where(row == block, uc, jnp.where(row == SITES, ub, 0.0)))
        return jnp.concatenate(out, axis=0)

    begin = (opened(0), opened(1))
    hop_b = cdot(begin, tb_parts)
    hop_c = cdot(begin, tc_parts)
    inner = []
    for c in range(2):
        out = []
        for site in range(2):
            g = jnp.zeros((ALPHA, WIDE), F32)
            for s in range(SITES + 1):
                at = site * ALPHA + s
                pair = rows_tab[s, :, WIDE : WIDE + LANES]
                g = g + jnp.concatenate([pair, pair], axis=1) * hop_b[c][at : at + 1]
                g = g + rows_tab[s, :, 0:WIDE] * hop_c[c][at : at + 1]
            out.append(g)
        inner.append(jnp.concatenate(out, axis=0))
    mean = rows_tab[SITES, SITES : SITES + 1, 0:WIDE]

    def eight(parts):
        return jnp.concatenate([jnp.broadcast_to(p, (8, WIDE)) for p in parts], axis=0)

    ends = tuple(
        eight([inner[c][site * ALPHA + SITES : site * ALPHA + SITES + 1] for site in range(2)])
        for c in range(2)
    )
    by_b = cdot(ends, tb_parts)
    by_c = cdot(tuple(inner), tc_parts)
    z = []
    for c in range(2):
        picked = []
        for site in range(2):
            lines = by_c[c][site * ALPHA : site * ALPHA + ALPHA]
            picked.append(jnp.sum(jnp.where(row == block, lines, 0.0), axis=0, keepdims=True))
        z.append(with_b[c] + with_c[c] * mean - ends[c] + by_b[c] + eight(picked))
    last = cdot(tuple(z), t_parts)
    return start[0] - last[0], start[1] - last[1]


def moment_stage(top_b, top_c, tc_full, tb_parts, tc_parts, x, x_parts, b_wide, c_wide, shift_tab, tab):
    def head(wide):
        return wide[0][:, 0:CHANS], wide[1][:, 0:CHANS]

    b_in, c_in = head(b_wide), head(c_wide)
    small = (
        jnp.concatenate([b_in[0], c_in[0]], axis=0),
        jnp.concatenate([b_in[1], c_in[1]], axis=0),
    )
    lead_b = cdot(small, csplit(top_b))
    lead_c = cdot(small, csplit(top_c))
    bb, cb = [v[0:CHANS] for v in lead_b], [v[CHANS:] for v in lead_b]
    bc, cc = [v[0:CHANS] for v in lead_c], [v[CHANS:] for v in lead_c]
    two = shift_tab[1, 0:1, :]
    mean = shift_tab[1, 0:1, 0:1]
    zero = [bb[c] + mean * (bc[c] + cb[c]) + two * cc[c] for c in range(2)]
    by_b = cdot(tuple(zero), tb_parts)
    by_c = cdot(tuple(jnp.concatenate([bb[c], cb[c]], axis=0) for c in range(2)), tc_parts)

    def scaled(which):
        return split(tc_full[0] * shift_tab[which]), split(tc_full[1] * shift_tab[which])

    pair = cdot(tuple(bc), scaled(0))
    triple = cdot(tuple(cc), scaled(1))
    line = []
    for c in range(2):
        third = by_b[c] + mean * by_c[c][0:CHANS] + two * by_c[c][CHANS:] + pair[c] + triple[c]
        line.append(third - (bb[c] + mean * (cb[c] + bc[c]) + two * cc[c]))
    m_cos = dot_exact(jnp.concatenate(line, axis=0), tab.wave_cos)
    m_sin = dot_exact(jnp.concatenate(line, axis=0), tab.wave_sin)
    m_r = m_cos[:CHANS] - m_sin[CHANS:] + b_wide[0] + mean * c_wide[0]
    m_i = m_sin[:CHANS] + m_cos[CHANS:] + b_wide[1] + mean * c_wide[1]
    d = cdot(cdot(x, block_diag_c((m_r, m_i), tab)), x_parts)
    return -d[0], -d[1]


def correction_stage(d, square, e, kmap, tab):
    onehot = ((iota((WIDE, LANES), 0) >> 4) == kmap[...]).astype(F32).astype(BF16)
    keep = tab.row_block == tab.col_in

    def spread(panel):
        high, low = split(panel)

        def one(part):
            full = jnp.where(keep, tile_rows(part.astype(F32), CHANS), 0.0)
            return dot(full.astype(BF16), onehot)

        return one(high) + one(low)

    dr, di = spread(d[0]), spread(d[1])
    sr, si = square[e, 0].reshape(WIDE, LANES), square[e, 1].reshape(WIDE, LANES)
    re = jnp.sum(dr * sr - di * si, axis=0, keepdims=True)
    im = jnp.sum(dr * si + di * sr, axis=0, keepdims=True)
    return re, im


def coarse_out(x, tab, store):
    fold = (tab.col_block == tab.row_in)
    pick = (iota((WIDE, MOMS), 0) >> 4 == iota((WIDE, MOMS), 1)).astype(F32).astype(BF16)
    high = x.astype(BF16)
    rest = x - high.astype(F32)
    mid = rest.astype(BF16)
    low = (rest - mid.astype(F32)).astype(BF16)
    total = None
    for part in (low, mid, high):
        wide = jnp.broadcast_to(part.astype(F32)[:, None, :], (CHANS, CHANS, WIDE))
        wide = jnp.where(tab.same_in, wide.reshape(WIDE, WIDE), 0.0).astype(BF16)
        piece = dot(wide, pick)
        total = piece if total is None else total + piece
    store(total.reshape(CHANS, CHANS, MOMS))


def gathered_panel(tiles, at):
    top = jnp.concatenate([tiles[at], tiles[at + 1]], axis=1)
    low = jnp.concatenate([tiles[at + 2], tiles[at + 3]], axis=1)
    return jnp.concatenate([top, low], axis=0)


def offsets(outer, inner, torus):
    def hops(step):
        first = min(step[0], outer - step[0])
        return first + (min(step[1], inner - step[1]) if torus else 0.5 * (step[1] > 0))

    steps = [(a, b) for a in range(outer) for b in range(inner) if a or b]
    return sorted(steps, key=lambda step: (-hops(step), step))


class Group:
    def __init__(self, axis, inner, torus):
        self.axis, self.inner = axis, inner
        self.count = lax.axis_size(axis)
        self.outer = self.count // inner
        self.steps = offsets(self.outer, inner, torus)
        self.me = lax.axis_index(axis)

    def peer(self, step):
        first = lax.rem(self.me // self.inner + step[0], self.outer)
        return first * self.inner + lax.rem(lax.rem(self.me, self.inner) + step[1], self.inner)

    def greet(self, barrier):
        for step in self.steps:
            pl.semaphore_signal(
                barrier, inc=1, device_id={self.axis: self.peer(step)}, device_id_type=MESH
            )


class Exchange:
    def __init__(self, group, slots, send, recv):
        self.group, self.slots, self.send, self.recv = group, slots, send, recv

    def copy(self, src, at, number, peer):
        return pltpu.make_async_remote_copy(
            src_ref=src, dst_ref=self.slots.at[at], send_sem=self.send.at[number],
            recv_sem=self.recv.at[at], device_id={self.group.axis: peer}, device_id_type=MESH,
        )

    def start(self, source):
        for number, step in enumerate(self.group.steps):
            peer = self.group.peer(step)
            self.copy(source(peer), self.group.me, number, peer).start()

    def wait(self, source):
        for number, step in enumerate(self.group.steps[::-1]):
            peer = self.group.peer(step)
            self.copy(source(self.group.me), peer, number, peer).wait_recv()

    def drain(self, source):
        for number, step in enumerate(self.group.steps):
            peer = self.group.peer(step)
            self.copy(source(self.group.me), self.group.me, number, peer).wait_send()


def kernel(
    per_moment, n_ka, n_cfg,
    structure_hbm, medium_hbm, kmap_hbm, occupation_hbm, weight, shift_a_hbm, shift_b_hbm,
    coarse, average, correction,
    structure, medium, kmap, occupation, shift_a, shift_b,
    spread, factor, inner, square, panels, rows_tab, shift_tab,
    row, own_rows, outgoing, first, part_a, part_b, total, block, slots,
    load_sem, row_send, row_recv, first_send, first_recv, part_send, part_recv,
    total_send, total_recv, slot_send, slot_recv,
):
    pairs = (
        (kmap_hbm, kmap), (medium_hbm, medium), (structure_hbm, structure),
        (occupation_hbm, occupation), (shift_a_hbm, shift_a), (shift_b_hbm, shift_b),
    )
    loads = [
        pltpu.make_async_copy(source, to, load_sem.at[at]) for at, (source, to) in enumerate(pairs)
    ]
    for load in loads[:3]:
        load.start()
    barrier = pltpu.get_barrier_semaphore()
    by_ka, by_cfg = Group("ka", 4, True), Group("cfg", 2, False)
    by_ka.greet(barrier)
    by_cfg.greet(barrier)
    for load in loads[3:]:
        load.start()
    energies = range(ENERGIES)
    parts = (part_a, part_b)
    rows_x = Exchange(by_cfg, own_rows, row_send, row_recv)
    first_x = [Exchange(by_cfg, first.at[e], first_send.at[e], first_recv.at[e]) for e in energies]
    part_x = [Exchange(by_ka, parts[e], part_send.at[e], part_recv.at[e]) for e in energies]
    total_x = [Exchange(by_cfg, total.at[e], total_send.at[e], total_recv.at[e]) for e in energies]
    slot_x = [Exchange(by_ka, slots.at[e], slot_send.at[e], slot_recv.at[e]) for e in energies]
    ka, cfg = lax.axis_index("ka"), lax.axis_index("cfg")

    def own_row(to):
        return row

    def own_sums(e):
        return lambda to: outgoing.at[e, to]

    def own_part(e):
        return lambda to: parts[e].at[ka]

    def own_total(e):
        return lambda to: total.at[e, cfg]

    def own_block(e):
        return lambda to: block.at[e]

    def make_sums(e):
        def write(at, value):
            outgoing[e, at] = value

        kpoint_sums(inner, onehot, e, write)

    def send_sums(e):
        first_x[e].start(own_sums(e))
        first[e, cfg] = outgoing[e, cfg]

    def send_part(e):
        first_x[e].wait(own_sums(e))
        value = first[e, 0]
        for at in range(1, n_cfg):
            value = value + first[e, at]
        parts[e][ka, 0] = value
        part_x[e].start(own_part(e))

    def send_total(e):
        part_x[e].wait(own_part(e))
        value = parts[e][0, 0]
        for at in range(1, n_ka):
            value = value + parts[e][at, 0]
        total[e, cfg] = value
        total_x[e].start(own_total(e))

    loads[0].wait()
    onehot = momentum_matrix(kmap)
    loads[1].wait()
    spread_medium(medium, kmap, spread)
    loads[2].wait()
    kpoint_factor(structure, spread, factor, 0)
    kpoint_inner(structure, factor, inner, 0)
    make_sums(0)
    kpoint_factor(structure, spread, factor, 1)
    for load in loads[3:]:
        load.wait()
    config_row(occupation, weight, row)
    pl.semaphore_wait(barrier, n_ka + n_cfg - 2)
    send_sums(0)
    kpoint_inner(structure, factor, inner, 1)
    make_sums(1)
    send_sums(1)
    rows_x.start(own_row)
    own_rows[cfg] = row[...]
    kpoint_squares(spread, factor, inner, square, 0)
    rows_x.wait(own_row)
    line = iota((8, LANES), 0)
    group = jnp.zeros((8, LANES), F32)
    for at in range(n_cfg):
        group = group + jnp.where(line == at, own_rows[at], 0.0)
    part_a[ka, 1] = group
    send_part(0)
    tab = Tables()
    y = [medium_panels(medium, tab, e) for e in energies]
    wide = [shift_panels(shift_a, shift_b, tab, e) for e in energies]
    y_b = [cdot(y[e], block_diag_c(wide[e][0], tab)) for e in energies]
    y_c = [cdot(y[e], block_diag_c(wide[e][1], tab)) for e in energies]
    y_all = [
        (block_diag_c(y[e], tab), block_diag_c(y_b[e], tab), block_diag_c(y_c[e], tab))
        for e in energies
    ]
    send_part(1)
    kpoint_squares(spread, factor, inner, square, 1)
    send_total(0)
    configs = jnp.concatenate([part_a[at, 1] for at in range(n_ka)], axis=0)
    moment_tables(configs, tab, rows_tab, shift_tab)
    send_total(1)
    kept = []
    for e in energies:
        total_x[e].wait(own_total(e))
        sum_t = (gathered_panel(total.at[e], 0), gathered_panel(total.at[e], 4))
        x, x_b, x_c = coarse_panels(y[e], y_b[e], y_c[e], y_all[e], sum_t, tab, per_moment)
        lines = []
        for at, panel in enumerate((x, x_b, x_c)):
            panels[e, at, 0] = panel[0]
            panels[e, at, 1] = panel[1]
            lines.append(
                (panels[e, at, 0, pl.ds(ka, 1), :], panels[e, at, 1, pl.ds(ka, 1), :])
            )
        (top, start), (top_b, with_b), (top_c, with_c) = first_rows(
            (x, x_b, x_c), lines, tab, cfg * 2
        )
        t_parts = translated_c(top)[1]
        tb_parts = translated_c(top_b)[1]
        tc_full, tc_parts = translated_c(top_c)
        avg = rows_stage(start, with_b, with_c, t_parts, tb_parts, tc_parts, rows_tab)
        out = jnp.zeros((8, LANES), F32)
        for c in range(2):
            for site in range(2):
                for side in range(2):
                    at = c * 4 + site * 2 + side
                    lanes = avg[c][site * 8 : site * 8 + 8, side * LANES : side * LANES + LANES]
                    out = jnp.where(line == at, lanes, out)
        block[e] = out
        slot_x[e].start(own_block(e))
        slots[e, ka] = out
        kept.append((top_b, top_c, tc_full, tb_parts, tc_parts, x))
    for e in energies:
        x = kept[e][5]
        d = moment_stage(
            *kept[e], block_diag_c(x, tab), wide[e][0], wide[e][1], shift_tab, tab
        )
        re, im = correction_stage(d, square, e, kmap, tab)
        correction[e, 0:1, :] = re
        correction[e, 1:2, :] = im
        for c in range(2):

            def store(value, e=e, c=c):
                coarse[e, c] = value

            coarse_out(x[c], tab, store)
    for e in energies:
        slot_x[e].wait(own_block(e))
        for at in range(n_ka):
            for c in range(2):
                for site in range(2):
                    for side in range(2):
                        of = c * 4 + site * 2 + side
                        to = site * CHANS + at
                        average[e, c, to : to + 1, side * LANES : side * LANES + LANES] = slots[
                            e, at, of : of + 1, :
                        ]
    rows_x.drain(own_row)
    for e in energies:
        first_x[e].drain(own_sums(e))
        part_x[e].drain(own_part(e))
        total_x[e].drain(own_total(e))
        slot_x[e].drain(own_block(e))


def output_kernel(coarse, average, correction, coarse_to, average_to, correction_to):
    coarse_to[...] = coarse[...]
    average_to[...] = average[...]
    correction_to[...] = correction[...]


def shape(*dims):
    return jax.ShapeDtypeStruct(dims, F32)


VMEM_SPEC = pl.BlockSpec(memory_space=pltpu.VMEM)
SMEM_SPEC = pl.BlockSpec(memory_space=pltpu.SMEM)


def per_device(medium_t, structure, kmap, occupation, cfg_weight, shift_a, shift_b):
    n_ka, n_cfg = lax.axis_size("ka"), lax.axis_size("cfg")
    per_moment = kmap.shape[0] * n_ka * n_cfg // MOMS
    kmap = kmap.reshape(1, LANES)
    kdims = (ENERGIES, 2, CHANS, CHANS, LANES)
    dma = pltpu.SemaphoreType.DMA

    def vmem(*dims):
        return pltpu.VMEM(dims, F32)

    any_spec = pl.BlockSpec(memory_space=pl.ANY)
    shapes = (
        shape(ENERGIES, 2, CHANS, CHANS, MOMS),
        shape(ENERGIES, 2, 2 * CHANS, WIDE),
        shape(ENERGIES, 2, LANES),
    )
    results = pl.pallas_call(
        functools.partial(kernel, per_moment, n_ka, n_cfg),
        out_shape=shapes,
        in_specs=[any_spec] * 4 + [SMEM_SPEC] + [any_spec] * 2,
        out_specs=(VMEM_SPEC,) * 3,
        scratch_shapes=[
            vmem(*kdims), vmem(ENERGIES, 2, CHANS, CHANS, MOMS),
            pltpu.VMEM((1, LANES), jnp.int32), pltpu.VMEM((1, SITES), jnp.int32),
            vmem(ENERGIES, 2, CHANS, CHANS), vmem(ENERGIES, 2, CHANS, CHANS),
            vmem(*kdims), vmem(*kdims), vmem(*kdims), vmem(*kdims),
            vmem(ENERGIES, 3, 2, CHANS, WIDE),
            vmem(SITES + 1, ALPHA, WIDE + LANES),
            vmem(2, WIDE, WIDE),
            vmem(8, LANES), vmem(n_cfg, 8, LANES),
            vmem(ENERGIES, n_cfg, 8, LANES), vmem(ENERGIES, n_cfg, 8, LANES),
            vmem(n_ka, 2, 8, LANES), vmem(n_ka, 1, 8, LANES),
            vmem(ENERGIES, n_cfg, 8, LANES),
            vmem(ENERGIES, 8, LANES), vmem(ENERGIES, n_ka, 8, LANES),
            dma((6,)),
            dma((n_cfg,)), dma((n_cfg,)),
            dma((ENERGIES, n_cfg)), dma((ENERGIES, n_cfg)),
            dma((ENERGIES, n_ka)), dma((ENERGIES, n_ka)),
            dma((ENERGIES, n_cfg)), dma((ENERGIES, n_cfg)),
            dma((ENERGIES, n_ka)), dma((ENERGIES, n_ka)),
        ],
        compiler_params=pltpu.CompilerParams(
            collective_id=0, has_side_effects=True, vmem_limit_bytes=56 * 1024 * 1024
        ),
    )(structure, medium_t, kmap, occupation, cfg_weight, shift_a, shift_b)
    return pl.pallas_call(
        output_kernel,
        out_shape=shapes,
        in_specs=[VMEM_SPEC] * 3,
        out_specs=(VMEM_SPEC,) * 3,
    )(*results)


def solution(mesh):
    placed = (
        P(),
        P(None, None, None, None, ("ka", "cfg")),
        P(("ka", "cfg")),
        P(("ka", "cfg"), None),
        P(("ka", "cfg")),
        P(),
        P(),
    )
    return jax.shard_map(
        per_device,
        mesh=mesh,
        in_specs=placed,
        out_specs=(P(), P(None, None, "cfg", None), P(None, None, ("ka", "cfg"))),
        check_vma=False,
    )
```

```python
import functools

import jax
import jax.numpy as jnp
from jax import lax
from jax.experimental import pallas as pl
from jax.experimental.pallas import tpu as pltpu
from jax.sharding import PartitionSpec as P

MESH = pl.DeviceIdType.MESH
F32 = jnp.float32
BF16 = jnp.bfloat16
NN = (((1,), (0,)), ((), ()))
NT = (((1,), (1,)), ((), ()))

ENERGIES = 2
SITES = 16
CHANS = 16
MOMS = 16
WIDE = SITES * CHANS
LANES = 128
ALPHA = 24


def split(x):
    high = x.astype(BF16)
    return high, (x - high.astype(F32)).astype(BF16)


def dot(left, right, dims=NN):
    return lax.dot_general(left, right, dims, preferred_element_type=F32)


def dot_exact(x, right, dims=NN):
    high, low = split(x)
    rows = x.shape[0]
    both = dot(jnp.concatenate([high, low], axis=0), right, dims)
    return both[:rows] + both[rows:]


def dot3(x, right, dims=NN):
    high, low = split(x)
    rows = x.shape[0]
    both = dot(jnp.concatenate([high, low], axis=0), right[0], dims)
    return both[:rows] + (both[rows:] + dot(high, right[1], dims))


def cdot(x, right, dims=NN):
    rows = x[0].shape[0]
    both = jnp.concatenate([x[0], x[1]], axis=0)
    by_re = dot3(both, right[0], dims)
    by_im = dot3(both, right[1], dims)
    return by_re[:rows] - by_im[rows:], by_im[:rows] + by_re[rows:]


def csplit(x):
    return split(x[0]), split(x[1])


def iota(shape, axis):
    return lax.broadcasted_iota(jnp.int32, shape, axis)


def tile_rows(x, times):
    return jnp.concatenate([x] * times, axis=0)


def quarter_turns(mom, site):
    half = site >> 3
    x = 2 * ((site >> 2) & 1) + half
    y = 2 * ((site >> 1) & 1) + half
    z = 2 * (site & 1) + half
    return ((mom >> 2) * x + ((mom >> 1) & 1) * y + (mom & 1) * z) & 3


def cos_sin(turns):
    sign = (1 - (turns & 2)).astype(F32)
    odd = (turns & 1) == 1
    return jnp.where(odd, 0.0, sign), jnp.where(odd, sign, 0.0)


def site_sum(first, second):
    carry = (first & second) >> 3
    return (first ^ second) ^ (7 * carry)


class Tables:
    def __init__(self):
        rows, cols = iota((WIDE, WIDE), 0), iota((WIDE, WIDE), 1)
        self.row_block, self.col_block = rows >> 4, cols >> 4
        self.row_in, self.col_in = rows & 15, cols & 15
        self.same_block = self.row_block == self.col_block
        self.same_in = self.row_in == self.col_in
        self.cos, self.sin = cos_sin(quarter_turns(self.col_block, self.row_block))
        self.wave_cos = jnp.where(self.same_in, self.cos, 0.0).astype(BF16)
        self.wave_sin = jnp.where(self.same_in, self.sin, 0.0).astype(BF16)
        small_r, small_c = iota((SITES, WIDE), 0), iota((SITES, WIDE), 1)
        self.pick_in = (small_r == (small_c & 15)).astype(F32).astype(BF16)
        self.pick_block = (small_r == (small_c >> 4)).astype(F32).astype(BF16)


def block_diag(panel, tab):
    def spread(part):
        return jnp.where(tab.same_block, tile_rows(part.astype(F32), SITES), 0.0).astype(BF16)

    high, low = split(panel)
    return spread(high), spread(low)


def block_diag_c(panel, tab):
    return block_diag(panel[0], tab), block_diag(panel[1], tab)


HELD_ROWS = 8


def kpoint_mul(store, left, right):
    def body(step, carry):
        start = step * HELD_ROWS
        zero = jnp.zeros((CHANS, LANES), F32)
        p, q, t = [zero] * HELD_ROWS, [zero] * HELD_ROWS, [zero] * HELD_ROWS
        for b in range(CHANS):
            rr, ri = right[0, b], right[1, b]
            less, more = ri - rr, rr + ri
            for j in range(HELD_ROWS):
                lr = left[0, start + j, pl.ds(b, 1), :]
                li = left[1, start + j, pl.ds(b, 1), :]
                p[j] = p[j] + (lr + li) * rr
                q[j] = q[j] + lr * less
                t[j] = t[j] + li * more
        for j in range(HELD_ROWS):
            store(start + j, p[j] - t[j], p[j] + q[j])
        return carry

    lax.fori_loop(0, CHANS // HELD_ROWS, body, 0)


def spread_medium(medium, kmap, spread):
    onehot = (iota((MOMS, LANES), 0) == kmap[...]).astype(F32).astype(BF16)
    for e in range(ENERGIES):
        for c in range(2):
            flat = medium[e, c].reshape(WIDE, MOMS)
            spread[e, c] = dot_exact(flat, onehot).reshape(CHANS, CHANS, LANES)


def kpoint_factor(structure, spread, factor, e):
    f = factor.at[e]

    def put(a, re, im):
        f[0, a] = re
        f[1, a] = im

    kpoint_mul(put, spread.at[e], structure.at[e])


def kpoint_inner(structure, factor, inner, e):
    g, h = structure.at[e], inner.at[e]

    def put(a, re, im):
        h[0, a] = g[0, a] + re
        h[1, a] = g[1, a] + im

    kpoint_mul(put, g, factor.at[e])


def momentum_matrix(kmap):
    onehot = jnp.transpose(((iota((WIDE, LANES), 0) >> 4) == kmap[...]).astype(F32)).astype(BF16)
    return jnp.concatenate([onehot, onehot], axis=0)


def kpoint_sums(inner, onehot, e, write_tile):
    keep = (iota((WIDE, WIDE), 0) >> 4) == (iota((WIDE, WIDE), 1) & 15)
    for c in range(2):
        flat = inner[e, c].reshape(WIDE, LANES)
        parts = jnp.concatenate(split(flat), axis=1)
        by_mom = jnp.where(keep, dot(parts, onehot), 0.0)
        panel = jnp.sum(by_mom.reshape(CHANS, CHANS, WIDE), axis=0)
        for half in range(2):
            for side in range(2):
                write_tile(
                    c * 4 + half * 2 + side,
                    panel[half * 8 : half * 8 + 8, side * LANES : side * LANES + LANES],
                )


def kpoint_squares(spread, factor, tau, square, e):
    y, f, t, s = spread.at[e], factor.at[e], tau.at[e], square.at[e]

    def put_q(a, re, im):
        s[0, a] = f[0, a] + re
        s[1, a] = f[1, a] + im

    def put_t(a, re, im):
        t[0, a] = y[0, a] + re
        t[1, a] = y[1, a] + im

    def put_s(a, re, im):
        s[0, a] = re
        s[1, a] = im

    kpoint_mul(put_q, f, f)
    kpoint_mul(put_t, s, y)
    kpoint_mul(put_s, t, t)


def config_row(occupation, weight, row):
    lane = iota((8, LANES), 1)
    row[...] = jnp.where(lane == SITES, 1.0, 0.0) + jnp.where(
        lane == SITES + 1, weight[0], 0.0
    )
    row[:, 0:SITES] = jnp.broadcast_to(occupation[...].astype(F32), (8, SITES))


def moment_tables(configs, tab, rows_tab, shift_tab):
    turned = jnp.transpose(configs)
    count = turned[0:ALPHA]
    weight = turned[SITES + 1 : SITES + 2]
    weight = weight / jnp.sum(weight, axis=1, keepdims=True)
    live = iota((ALPHA, LANES), 0) <= SITES
    count = jnp.where(live, count, 0.0)
    weighted = count * weight
    flat = configs.astype(BF16)
    lane_r, lane_c = iota((LANES, WIDE), 0), iota((LANES, WIDE), 1)
    pick = (lane_r == (lane_c >> 4)).astype(F32).astype(BF16)
    wide = dot(flat, pick).astype(BF16)
    ones = jnp.ones((LANES, LANES), BF16)
    for s in range(SITES + 1):
        product = weighted * count[s : s + 1]
        rows_tab[s, :, 0:WIDE] = dot_exact(product, wide)
        rows_tab[s, :, WIDE : WIDE + LANES] = dot_exact(product, ones)
    r, c = iota((WIDE, LANES), 0), iota((WIDE, LANES), 1)
    move = (site_sum(r >> 4, r & 15) == c).astype(F32).astype(BF16)
    moved = dot(move, flat, NT)
    moved_b = moved.astype(BF16)
    own = dot(((r >> 4) == c).astype(F32).astype(BF16), flat, NT)
    base = moved * (weight * (1.0 / SITES))
    fold = (tab.row_in == tab.col_block).astype(F32).astype(BF16)
    for which, left in ((0, base), (1, base * own)):
        full = dot_exact(left, moved_b, NT)
        kept = jnp.where(tab.same_block, full, 0.0)
        small = jnp.sum(kept.reshape(SITES, SITES, WIDE), axis=0)
        lanes = dot_exact(small, fold)
        shift_tab[which] = jnp.broadcast_to(
            lanes[:, None, :], (SITES, CHANS, WIDE)
        ).reshape(WIDE, WIDE)


def medium_panels(medium, tab, e):
    out = []
    for c in range(2):
        flat = medium[e, c].reshape(WIDE, MOMS)
        pick = ((iota((MOMS, WIDE), 1) >> 4) == iota((MOMS, WIDE), 0)).astype(F32).astype(BF16)
        by_mom = jnp.where(tab.same_in, dot_exact(flat, pick), 0.0)
        out.append(jnp.sum(by_mom.reshape(CHANS, CHANS, WIDE), axis=1))
    return tuple(out)


def shift_panels(shift_a, shift_b, tab, e):
    def wide(x):
        return dot_exact(x, tab.pick_in)

    b = (wide(shift_b[e, 0]), wide(shift_b[e, 1]))
    c = (
        wide(shift_a[e, 0] - shift_b[e, 0]),
        wide(shift_a[e, 1] - shift_b[e, 1]),
    )
    return b, c


def coarse_panels(y, y_b, y_c, y_all, sum_t, tab, per_moment):
    left = cdot(y, block_diag_c(sum_t, tab), NT)
    scale = 1.0 / per_moment
    left = (left[0] * scale, left[1] * scale)
    out = []
    for base, parts in zip((y, y_b, y_c), y_all):
        step = cdot(left, parts)
        out.append((base[0] + step[0], base[1] + step[1]))
    return out


def first_rows(panels, lines, tab, site0):
    mom = iota((16, WIDE), 1) >> 4
    second = (iota((16, WIDE), 0) >> 3).astype(jnp.int32)
    cos, sin = cos_sin(quarter_turns(mom, site0 + second))
    left_r, left_i = [], []
    for panel, line in zip(panels, lines):
        lr, li = jnp.broadcast_to(line[0], (16, WIDE)), jnp.broadcast_to(line[1], (16, WIDE))
        left_r += [panel[0], lr * cos - li * sin]
        left_i += [panel[1], lr * sin + li * cos]
    rows = 32 * len(panels)
    both = jnp.concatenate(left_r + left_i, axis=0) * (1.0 / SITES)
    by_cos = dot_exact(both, tab.wave_cos, NT)
    by_sin = dot_exact(both, tab.wave_sin, NT)
    real = by_cos[:rows] + by_sin[rows:]
    imag = by_cos[rows:] - by_sin[:rows]
    out = []
    for at in range(0, rows, 32):
        out.append(
            (
                (real[at : at + 16], imag[at : at + 16]),
                (real[at + 16 : at + 32], imag[at + 16 : at + 32]),
            )
        )
    return out


def swap_blocks(x, bit):
    step = 16 * bit
    up = pltpu.roll(x, LANES - step, axis=1)
    if bit == 4:
        return up
    down = pltpu.roll(x, step, axis=1)
    high = ((iota(x.shape, 1) >> 4) & bit) != 0
    return jnp.where(high, down, up)


def all_swaps(x):
    out = {0: x}
    out[4] = swap_blocks(x, 4)
    for at in (0, 4):
        out[at | 2] = swap_blocks(out[at], 2)
    for at in (0, 2, 4, 6):
        out[at | 1] = swap_blocks(out[at], 1)
    return out


def translated(panel):
    low = all_swaps(panel[:, 0:LANES])
    top = all_swaps(panel[:, LANES:WIDE])

    def whole(a, b):
        rows = [jnp.concatenate([a[q], b[q]], axis=1) for q in range(8)]
        rows += [jnp.concatenate([b[q ^ 7], a[q]], axis=1) for q in range(8)]
        return jnp.concatenate(rows, axis=0)

    low_parts = {q: split(v) for q, v in low.items()}
    top_parts = {q: split(v) for q, v in top.items()}
    parts = tuple(
        whole({q: v[p] for q, v in low_parts.items()}, {q: v[p] for q, v in top_parts.items()})
        for p in range(2)
    )
    return whole(low, top), parts


def translated_c(panel):
    real, imag = translated(panel[0]), translated(panel[1])
    return (real[0], imag[0]), (real[1], imag[1])


def rows_stage(start, with_b, with_c, t_parts, tb_parts, tc_parts, rows_tab):
    row = iota((ALPHA, WIDE), 0)
    block = iota((ALPHA, WIDE), 1) >> 4

    def opened(c):
        out = []
        for at in (0, 8):
            ub = jnp.broadcast_to(with_b[c][at : at + 1], (ALPHA, WIDE))
            uc = jnp.broadcast_to(with_c[c][at : at + 1], (ALPHA, WIDE))
            out.append(jnp.where(row == block, uc, jnp.where(row == SITES, ub, 0.0)))
        return jnp.concatenate(out, axis=0)

    begin = (opened(0), opened(1))
    hop_b = cdot(begin, tb_parts)
    hop_c = cdot(begin, tc_parts)
    inner = []
    for c in range(2):
        out = []
        for site in range(2):
            g = jnp.zeros((ALPHA, WIDE), F32)
            for s in range(SITES + 1):
                at = site * ALPHA + s
                pair = rows_tab[s, :, WIDE : WIDE + LANES]
                g = g + jnp.concatenate([pair, pair], axis=1) * hop_b[c][at : at + 1]
                g = g + rows_tab[s, :, 0:WIDE] * hop_c[c][at : at + 1]
            out.append(g)
        inner.append(jnp.concatenate(out, axis=0))
    mean = rows_tab[SITES, SITES : SITES + 1, 0:WIDE]

    def eight(parts):
        return jnp.concatenate([jnp.broadcast_to(p, (8, WIDE)) for p in parts], axis=0)

    ends = tuple(
        eight([inner[c][site * ALPHA + SITES : site * ALPHA + SITES + 1] for site in range(2)])
        for c in range(2)
    )
    by_b = cdot(ends, tb_parts)
    by_c = cdot(tuple(inner), tc_parts)
    z = []
    for c in range(2):
        picked = []
        for site in range(2):
            lines = by_c[c][site * ALPHA : site * ALPHA + ALPHA]
            picked.append(jnp.sum(jnp.where(row == block, lines, 0.0), axis=0, keepdims=True))
        z.append(with_b[c] + with_c[c] * mean - ends[c] + by_b[c] + eight(picked))
    last = cdot(tuple(z), t_parts)
    return start[0] - last[0], start[1] - last[1]


def moment_stage(top_b, top_c, tc_full, tb_parts, tc_parts, x, x_parts, b_wide, c_wide, shift_tab, tab):
    def head(wide):
        return wide[0][:, 0:CHANS], wide[1][:, 0:CHANS]

    b_in, c_in = head(b_wide), head(c_wide)
    small = (
        jnp.concatenate([b_in[0], c_in[0]], axis=0),
        jnp.concatenate([b_in[1], c_in[1]], axis=0),
    )
    lead_b = cdot(small, csplit(top_b))
    lead_c = cdot(small, csplit(top_c))
    bb, cb = [v[0:CHANS] for v in lead_b], [v[CHANS:] for v in lead_b]
    bc, cc = [v[0:CHANS] for v in lead_c], [v[CHANS:] for v in lead_c]
    two = shift_tab[1, 0:1, :]
    mean = shift_tab[1, 0:1, 0:1]
    zero = [bb[c] + mean * (bc[c] + cb[c]) + two * cc[c] for c in range(2)]
    by_b = cdot(tuple(zero), tb_parts)
    by_c = cdot(tuple(jnp.concatenate([bb[c], cb[c]], axis=0) for c in range(2)), tc_parts)

    def scaled(which):
        return split(tc_full[0] * shift_tab[which]), split(tc_full[1] * shift_tab[which])

    pair = cdot(tuple(bc), scaled(0))
    triple = cdot(tuple(cc), scaled(1))
    line = []
    for c in range(2):
        third = by_b[c] + mean * by_c[c][0:CHANS] + two * by_c[c][CHANS:] + pair[c] + triple[c]
        line.append(third - (bb[c] + mean * (cb[c] + bc[c]) + two * cc[c]))
    m_cos = dot_exact(jnp.concatenate(line, axis=0), tab.wave_cos)
    m_sin = dot_exact(jnp.concatenate(line, axis=0), tab.wave_sin)
    m_r = m_cos[:CHANS] - m_sin[CHANS:] + b_wide[0] + mean * c_wide[0]
    m_i = m_sin[:CHANS] + m_cos[CHANS:] + b_wide[1] + mean * c_wide[1]
    d = cdot(cdot(x, block_diag_c((m_r, m_i), tab)), x_parts)
    return -d[0], -d[1]


def correction_stage(d, square, e, kmap, tab):
    onehot = ((iota((WIDE, LANES), 0) >> 4) == kmap[...]).astype(F32).astype(BF16)
    keep = tab.row_block == tab.col_in

    def spread(panel):
        high, low = split(panel)

        def one(part):
            full = jnp.where(keep, tile_rows(part.astype(F32), CHANS), 0.0)
            return dot(full.astype(BF16), onehot)

        return one(high) + one(low)

    dr, di = spread(d[0]), spread(d[1])
    sr, si = square[e, 0].reshape(WIDE, LANES), square[e, 1].reshape(WIDE, LANES)
    re = jnp.sum(dr * sr - di * si, axis=0, keepdims=True)
    im = jnp.sum(dr * si + di * sr, axis=0, keepdims=True)
    return re, im


def coarse_out(x, tab, store):
    fold = (tab.col_block == tab.row_in)
    pick = (iota((WIDE, MOMS), 0) >> 4 == iota((WIDE, MOMS), 1)).astype(F32).astype(BF16)
    high = x.astype(BF16)
    rest = x - high.astype(F32)
    mid = rest.astype(BF16)
    low = (rest - mid.astype(F32)).astype(BF16)
    total = None
    for part in (low, mid, high):
        wide = jnp.broadcast_to(part.astype(F32)[:, None, :], (CHANS, CHANS, WIDE))
        wide = jnp.where(tab.same_in, wide.reshape(WIDE, WIDE), 0.0).astype(BF16)
        piece = dot(wide, pick)
        total = piece if total is None else total + piece
    store(total.reshape(CHANS, CHANS, MOMS))


def gathered_panel(tiles, at):
    top = jnp.concatenate([tiles[at], tiles[at + 1]], axis=1)
    low = jnp.concatenate([tiles[at + 2], tiles[at + 3]], axis=1)
    return jnp.concatenate([top, low], axis=0)


def offsets(outer, inner, torus):
    def hops(step):
        first = min(step[0], outer - step[0])
        return first + (min(step[1], inner - step[1]) if torus else 0.5 * (step[1] > 0))

    steps = [(a, b) for a in range(outer) for b in range(inner) if a or b]
    return sorted(steps, key=lambda step: (-hops(step), step))


class Group:
    def __init__(self, axis, inner, torus):
        self.axis, self.inner = axis, inner
        self.count = lax.axis_size(axis)
        self.outer = self.count // inner
        self.steps = offsets(self.outer, inner, torus)
        self.me = lax.axis_index(axis)

    def peer(self, step):
        first = lax.rem(self.me // self.inner + step[0], self.outer)
        return first * self.inner + lax.rem(lax.rem(self.me, self.inner) + step[1], self.inner)

    def greet(self, barrier):
        for step in self.steps:
            pl.semaphore_signal(
                barrier, inc=1, device_id={self.axis: self.peer(step)}, device_id_type=MESH
            )


class Exchange:
    def __init__(self, group, slots, send, recv):
        self.group, self.slots, self.send, self.recv = group, slots, send, recv

    def copy(self, src, at, number, peer):
        return pltpu.make_async_remote_copy(
            src_ref=src, dst_ref=self.slots.at[at], send_sem=self.send.at[number],
            recv_sem=self.recv.at[at], device_id={self.group.axis: peer}, device_id_type=MESH,
        )

    def start(self, source):
        for number, step in enumerate(self.group.steps):
            peer = self.group.peer(step)
            self.copy(source(peer), self.group.me, number, peer).start()

    def wait(self, source):
        for number, step in enumerate(self.group.steps[::-1]):
            peer = self.group.peer(step)
            self.copy(source(self.group.me), peer, number, peer).wait_recv()

    def drain(self, source):
        for number, step in enumerate(self.group.steps):
            peer = self.group.peer(step)
            self.copy(source(self.group.me), self.group.me, number, peer).wait_send()


def kernel(
    per_moment, n_ka, n_cfg,
    structure_hbm, medium_hbm, kmap_hbm, occupation_hbm, weight, shift_a_hbm, shift_b_hbm,
    coarse, average, correction,
    structure, medium, kmap, occupation, shift_a, shift_b,
    spread, factor, inner, square, panels, rows_tab, shift_tab,
    row, own_rows, outgoing, first, part, total, block, slots,
    load_sem, row_send, row_recv, first_send, first_recv, part_send, part_recv,
    total_send, total_recv, slot_send, slot_recv,
):
    pairs = (
        (kmap_hbm, kmap), (medium_hbm, medium), (structure_hbm, structure),
        (occupation_hbm, occupation), (shift_a_hbm, shift_a), (shift_b_hbm, shift_b),
    )
    loads = [
        pltpu.make_async_copy(source, to, load_sem.at[at]) for at, (source, to) in enumerate(pairs)
    ]
    for load in loads[:3]:
        load.start()
    barrier = pltpu.get_barrier_semaphore()
    by_ka, by_cfg = Group("ka", 4, True), Group("cfg", 2, False)
    by_ka.greet(barrier)
    by_cfg.greet(barrier)
    for load in loads[3:]:
        load.start()
    energies = range(ENERGIES)
    rows_x = Exchange(by_cfg, own_rows, row_send, row_recv)
    first_x = Exchange(by_cfg, first, first_send, first_recv)
    part_x = Exchange(by_ka, part, part_send, part_recv)
    total_x = Exchange(by_cfg, total, total_send, total_recv)
    slot_x = Exchange(by_ka, slots, slot_send, slot_recv)
    ka, cfg = lax.axis_index("ka"), lax.axis_index("cfg")

    def own_row(to):
        return row

    def own_sums(to):
        return outgoing.at[to]

    def own_part(to):
        return part.at[ka]

    def own_total(to):
        return total.at[cfg]

    def own_block(to):
        return block

    loads[0].wait()
    onehot = momentum_matrix(kmap)
    loads[1].wait()
    spread_medium(medium, kmap, spread)
    loads[2].wait()
    for e in energies:
        kpoint_factor(structure, spread, factor, e)
        kpoint_inner(structure, factor, inner, e)

        def write(at, value, e=e):
            outgoing[at, e] = value

        kpoint_sums(inner, onehot, e, write)
    for load in loads[3:]:
        load.wait()
    config_row(occupation, weight, row)
    pl.semaphore_wait(barrier, n_ka + n_cfg - 2)
    first_x.start(own_sums)
    first[cfg] = outgoing[cfg]
    rows_x.start(own_row)
    own_rows[cfg] = row[...]
    kpoint_squares(spread, factor, inner, square, 0)
    rows_x.wait(own_row)
    line = iota((8, LANES), 0)
    group = jnp.zeros((8, LANES), F32)
    for at in range(n_cfg):
        group = group + jnp.where(line == at, own_rows[at], 0.0)
    first_x.wait(own_sums)
    for e in energies:
        value = first[0, e]
        for at in range(1, n_cfg):
            value = value + first[at, e]
        part[ka, e] = value
    part[ka, ENERGIES] = group
    part_x.start(own_part)
    tab = Tables()
    y = [medium_panels(medium, tab, e) for e in energies]
    wide = [shift_panels(shift_a, shift_b, tab, e) for e in energies]
    y_b = [cdot(y[e], block_diag_c(wide[e][0], tab)) for e in energies]
    y_c = [cdot(y[e], block_diag_c(wide[e][1], tab)) for e in energies]
    y_all = [
        (block_diag_c(y[e], tab), block_diag_c(y_b[e], tab), block_diag_c(y_c[e], tab))
        for e in energies
    ]
    kpoint_squares(spread, factor, inner, square, 1)
    part_x.wait(own_part)
    for e in energies:
        value = part[0, e]
        for at in range(1, n_ka):
            value = value + part[at, e]
        total[cfg, e] = value
    total_x.start(own_total)
    configs = jnp.concatenate([part[at, ENERGIES] for at in range(n_ka)], axis=0)
    moment_tables(configs, tab, rows_tab, shift_tab)
    total_x.wait(own_total)
    found = []
    for e in energies:
        tiles = [total[at, e] for at in range(n_cfg)]
        sum_t = (gathered_panel(tiles, 0), gathered_panel(tiles, 4))
        found.append(coarse_panels(y[e], y_b[e], y_c[e], y_all[e], sum_t, tab, per_moment))
    rows = []
    for e in energies:
        lines = []
        for at, panel in enumerate(found[e]):
            panels[e, at, 0] = panel[0]
            panels[e, at, 1] = panel[1]
            lines.append(
                (panels[e, at, 0, pl.ds(ka, 1), :], panels[e, at, 1, pl.ds(ka, 1), :])
            )
        rows.append(first_rows(found[e], lines, tab, cfg * 2))
    t_all = [translated_c(rows[e][0][0])[1] for e in energies]
    tb_all = [translated_c(rows[e][1][0])[1] for e in energies]
    tc_all = [translated_c(rows[e][2][0]) for e in energies]
    averages = [
        rows_stage(
            rows[e][0][1], rows[e][1][1], rows[e][2][1], t_all[e], tb_all[e], tc_all[e][1], rows_tab
        )
        for e in energies
    ]
    for e in energies:
        out = jnp.zeros((8, LANES), F32)
        for c in range(2):
            for site in range(2):
                for side in range(2):
                    at = c * 4 + site * 2 + side
                    lanes = averages[e][c][
                        site * 8 : site * 8 + 8, side * LANES : side * LANES + LANES
                    ]
                    out = jnp.where(line == at, lanes, out)
        block[e] = out
    slot_x.start(own_block)
    slots[ka] = block[...]
    moments = [
        moment_stage(
            rows[e][1][0], rows[e][2][0], tc_all[e][0], tb_all[e], tc_all[e][1], found[e][0],
            block_diag_c(found[e][0], tab), wide[e][0], wide[e][1], shift_tab, tab,
        )
        for e in energies
    ]
    for e in energies:
        re, im = correction_stage(moments[e], square, e, kmap, tab)
        correction[e, 0:1, :] = re
        correction[e, 1:2, :] = im
        for c in range(2):

            def store(value, e=e, c=c):
                coarse[e, c] = value

            coarse_out(found[e][0][c], tab, store)
    slot_x.wait(own_block)
    for e in energies:
        for at in range(n_ka):
            for c in range(2):
                for site in range(2):
                    for side in range(2):
                        of = c * 4 + site * 2 + side
                        to = site * CHANS + at
                        average[e, c, to : to + 1, side * LANES : side * LANES + LANES] = slots[
                            at, e, of : of + 1, :
                        ]
    rows_x.drain(own_row)
    first_x.drain(own_sums)
    part_x.drain(own_part)
    total_x.drain(own_total)
    slot_x.drain(own_block)


def output_kernel(coarse, average, correction, coarse_to, average_to, correction_to):
    coarse_to[...] = coarse[...]
    average_to[...] = average[...]
    correction_to[...] = correction[...]


def shape(*dims):
    return jax.ShapeDtypeStruct(dims, F32)


VMEM_SPEC = pl.BlockSpec(memory_space=pltpu.VMEM)
SMEM_SPEC = pl.BlockSpec(memory_space=pltpu.SMEM)


def per_device(medium_t, structure, kmap, occupation, cfg_weight, shift_a, shift_b):
    n_ka, n_cfg = lax.axis_size("ka"), lax.axis_size("cfg")
    per_moment = kmap.shape[0] * n_ka * n_cfg // MOMS
    kmap = kmap.reshape(1, LANES)
    kdims = (ENERGIES, 2, CHANS, CHANS, LANES)
    dma = pltpu.SemaphoreType.DMA

    def vmem(*dims):
        return pltpu.VMEM(dims, F32)

    any_spec = pl.BlockSpec(memory_space=pl.ANY)
    shapes = (
        shape(ENERGIES, 2, CHANS, CHANS, MOMS),
        shape(ENERGIES, 2, 2 * CHANS, WIDE),
        shape(ENERGIES, 2, LANES),
    )
    results = pl.pallas_call(
        functools.partial(kernel, per_moment, n_ka, n_cfg),
        out_shape=shapes,
        in_specs=[any_spec] * 4 + [SMEM_SPEC] + [any_spec] * 2,
        out_specs=(VMEM_SPEC,) * 3,
        scratch_shapes=[
            vmem(*kdims), vmem(ENERGIES, 2, CHANS, CHANS, MOMS),
            pltpu.VMEM((1, LANES), jnp.int32), pltpu.VMEM((1, SITES), jnp.int32),
            vmem(ENERGIES, 2, CHANS, CHANS), vmem(ENERGIES, 2, CHANS, CHANS),
            vmem(*kdims), vmem(*kdims), vmem(*kdims), vmem(*kdims),
            vmem(ENERGIES, 3, 2, CHANS, WIDE),
            vmem(SITES + 1, ALPHA, WIDE + LANES),
            vmem(2, WIDE, WIDE),
            vmem(8, LANES), vmem(n_cfg, 8, LANES),
            vmem(n_cfg, ENERGIES, 8, LANES), vmem(n_cfg, ENERGIES, 8, LANES),
            vmem(n_ka, ENERGIES + 1, 8, LANES),
            vmem(n_cfg, ENERGIES, 8, LANES),
            vmem(ENERGIES, 8, LANES), vmem(n_ka, ENERGIES, 8, LANES),
            dma((6,)),
            dma((n_cfg,)), dma((n_cfg,)),
            dma((n_cfg,)), dma((n_cfg,)),
            dma((n_ka,)), dma((n_ka,)),
            dma((n_cfg,)), dma((n_cfg,)),
            dma((n_ka,)), dma((n_ka,)),
        ],
        compiler_params=pltpu.CompilerParams(
            collective_id=0, has_side_effects=True, vmem_limit_bytes=56 * 1024 * 1024
        ),
    )(structure, medium_t, kmap, occupation, cfg_weight, shift_a, shift_b)
    return pl.pallas_call(
        output_kernel,
        out_shape=shapes,
        in_specs=[VMEM_SPEC] * 3,
        out_specs=(VMEM_SPEC,) * 3,
    )(*results)


def solution(mesh):
    placed = (
        P(),
        P(None, None, None, None, ("ka", "cfg")),
        P(("ka", "cfg")),
        P(("ka", "cfg"), None),
        P(("ka", "cfg")),
        P(),
        P(),
    )
    return jax.shard_map(
        per_device,
        mesh=mesh,
        in_specs=placed,
        out_specs=(P(), P(None, None, "cfg", None), P(None, None, ("ka", "cfg"))),
        check_vma=False,
    )
```

```python
import functools

import jax
import jax.numpy as jnp
from jax import lax
from jax.experimental import pallas as pl
from jax.experimental.pallas import tpu as pltpu
from jax.sharding import PartitionSpec as P

MESH = pl.DeviceIdType.MESH
F32 = jnp.float32
BF16 = jnp.bfloat16
NN = (((1,), (0,)), ((), ()))
NT = (((1,), (1,)), ((), ()))

ENERGIES = 2
SITES = 16
CHANS = 16
MOMS = 16
WIDE = SITES * CHANS
LANES = 128
ALPHA = 24


def split(x):
    high = x.astype(BF16)
    return high, (x - high.astype(F32)).astype(BF16)


def dot(left, right, dims=NN):
    return lax.dot_general(left, right, dims, preferred_element_type=F32)


def dot_exact(x, right, dims=NN):
    high, low = split(x)
    rows = x.shape[0]
    both = dot(jnp.concatenate([high, low], axis=0), right, dims)
    return both[:rows] + both[rows:]


def dot3(x, right, dims=NN):
    high, low = split(x)
    rows = x.shape[0]
    both = dot(jnp.concatenate([high, low], axis=0), right[0], dims)
    return both[:rows] + (both[rows:] + dot(high, right[1], dims))


def cdot(x, right, dims=NN):
    rows = x[0].shape[0]
    both = jnp.concatenate([x[0], x[1]], axis=0)
    by_re = dot3(both, right[0], dims)
    by_im = dot3(both, right[1], dims)
    return by_re[:rows] - by_im[rows:], by_im[:rows] + by_re[rows:]


def csplit(x):
    return split(x[0]), split(x[1])


def iota(shape, axis):
    return lax.broadcasted_iota(jnp.int32, shape, axis)


def tile_rows(x, times):
    return jnp.concatenate([x] * times, axis=0)


def quarter_turns(mom, site):
    half = site >> 3
    x = 2 * ((site >> 2) & 1) + half
    y = 2 * ((site >> 1) & 1) + half
    z = 2 * (site & 1) + half
    return ((mom >> 2) * x + ((mom >> 1) & 1) * y + (mom & 1) * z) & 3


def cos_sin(turns):
    sign = (1 - (turns & 2)).astype(F32)
    odd = (turns & 1) == 1
    return jnp.where(odd, 0.0, sign), jnp.where(odd, sign, 0.0)


def site_sum(first, second):
    carry = (first & second) >> 3
    return (first ^ second) ^ (7 * carry)


class Tables:
    def __init__(self):
        rows, cols = iota((WIDE, WIDE), 0), iota((WIDE, WIDE), 1)
        self.row_block, self.col_block = rows >> 4, cols >> 4
        self.row_in, self.col_in = rows & 15, cols & 15
        self.same_block = self.row_block == self.col_block
        self.same_in = self.row_in == self.col_in
        self.cos, self.sin = cos_sin(quarter_turns(self.col_block, self.row_block))
        self.wave_cos = jnp.where(self.same_in, self.cos, 0.0).astype(BF16)
        self.wave_sin = jnp.where(self.same_in, self.sin, 0.0).astype(BF16)
        small_r, small_c = iota((SITES, WIDE), 0), iota((SITES, WIDE), 1)
        self.pick_in = (small_r == (small_c & 15)).astype(F32).astype(BF16)
        self.pick_block = (small_r == (small_c >> 4)).astype(F32).astype(BF16)


def block_diag(panel, tab):
    def spread(part):
        return jnp.where(tab.same_block, tile_rows(part.astype(F32), SITES), 0.0).astype(BF16)

    high, low = split(panel)
    return spread(high), spread(low)


def block_diag_c(panel, tab):
    return block_diag(panel[0], tab), block_diag(panel[1], tab)


HELD_ROWS = 8


def kpoint_mul(store, left, right):
    def body(step, carry):
        start = step * HELD_ROWS
        zero = jnp.zeros((CHANS, LANES), F32)
        p, q, t = [zero] * HELD_ROWS, [zero] * HELD_ROWS, [zero] * HELD_ROWS
        for b in range(CHANS):
            rr, ri = right[0, b], right[1, b]
            less, more = ri - rr, rr + ri
            for j in range(HELD_ROWS):
                lr = left[0, start + j, pl.ds(b, 1), :]
                li = left[1, start + j, pl.ds(b, 1), :]
                p[j] = p[j] + (lr + li) * rr
                q[j] = q[j] + lr * less
                t[j] = t[j] + li * more
        for j in range(HELD_ROWS):
            store(start + j, p[j] - t[j], p[j] + q[j])
        return carry

    lax.fori_loop(0, CHANS // HELD_ROWS, body, 0)


def spread_medium(medium, kmap, spread):
    onehot = (iota((MOMS, LANES), 0) == kmap[...]).astype(F32).astype(BF16)
    for e in range(ENERGIES):
        for c in range(2):
            flat = medium[e, c].reshape(WIDE, MOMS)
            spread[e, c] = dot_exact(flat, onehot).reshape(CHANS, CHANS, LANES)


def kpoint_factor(structure, spread, factor, e):
    f = factor.at[e]

    def put(a, re, im):
        f[0, a] = re
        f[1, a] = im

    kpoint_mul(put, spread.at[e], structure.at[e])


def kpoint_inner(structure, factor, inner, e):
    g, h = structure.at[e], inner.at[e]

    def put(a, re, im):
        h[0, a] = g[0, a] + re
        h[1, a] = g[1, a] + im

    kpoint_mul(put, g, factor.at[e])


def momentum_matrix(kmap):
    onehot = jnp.transpose(((iota((WIDE, LANES), 0) >> 4) == kmap[...]).astype(F32)).astype(BF16)
    return jnp.concatenate([onehot, onehot], axis=0)


def kpoint_sums(inner, onehot, e, write_tile):
    keep = (iota((WIDE, WIDE), 0) >> 4) == (iota((WIDE, WIDE), 1) & 15)
    for c in range(2):
        flat = inner[e, c].reshape(WIDE, LANES)
        parts = jnp.concatenate(split(flat), axis=1)
        by_mom = jnp.where(keep, dot(parts, onehot), 0.0)
        panel = jnp.sum(by_mom.reshape(CHANS, CHANS, WIDE), axis=0)
        for half in range(2):
            for side in range(2):
                write_tile(
                    c * 4 + half * 2 + side,
                    panel[half * 8 : half * 8 + 8, side * LANES : side * LANES + LANES],
                )


def kpoint_squares(spread, factor, tau, square, e):
    y, f, t, s = spread.at[e], factor.at[e], tau.at[e], square.at[e]

    def put_q(a, re, im):
        s[0, a] = f[0, a] + re
        s[1, a] = f[1, a] + im

    def put_t(a, re, im):
        t[0, a] = y[0, a] + re
        t[1, a] = y[1, a] + im

    def put_s(a, re, im):
        s[0, a] = re
        s[1, a] = im

    kpoint_mul(put_q, f, f)
    kpoint_mul(put_t, s, y)
    kpoint_mul(put_s, t, t)


def config_row(occupation, weight, row):
    lane = iota((8, LANES), 1)
    row[...] = jnp.where(lane == SITES, 1.0, 0.0) + jnp.where(
        lane == SITES + 1, weight[0], 0.0
    )
    row[:, 0:SITES] = jnp.broadcast_to(occupation[...].astype(F32), (8, SITES))


def moment_tables(configs, tab, rows_tab, shift_tab):
    turned = jnp.transpose(configs)
    count = turned[0:ALPHA]
    weight = turned[SITES + 1 : SITES + 2]
    weight = weight / jnp.sum(weight, axis=1, keepdims=True)
    live = iota((ALPHA, LANES), 0) <= SITES
    count = jnp.where(live, count, 0.0)
    weighted = count * weight
    flat = configs.astype(BF16)
    lane_r, lane_c = iota((LANES, WIDE), 0), iota((LANES, WIDE), 1)
    pick = (lane_r == (lane_c >> 4)).astype(F32).astype(BF16)
    wide = dot(flat, pick).astype(BF16)
    ones = jnp.ones((LANES, LANES), BF16)
    for s in range(SITES + 1):
        product = weighted * count[s : s + 1]
        rows_tab[s, :, 0:WIDE] = dot_exact(product, wide)
        rows_tab[s, :, WIDE : WIDE + LANES] = dot_exact(product, ones)
    r, c = iota((WIDE, LANES), 0), iota((WIDE, LANES), 1)
    move = (site_sum(r >> 4, r & 15) == c).astype(F32).astype(BF16)
    moved = dot(move, flat, NT)
    moved_b = moved.astype(BF16)
    own = dot(((r >> 4) == c).astype(F32).astype(BF16), flat, NT)
    base = moved * (weight * (1.0 / SITES))
    fold = (tab.row_in == tab.col_block).astype(F32).astype(BF16)
    for which, left in ((0, base), (1, base * own)):
        full = dot_exact(left, moved_b, NT)
        kept = jnp.where(tab.same_block, full, 0.0)
        small = jnp.sum(kept.reshape(SITES, SITES, WIDE), axis=0)
        lanes = dot_exact(small, fold)
        shift_tab[which] = jnp.broadcast_to(
            lanes[:, None, :], (SITES, CHANS, WIDE)
        ).reshape(WIDE, WIDE)


def medium_panels(medium, tab, e):
    out = []
    for c in range(2):
        flat = medium[e, c].reshape(WIDE, MOMS)
        pick = ((iota((MOMS, WIDE), 1) >> 4) == iota((MOMS, WIDE), 0)).astype(F32).astype(BF16)
        by_mom = jnp.where(tab.same_in, dot_exact(flat, pick), 0.0)
        out.append(jnp.sum(by_mom.reshape(CHANS, CHANS, WIDE), axis=1))
    return tuple(out)


def shift_panels(shift_a, shift_b, tab, e):
    def wide(x):
        return dot_exact(x, tab.pick_in)

    b = (wide(shift_b[e, 0]), wide(shift_b[e, 1]))
    c = (
        wide(shift_a[e, 0] - shift_b[e, 0]),
        wide(shift_a[e, 1] - shift_b[e, 1]),
    )
    return b, c


def coarse_panels(y, y_b, y_c, y_all, sum_t, tab, per_moment):
    left = cdot(y, block_diag_c(sum_t, tab), NT)
    scale = 1.0 / per_moment
    left = (left[0] * scale, left[1] * scale)
    out = []
    for base, parts in zip((y, y_b, y_c), y_all):
        step = cdot(left, parts)
        out.append((base[0] + step[0], base[1] + step[1]))
    return out


def first_rows(panels, lines, tab, site0):
    mom = iota((16, WIDE), 1) >> 4
    second = (iota((16, WIDE), 0) >> 3).astype(jnp.int32)
    cos, sin = cos_sin(quarter_turns(mom, site0 + second))
    left_r, left_i = [], []
    for panel, line in zip(panels, lines):
        lr, li = jnp.broadcast_to(line[0], (16, WIDE)), jnp.broadcast_to(line[1], (16, WIDE))
        left_r += [panel[0], lr * cos - li * sin]
        left_i += [panel[1], lr * sin + li * cos]
    rows = 32 * len(panels)
    both = jnp.concatenate(left_r + left_i, axis=0) * (1.0 / SITES)
    by_cos = dot_exact(both, tab.wave_cos, NT)
    by_sin = dot_exact(both, tab.wave_sin, NT)
    real = by_cos[:rows] + by_sin[rows:]
    imag = by_cos[rows:] - by_sin[:rows]
    out = []
    for at in range(0, rows, 32):
        out.append(
            (
                (real[at : at + 16], imag[at : at + 16]),
                (real[at + 16 : at + 32], imag[at + 16 : at + 32]),
            )
        )
    return out


def swap_blocks(x, bit):
    step = 16 * bit
    up = pltpu.roll(x, LANES - step, axis=1)
    if bit == 4:
        return up
    down = pltpu.roll(x, step, axis=1)
    high = ((iota(x.shape, 1) >> 4) & bit) != 0
    return jnp.where(high, down, up)


def all_swaps(x):
    out = {0: x}
    out[4] = swap_blocks(x, 4)
    for at in (0, 4):
        out[at | 2] = swap_blocks(out[at], 2)
    for at in (0, 2, 4, 6):
        out[at | 1] = swap_blocks(out[at], 1)
    return out


def translated(panel):
    low = all_swaps(panel[:, 0:LANES])
    top = all_swaps(panel[:, LANES:WIDE])

    def whole(a, b):
        rows = [jnp.concatenate([a[q], b[q]], axis=1) for q in range(8)]
        rows += [jnp.concatenate([b[q ^ 7], a[q]], axis=1) for q in range(8)]
        return jnp.concatenate(rows, axis=0)

    low_parts = {q: split(v) for q, v in low.items()}
    top_parts = {q: split(v) for q, v in top.items()}
    parts = tuple(
        whole({q: v[p] for q, v in low_parts.items()}, {q: v[p] for q, v in top_parts.items()})
        for p in range(2)
    )
    return whole(low, top), parts


def translated_c(panel):
    real, imag = translated(panel[0]), translated(panel[1])
    return (real[0], imag[0]), (real[1], imag[1])


def rows_stage(start, with_b, with_c, t_parts, tb_parts, tc_parts, rows_tab):
    row = iota((ALPHA, WIDE), 0)
    block = iota((ALPHA, WIDE), 1) >> 4

    def opened(c):
        out = []
        for at in (0, 8):
            ub = jnp.broadcast_to(with_b[c][at : at + 1], (ALPHA, WIDE))
            uc = jnp.broadcast_to(with_c[c][at : at + 1], (ALPHA, WIDE))
            out.append(jnp.where(row == block, uc, jnp.where(row == SITES, ub, 0.0)))
        return jnp.concatenate(out, axis=0)

    begin = (opened(0), opened(1))
    hop_b = cdot(begin, tb_parts)
    hop_c = cdot(begin, tc_parts)
    inner = []
    for c in range(2):
        out = []
        for site in range(2):
            g = jnp.zeros((ALPHA, WIDE), F32)
            for s in range(SITES + 1):
                at = site * ALPHA + s
                pair = rows_tab[s, :, WIDE : WIDE + LANES]
                g = g + jnp.concatenate([pair, pair], axis=1) * hop_b[c][at : at + 1]
                g = g + rows_tab[s, :, 0:WIDE] * hop_c[c][at : at + 1]
            out.append(g)
        inner.append(jnp.concatenate(out, axis=0))
    mean = rows_tab[SITES, SITES : SITES + 1, 0:WIDE]

    def eight(parts):
        return jnp.concatenate([jnp.broadcast_to(p, (8, WIDE)) for p in parts], axis=0)

    ends = tuple(
        eight([inner[c][site * ALPHA + SITES : site * ALPHA + SITES + 1] for site in range(2)])
        for c in range(2)
    )
    by_b = cdot(ends, tb_parts)
    by_c = cdot(tuple(inner), tc_parts)
    z = []
    for c in range(2):
        picked = []
        for site in range(2):
            lines = by_c[c][site * ALPHA : site * ALPHA + ALPHA]
            picked.append(jnp.sum(jnp.where(row == block, lines, 0.0), axis=0, keepdims=True))
        z.append(with_b[c] + with_c[c] * mean - ends[c] + by_b[c] + eight(picked))
    last = cdot(tuple(z), t_parts)
    return start[0] - last[0], start[1] - last[1]


def moment_stage(top_b, top_c, tc_full, tb_parts, tc_parts, x, x_parts, b_wide, c_wide, shift_tab, tab):
    def head(wide):
        return wide[0][:, 0:CHANS], wide[1][:, 0:CHANS]

    b_in, c_in = head(b_wide), head(c_wide)
    small = (
        jnp.concatenate([b_in[0], c_in[0]], axis=0),
        jnp.concatenate([b_in[1], c_in[1]], axis=0),
    )
    lead_b = cdot(small, csplit(top_b))
    lead_c = cdot(small, csplit(top_c))
    bb, cb = [v[0:CHANS] for v in lead_b], [v[CHANS:] for v in lead_b]
    bc, cc = [v[0:CHANS] for v in lead_c], [v[CHANS:] for v in lead_c]
    two = shift_tab[1, 0:1, :]
    mean = shift_tab[1, 0:1, 0:1]
    zero = [bb[c] + mean * (bc[c] + cb[c]) + two * cc[c] for c in range(2)]
    by_b = cdot(tuple(zero), tb_parts)
    by_c = cdot(tuple(jnp.concatenate([bb[c], cb[c]], axis=0) for c in range(2)), tc_parts)

    def scaled(which):
        return split(tc_full[0] * shift_tab[which]), split(tc_full[1] * shift_tab[which])

    pair = cdot(tuple(bc), scaled(0))
    triple = cdot(tuple(cc), scaled(1))
    line = []
    for c in range(2):
        third = by_b[c] + mean * by_c[c][0:CHANS] + two * by_c[c][CHANS:] + pair[c] + triple[c]
        line.append(third - (bb[c] + mean * (cb[c] + bc[c]) + two * cc[c]))
    m_cos = dot_exact(jnp.concatenate(line, axis=0), tab.wave_cos)
    m_sin = dot_exact(jnp.concatenate(line, axis=0), tab.wave_sin)
    m_r = m_cos[:CHANS] - m_sin[CHANS:] + b_wide[0] + mean * c_wide[0]
    m_i = m_sin[:CHANS] + m_cos[CHANS:] + b_wide[1] + mean * c_wide[1]
    d = cdot(cdot(x, block_diag_c((m_r, m_i), tab)), x_parts)
    return -d[0], -d[1]


def correction_stage(d, square, e, kmap, tab):
    onehot = ((iota((WIDE, LANES), 0) >> 4) == kmap[...]).astype(F32).astype(BF16)
    keep = tab.row_block == tab.col_in

    def spread(panel):
        high, low = split(panel)

        def one(part):
            full = jnp.where(keep, tile_rows(part.astype(F32), CHANS), 0.0)
            return dot(full.astype(BF16), onehot)

        return one(high) + one(low)

    dr, di = spread(d[0]), spread(d[1])
    sr, si = square[e, 0].reshape(WIDE, LANES), square[e, 1].reshape(WIDE, LANES)
    re = jnp.sum(dr * sr - di * si, axis=0, keepdims=True)
    im = jnp.sum(dr * si + di * sr, axis=0, keepdims=True)
    return re, im


def coarse_out(x, tab, store):
    fold = (tab.col_block == tab.row_in)
    pick = (iota((WIDE, MOMS), 0) >> 4 == iota((WIDE, MOMS), 1)).astype(F32).astype(BF16)
    high = x.astype(BF16)
    rest = x - high.astype(F32)
    mid = rest.astype(BF16)
    low = (rest - mid.astype(F32)).astype(BF16)
    total = None
    for part in (low, mid, high):
        wide = jnp.broadcast_to(part.astype(F32)[:, None, :], (CHANS, CHANS, WIDE))
        wide = jnp.where(tab.same_in, wide.reshape(WIDE, WIDE), 0.0).astype(BF16)
        piece = dot(wide, pick)
        total = piece if total is None else total + piece
    store(total.reshape(CHANS, CHANS, MOMS))


def gathered_panel(tiles, at):
    top = jnp.concatenate([tiles[at], tiles[at + 1]], axis=1)
    low = jnp.concatenate([tiles[at + 2], tiles[at + 3]], axis=1)
    return jnp.concatenate([top, low], axis=0)


def offsets(outer, inner, torus):
    def hops(step):
        first = min(step[0], outer - step[0])
        return first + (min(step[1], inner - step[1]) if torus else 0.5 * (step[1] > 0))

    steps = [(a, b) for a in range(outer) for b in range(inner) if a or b]
    return sorted(steps, key=lambda step: (-hops(step), step))


class Group:
    def __init__(self, axis, inner, torus):
        self.axis, self.inner = axis, inner
        self.count = lax.axis_size(axis)
        self.outer = self.count // inner
        self.steps = offsets(self.outer, inner, torus)
        self.me = lax.axis_index(axis)

    def peer(self, step):
        first = lax.rem(self.me // self.inner + step[0], self.outer)
        return first * self.inner + lax.rem(lax.rem(self.me, self.inner) + step[1], self.inner)

    def greet(self, barrier):
        for step in self.steps:
            pl.semaphore_signal(
                barrier, inc=1, device_id={self.axis: self.peer(step)}, device_id_type=MESH
            )


class Exchange:
    def __init__(self, group, slots, send, recv):
        self.group, self.slots, self.send, self.recv = group, slots, send, recv

    def copy(self, src, at, number, peer):
        return pltpu.make_async_remote_copy(
            src_ref=src, dst_ref=self.slots.at[at], send_sem=self.send.at[number],
            recv_sem=self.recv.at[at], device_id={self.group.axis: peer}, device_id_type=MESH,
        )

    def start(self, source):
        for number, step in enumerate(self.group.steps):
            peer = self.group.peer(step)
            self.copy(source(peer), self.group.me, number, peer).start()

    def wait(self, source):
        for number, step in enumerate(self.group.steps[::-1]):
            peer = self.group.peer(step)
            self.copy(source(self.group.me), peer, number, peer).wait_recv()

    def drain(self, source):
        for number, step in enumerate(self.group.steps):
            peer = self.group.peer(step)
            self.copy(source(self.group.me), self.group.me, number, peer).wait_send()


def kernel(
    per_moment, n_ka, n_cfg,
    structure_hbm, medium_hbm, kmap_hbm, occupation_hbm, weight, shift_a_hbm, shift_b_hbm,
    coarse_hbm, slots, correction_hbm,
    structure, medium, kmap, occupation, shift_a, shift_b,
    spread, factor, inner, square, panels, rows_tab, shift_tab,
    row, own_rows, outgoing, first, part, total, block, coarse, correction,
    load_sem, out_sem, row_send, row_recv, first_send, first_recv, part_send, part_recv,
    total_send, total_recv, slot_send, slot_recv,
):
    pairs = (
        (kmap_hbm, kmap), (medium_hbm, medium), (structure_hbm, structure),
        (occupation_hbm, occupation), (shift_a_hbm, shift_a), (shift_b_hbm, shift_b),
    )
    loads = [
        pltpu.make_async_copy(source, to, load_sem.at[at]) for at, (source, to) in enumerate(pairs)
    ]
    for load in loads[:3]:
        load.start()
    barrier = pltpu.get_barrier_semaphore()
    by_ka, by_cfg = Group("ka", 4, True), Group("cfg", 2, False)
    by_ka.greet(barrier)
    by_cfg.greet(barrier)
    for load in loads[3:]:
        load.start()
    energies = range(ENERGIES)
    rows_x = Exchange(by_cfg, own_rows, row_send, row_recv)
    first_x = Exchange(by_cfg, first, first_send, first_recv)
    part_x = Exchange(by_ka, part, part_send, part_recv)
    total_x = Exchange(by_cfg, total, total_send, total_recv)
    slot_x = Exchange(by_ka, slots, slot_send, slot_recv)
    ka, cfg = lax.axis_index("ka"), lax.axis_index("cfg")

    def own_row(to):
        return row

    def own_sums(to):
        return outgoing.at[to]

    def own_part(to):
        return part.at[ka]

    def own_total(to):
        return total.at[cfg]

    def own_block(to):
        return block

    loads[0].wait()
    onehot = momentum_matrix(kmap)
    loads[1].wait()
    spread_medium(medium, kmap, spread)
    loads[2].wait()
    for e in energies:
        kpoint_factor(structure, spread, factor, e)
        kpoint_inner(structure, factor, inner, e)

        def write(at, value, e=e):
            outgoing[at, e] = value

        kpoint_sums(inner, onehot, e, write)
    for load in loads[3:]:
        load.wait()
    config_row(occupation, weight, row)
    pl.semaphore_wait(barrier, n_ka + n_cfg - 2)
    first_x.start(own_sums)
    first[cfg] = outgoing[cfg]
    rows_x.start(own_row)
    own_rows[cfg] = row[...]
    kpoint_squares(spread, factor, inner, square, 0)
    rows_x.wait(own_row)
    line = iota((8, LANES), 0)
    group = jnp.zeros((8, LANES), F32)
    for at in range(n_cfg):
        group = group + jnp.where(line == at, own_rows[at], 0.0)
    first_x.wait(own_sums)
    for e in energies:
        value = first[0, e]
        for at in range(1, n_cfg):
            value = value + first[at, e]
        part[ka, e] = value
    part[ka, ENERGIES] = group
    part_x.start(own_part)
    tab = Tables()
    y = [medium_panels(medium, tab, e) for e in energies]
    wide = [shift_panels(shift_a, shift_b, tab, e) for e in energies]
    y_b = [cdot(y[e], block_diag_c(wide[e][0], tab)) for e in energies]
    y_c = [cdot(y[e], block_diag_c(wide[e][1], tab)) for e in energies]
    y_all = [
        (block_diag_c(y[e], tab), block_diag_c(y_b[e], tab), block_diag_c(y_c[e], tab))
        for e in energies
    ]
    kpoint_squares(spread, factor, inner, square, 1)
    part_x.wait(own_part)
    for e in energies:
        value = part[0, e]
        for at in range(1, n_ka):
            value = value + part[at, e]
        total[cfg, e] = value
    total_x.start(own_total)
    configs = jnp.concatenate([part[at, ENERGIES] for at in range(n_ka)], axis=0)
    moment_tables(configs, tab, rows_tab, shift_tab)
    total_x.wait(own_total)
    found = []
    for e in energies:
        tiles = [total[at, e] for at in range(n_cfg)]
        sum_t = (gathered_panel(tiles, 0), gathered_panel(tiles, 4))
        found.append(coarse_panels(y[e], y_b[e], y_c[e], y_all[e], sum_t, tab, per_moment))
    rows = []
    for e in energies:
        lines = []
        for at, panel in enumerate(found[e]):
            panels[e, at, 0] = panel[0]
            panels[e, at, 1] = panel[1]
            lines.append(
                (panels[e, at, 0, pl.ds(ka, 1), :], panels[e, at, 1, pl.ds(ka, 1), :])
            )
        rows.append(first_rows(found[e], lines, tab, cfg * 2))
    t_all = [translated_c(rows[e][0][0])[1] for e in energies]
    tb_all = [translated_c(rows[e][1][0])[1] for e in energies]
    tc_all = [translated_c(rows[e][2][0]) for e in energies]
    averages = [
        rows_stage(
            rows[e][0][1], rows[e][1][1], rows[e][2][1], t_all[e], tb_all[e], tc_all[e][1], rows_tab
        )
        for e in energies
    ]
    for e in energies:
        out = jnp.zeros((8, LANES), F32)
        for c in range(2):
            for site in range(2):
                for side in range(2):
                    at = c * 4 + site * 2 + side
                    lanes = averages[e][c][
                        site * 8 : site * 8 + 8, side * LANES : side * LANES + LANES
                    ]
                    out = jnp.where(line == at, lanes, out)
        block[e] = out
    slot_x.start(own_block)
    own = pltpu.make_async_copy(block, slots.at[ka], out_sem.at[0])
    own.start()
    moments = [
        moment_stage(
            rows[e][1][0], rows[e][2][0], tc_all[e][0], tb_all[e], tc_all[e][1], found[e][0],
            block_diag_c(found[e][0], tab), wide[e][0], wide[e][1], shift_tab, tab,
        )
        for e in energies
    ]
    for e in energies:
        re, im = correction_stage(moments[e], square, e, kmap, tab)
        correction[e, 0:1, :] = re
        correction[e, 1:2, :] = im
        for c in range(2):

            def store(value, e=e, c=c):
                coarse[e, c] = value

            coarse_out(found[e][0][c], tab, store)
    leave = [
        pltpu.make_async_copy(coarse, coarse_hbm, out_sem.at[1]),
        pltpu.make_async_copy(correction, correction_hbm, out_sem.at[2]),
    ]
    for copy in leave:
        copy.start()
    slot_x.wait(own_block)
    rows_x.drain(own_row)
    first_x.drain(own_sums)
    part_x.drain(own_part)
    total_x.drain(own_total)
    slot_x.drain(own_block)
    own.wait()
    for copy in leave:
        copy.wait()


def output_kernel(coarse, slots, correction, coarse_to, average, correction_to):
    coarse_to[...] = coarse[...]
    correction_to[...] = correction[...]
    for e in range(ENERGIES):
        for at in range(slots.shape[0]):
            for c in range(2):
                for site in range(2):
                    for side in range(2):
                        of = c * 4 + site * 2 + side
                        to = site * CHANS + at
                        average[e, c, to : to + 1, side * LANES : side * LANES + LANES] = slots[
                            at, e, of : of + 1, :
                        ]


def shape(*dims):
    return jax.ShapeDtypeStruct(dims, F32)


VMEM_SPEC = pl.BlockSpec(memory_space=pltpu.VMEM)
SMEM_SPEC = pl.BlockSpec(memory_space=pltpu.SMEM)


def per_device(medium_t, structure, kmap, occupation, cfg_weight, shift_a, shift_b):
    n_ka, n_cfg = lax.axis_size("ka"), lax.axis_size("cfg")
    per_moment = kmap.shape[0] * n_ka * n_cfg // MOMS
    kmap = kmap.reshape(1, LANES)
    kdims = (ENERGIES, 2, CHANS, CHANS, LANES)
    dma = pltpu.SemaphoreType.DMA

    def vmem(*dims):
        return pltpu.VMEM(dims, F32)

    any_spec = pl.BlockSpec(memory_space=pl.ANY)
    shapes = (
        shape(ENERGIES, 2, CHANS, CHANS, MOMS),
        shape(ENERGIES, 2, 2 * CHANS, WIDE),
        shape(ENERGIES, 2, LANES),
    )
    results = pl.pallas_call(
        functools.partial(kernel, per_moment, n_ka, n_cfg),
        out_shape=(shapes[0], shape(n_ka, ENERGIES, 8, LANES), shapes[2]),
        in_specs=[any_spec] * 4 + [SMEM_SPEC] + [any_spec] * 2,
        out_specs=(any_spec,) * 3,
        scratch_shapes=[
            vmem(*kdims), vmem(ENERGIES, 2, CHANS, CHANS, MOMS),
            pltpu.VMEM((1, LANES), jnp.int32), pltpu.VMEM((1, SITES), jnp.int32),
            vmem(ENERGIES, 2, CHANS, CHANS), vmem(ENERGIES, 2, CHANS, CHANS),
            vmem(*kdims), vmem(*kdims), vmem(*kdims), vmem(*kdims),
            vmem(ENERGIES, 3, 2, CHANS, WIDE),
            vmem(SITES + 1, ALPHA, WIDE + LANES),
            vmem(2, WIDE, WIDE),
            vmem(8, LANES), vmem(n_cfg, 8, LANES),
            vmem(n_cfg, ENERGIES, 8, LANES), vmem(n_cfg, ENERGIES, 8, LANES),
            vmem(n_ka, ENERGIES + 1, 8, LANES),
            vmem(n_cfg, ENERGIES, 8, LANES),
            vmem(ENERGIES, 8, LANES),
            vmem(ENERGIES, 2, CHANS, CHANS, MOMS), vmem(ENERGIES, 2, LANES),
            dma((6,)), dma((3,)),
            dma((n_cfg,)), dma((n_cfg,)),
            dma((n_cfg,)), dma((n_cfg,)),
            dma((n_ka,)), dma((n_ka,)),
            dma((n_cfg,)), dma((n_cfg,)),
            dma((n_ka,)), dma((n_ka,)),
        ],
        compiler_params=pltpu.CompilerParams(
            collective_id=0, has_side_effects=True, vmem_limit_bytes=56 * 1024 * 1024
        ),
    )(structure, medium_t, kmap, occupation, cfg_weight, shift_a, shift_b)
    return pl.pallas_call(
        output_kernel,
        out_shape=shapes,
        in_specs=[VMEM_SPEC] * 3,
        out_specs=(VMEM_SPEC,) * 3,
    )(*results)


def solution(mesh):
    placed = (
        P(),
        P(None, None, None, None, ("ka", "cfg")),
        P(("ka", "cfg")),
        P(("ka", "cfg"), None),
        P(("ka", "cfg")),
        P(),
        P(),
    )
    return jax.shard_map(
        per_device,
        mesh=mesh,
        in_specs=placed,
        out_specs=(P(), P(None, None, "cfg", None), P(None, None, ("ka", "cfg"))),
        check_vma=False,
    )
```

```python
import functools

import jax
import jax.numpy as jnp
from jax import lax
from jax.experimental import pallas as pl
from jax.experimental.pallas import tpu as pltpu
from jax.sharding import PartitionSpec as P

MESH = pl.DeviceIdType.MESH
F32 = jnp.float32
BF16 = jnp.bfloat16
NN = (((1,), (0,)), ((), ()))
NT = (((1,), (1,)), ((), ()))

ENERGIES = 2
SITES = 16
CHANS = 16
MOMS = 16
WIDE = SITES * CHANS
LANES = 128
ALPHA = 24


def split(x):
    high = x.astype(BF16)
    return high, (x - high.astype(F32)).astype(BF16)


def dot(left, right, dims=NN):
    return lax.dot_general(left, right, dims, preferred_element_type=F32)


def dot_exact(x, right, dims=NN):
    high, low = split(x)
    rows = x.shape[0]
    both = dot(jnp.concatenate([high, low], axis=0), right, dims)
    return both[:rows] + both[rows:]


def dot3(x, right, dims=NN):
    high, low = split(x)
    rows = x.shape[0]
    both = dot(jnp.concatenate([high, low], axis=0), right[0], dims)
    return both[:rows] + (both[rows:] + dot(high, right[1], dims))


def cdot(x, right, dims=NN):
    rows = x[0].shape[0]
    both = jnp.concatenate([x[0], x[1]], axis=0)
    by_re = dot3(both, right[0], dims)
    by_im = dot3(both, right[1], dims)
    return by_re[:rows] - by_im[rows:], by_im[:rows] + by_re[rows:]


def csplit(x):
    return split(x[0]), split(x[1])


def iota(shape, axis):
    return lax.broadcasted_iota(jnp.int32, shape, axis)


def tile_rows(x, times):
    return jnp.concatenate([x] * times, axis=0)


def quarter_turns(mom, site):
    half = site >> 3
    x = 2 * ((site >> 2) & 1) + half
    y = 2 * ((site >> 1) & 1) + half
    z = 2 * (site & 1) + half
    return ((mom >> 2) * x + ((mom >> 1) & 1) * y + (mom & 1) * z) & 3


def cos_sin(turns):
    sign = (1 - (turns & 2)).astype(F32)
    odd = (turns & 1) == 1
    return jnp.where(odd, 0.0, sign), jnp.where(odd, sign, 0.0)


def site_sum(first, second):
    carry = (first & second) >> 3
    return (first ^ second) ^ (7 * carry)


class Tables:
    def __init__(self):
        rows, cols = iota((WIDE, WIDE), 0), iota((WIDE, WIDE), 1)
        self.row_block, self.col_block = rows >> 4, cols >> 4
        self.row_in, self.col_in = rows & 15, cols & 15
        self.same_block = self.row_block == self.col_block
        self.same_in = self.row_in == self.col_in
        self.cos, self.sin = cos_sin(quarter_turns(self.col_block, self.row_block))
        self.wave_cos = jnp.where(self.same_in, self.cos, 0.0).astype(BF16)
        self.wave_sin = jnp.where(self.same_in, self.sin, 0.0).astype(BF16)
        small_r, small_c = iota((SITES, WIDE), 0), iota((SITES, WIDE), 1)
        self.pick_in = (small_r == (small_c & 15)).astype(F32).astype(BF16)
        self.pick_block = (small_r == (small_c >> 4)).astype(F32).astype(BF16)


def block_diag(panel, tab):
    def spread(part):
        return jnp.where(tab.same_block, tile_rows(part.astype(F32), SITES), 0.0).astype(BF16)

    high, low = split(panel)
    return spread(high), spread(low)


def block_diag_c(panel, tab):
    return block_diag(panel[0], tab), block_diag(panel[1], tab)


HELD_ROWS = 8


def kpoint_mul(store, left, right):
    def body(step, carry):
        start = step * HELD_ROWS
        zero = jnp.zeros((CHANS, LANES), F32)
        p, q, t = [zero] * HELD_ROWS, [zero] * HELD_ROWS, [zero] * HELD_ROWS
        for b in range(CHANS):
            rr, ri = right[0, b], right[1, b]
            less, more = ri - rr, rr + ri
            for j in range(HELD_ROWS):
                lr = left[0, start + j, pl.ds(b, 1), :]
                li = left[1, start + j, pl.ds(b, 1), :]
                p[j] = p[j] + (lr + li) * rr
                q[j] = q[j] + lr * less
                t[j] = t[j] + li * more
        for j in range(HELD_ROWS):
            store(start + j, p[j] - t[j], p[j] + q[j])
        return carry

    lax.fori_loop(0, CHANS // HELD_ROWS, body, 0)


def spread_medium(medium, kmap, spread):
    onehot = (iota((MOMS, LANES), 0) == kmap[...]).astype(F32).astype(BF16)
    for e in range(ENERGIES):
        for c in range(2):
            flat = medium[e, c].reshape(WIDE, MOMS)
            spread[e, c] = dot_exact(flat, onehot).reshape(CHANS, CHANS, LANES)


def kpoint_factor(structure, spread, factor, e):
    f = factor.at[e]

    def put(a, re, im):
        f[0, a] = re
        f[1, a] = im

    kpoint_mul(put, spread.at[e], structure.at[e])


def kpoint_inner(structure, factor, inner, e):
    g, h = structure.at[e], inner.at[e]

    def put(a, re, im):
        h[0, a] = g[0, a] + re
        h[1, a] = g[1, a] + im

    kpoint_mul(put, g, factor.at[e])


def momentum_matrix(kmap):
    onehot = jnp.transpose(((iota((WIDE, LANES), 0) >> 4) == kmap[...]).astype(F32)).astype(BF16)
    return jnp.concatenate([onehot, onehot], axis=0)


def kpoint_sums(inner, onehot, e, write_tile):
    keep = (iota((WIDE, WIDE), 0) >> 4) == (iota((WIDE, WIDE), 1) & 15)
    for c in range(2):
        flat = inner[e, c].reshape(WIDE, LANES)
        parts = jnp.concatenate(split(flat), axis=1)
        by_mom = jnp.where(keep, dot(parts, onehot), 0.0)
        panel = jnp.sum(by_mom.reshape(CHANS, CHANS, WIDE), axis=0)
        for half in range(2):
            for side in range(2):
                write_tile(
                    c * 4 + half * 2 + side,
                    panel[half * 8 : half * 8 + 8, side * LANES : side * LANES + LANES],
                )


def kpoint_squares(spread, factor, tau, square, e):
    y, f, t, s = spread.at[e], factor.at[e], tau.at[e], square.at[e]

    def put_q(a, re, im):
        s[0, a] = f[0, a] + re
        s[1, a] = f[1, a] + im

    def put_t(a, re, im):
        t[0, a] = y[0, a] + re
        t[1, a] = y[1, a] + im

    def put_s(a, re, im):
        s[0, a] = re
        s[1, a] = im

    kpoint_mul(put_q, f, f)
    kpoint_mul(put_t, s, y)
    kpoint_mul(put_s, t, t)


def config_row(occupation, weight, row):
    lane = iota((8, LANES), 1)
    row[...] = jnp.where(lane == SITES, 1.0, 0.0) + jnp.where(
        lane == SITES + 1, weight[0], 0.0
    )
    row[:, 0:SITES] = jnp.broadcast_to(occupation[...].astype(F32), (8, SITES))


def moment_tables(configs, tab, rows_tab, shift_tab):
    turned = jnp.transpose(configs)
    count = turned[0:ALPHA]
    weight = turned[SITES + 1 : SITES + 2]
    weight = weight / jnp.sum(weight, axis=1, keepdims=True)
    live = iota((ALPHA, LANES), 0) <= SITES
    count = jnp.where(live, count, 0.0)
    weighted = count * weight
    flat = configs.astype(BF16)
    lane_r, lane_c = iota((LANES, WIDE), 0), iota((LANES, WIDE), 1)
    pick = (lane_r == (lane_c >> 4)).astype(F32).astype(BF16)
    wide = dot(flat, pick).astype(BF16)
    ones = jnp.ones((LANES, LANES), BF16)
    for s in range(SITES + 1):
        product = weighted * count[s : s + 1]
        rows_tab[s, :, 0:WIDE] = dot_exact(product, wide)
        rows_tab[s, :, WIDE : WIDE + LANES] = dot_exact(product, ones)
    r, c = iota((WIDE, LANES), 0), iota((WIDE, LANES), 1)
    move = (site_sum(r >> 4, r & 15) == c).astype(F32).astype(BF16)
    moved = dot(move, flat, NT)
    moved_b = moved.astype(BF16)
    own = dot(((r >> 4) == c).astype(F32).astype(BF16), flat, NT)
    base = moved * (weight * (1.0 / SITES))
    fold = (tab.row_in == tab.col_block).astype(F32).astype(BF16)
    for which, left in ((0, base), (1, base * own)):
        full = dot_exact(left, moved_b, NT)
        kept = jnp.where(tab.same_block, full, 0.0)
        small = jnp.sum(kept.reshape(SITES, SITES, WIDE), axis=0)
        lanes = dot_exact(small, fold)
        shift_tab[which] = jnp.broadcast_to(
            lanes[:, None, :], (SITES, CHANS, WIDE)
        ).reshape(WIDE, WIDE)


def medium_panels(medium, tab, e):
    out = []
    for c in range(2):
        flat = medium[e, c].reshape(WIDE, MOMS)
        pick = ((iota((MOMS, WIDE), 1) >> 4) == iota((MOMS, WIDE), 0)).astype(F32).astype(BF16)
        by_mom = jnp.where(tab.same_in, dot_exact(flat, pick), 0.0)
        out.append(jnp.sum(by_mom.reshape(CHANS, CHANS, WIDE), axis=1))
    return tuple(out)


def shift_panels(shift_a, shift_b, tab, e):
    def wide(x):
        return dot_exact(x, tab.pick_in)

    b = (wide(shift_b[e, 0]), wide(shift_b[e, 1]))
    c = (
        wide(shift_a[e, 0] - shift_b[e, 0]),
        wide(shift_a[e, 1] - shift_b[e, 1]),
    )
    return b, c


def left_panel(y, sum_t, tab, per_moment):
    left = cdot(y, block_diag_c(sum_t, tab), NT)
    return left[0] * (1.0 / per_moment), left[1] * (1.0 / per_moment)


def site_matrix(parts, tab):
    both = jnp.concatenate([parts[0][0], parts[0][1], parts[1][0], parts[1][1]], axis=0)

    def fold(full):
        return full[:WIDE] + full[WIDE : 2 * WIDE], full[2 * WIDE : 3 * WIDE] + full[3 * WIDE :]

    re_cos, im_cos = fold(dot(both, tab.wave_cos, NT))
    re_sin, im_sin = fold(dot(both, tab.wave_sin, NT))
    scale = 1.0 / SITES
    return csplit(((re_cos + im_sin) * scale, (im_cos - re_sin) * scale))


def site_phases(site0):
    mom = iota((16, WIDE), 1) >> 4
    return cos_sin(quarter_turns(mom, site0 + (iota((16, WIDE), 0) >> 3)))


def more_rows(known, left, line, phases, matrices):
    cos, sin = phases
    lr, li = jnp.broadcast_to(line[0], (16, WIDE)), jnp.broadcast_to(line[1], (16, WIDE))
    both = (
        jnp.concatenate([left[0], lr * cos - li * sin], axis=0),
        jnp.concatenate([left[1], lr * sin + li * cos], axis=0),
    )
    out = []
    for (top, own), matrix in zip(known, matrices):
        step = cdot(both, matrix)
        out.append(
            (
                (top[0] + step[0][:16], top[1] + step[1][:16]),
                (own[0] + step[0][16:], own[1] + step[1][16:]),
            )
        )
    return out


def first_rows(panels, lines, tab, phases):
    cos, sin = phases
    left_r, left_i = [], []
    for panel, line in zip(panels, lines):
        lr, li = jnp.broadcast_to(line[0], (16, WIDE)), jnp.broadcast_to(line[1], (16, WIDE))
        left_r += [panel[0], lr * cos - li * sin]
        left_i += [panel[1], lr * sin + li * cos]
    rows = 32 * len(panels)
    both = jnp.concatenate(left_r + left_i, axis=0) * (1.0 / SITES)
    by_cos = dot_exact(both, tab.wave_cos, NT)
    by_sin = dot_exact(both, tab.wave_sin, NT)
    real = by_cos[:rows] + by_sin[rows:]
    imag = by_cos[rows:] - by_sin[:rows]
    out = []
    for at in range(0, rows, 32):
        out.append(
            (
                (real[at : at + 16], imag[at : at + 16]),
                (real[at + 16 : at + 32], imag[at + 16 : at + 32]),
            )
        )
    return out


def swap_blocks(x, bit):
    step = 16 * bit
    up = pltpu.roll(x, LANES - step, axis=1)
    if bit == 4:
        return up
    down = pltpu.roll(x, step, axis=1)
    high = ((iota(x.shape, 1) >> 4) & bit) != 0
    return jnp.where(high, down, up)


def all_swaps(x):
    out = {0: x}
    out[4] = swap_blocks(x, 4)
    for at in (0, 4):
        out[at | 2] = swap_blocks(out[at], 2)
    for at in (0, 2, 4, 6):
        out[at | 1] = swap_blocks(out[at], 1)
    return out


def translated(panel):
    low = all_swaps(panel[:, 0:LANES])
    top = all_swaps(panel[:, LANES:WIDE])

    def whole(a, b):
        rows = [jnp.concatenate([a[q], b[q]], axis=1) for q in range(8)]
        rows += [jnp.concatenate([b[q ^ 7], a[q]], axis=1) for q in range(8)]
        return jnp.concatenate(rows, axis=0)

    low_parts = {q: split(v) for q, v in low.items()}
    top_parts = {q: split(v) for q, v in top.items()}
    parts = tuple(
        whole({q: v[p] for q, v in low_parts.items()}, {q: v[p] for q, v in top_parts.items()})
        for p in range(2)
    )
    return whole(low, top), parts


def translated_c(panel):
    real, imag = translated(panel[0]), translated(panel[1])
    return (real[0], imag[0]), (real[1], imag[1])


def rows_stage(start, with_b, with_c, t_parts, tb_parts, tc_parts, rows_tab):
    row = iota((ALPHA, WIDE), 0)
    block = iota((ALPHA, WIDE), 1) >> 4

    def opened(c):
        out = []
        for at in (0, 8):
            ub = jnp.broadcast_to(with_b[c][at : at + 1], (ALPHA, WIDE))
            uc = jnp.broadcast_to(with_c[c][at : at + 1], (ALPHA, WIDE))
            out.append(jnp.where(row == block, uc, jnp.where(row == SITES, ub, 0.0)))
        return jnp.concatenate(out, axis=0)

    begin = (opened(0), opened(1))
    hop_b = cdot(begin, tb_parts)
    hop_c = cdot(begin, tc_parts)
    inner = []
    for c in range(2):
        out = []
        for site in range(2):
            g = jnp.zeros((ALPHA, WIDE), F32)
            for s in range(SITES + 1):
                at = site * ALPHA + s
                pair = rows_tab[s, :, WIDE : WIDE + LANES]
                g = g + jnp.concatenate([pair, pair], axis=1) * hop_b[c][at : at + 1]
                g = g + rows_tab[s, :, 0:WIDE] * hop_c[c][at : at + 1]
            out.append(g)
        inner.append(jnp.concatenate(out, axis=0))
    mean = rows_tab[SITES, SITES : SITES + 1, 0:WIDE]

    def eight(parts):
        return jnp.concatenate([jnp.broadcast_to(p, (8, WIDE)) for p in parts], axis=0)

    ends = tuple(
        eight([inner[c][site * ALPHA + SITES : site * ALPHA + SITES + 1] for site in range(2)])
        for c in range(2)
    )
    by_b = cdot(ends, tb_parts)
    by_c = cdot(tuple(inner), tc_parts)
    z = []
    for c in range(2):
        picked = []
        for site in range(2):
            lines = by_c[c][site * ALPHA : site * ALPHA + ALPHA]
            picked.append(jnp.sum(jnp.where(row == block, lines, 0.0), axis=0, keepdims=True))
        z.append(with_b[c] + with_c[c] * mean - ends[c] + by_b[c] + eight(picked))
    last = cdot(tuple(z), t_parts)
    return start[0] - last[0], start[1] - last[1]


def moment_stage(top_b, top_c, tc_full, tb_parts, tc_parts, x, x_parts, b_wide, c_wide, shift_tab, tab):
    def head(wide):
        return wide[0][:, 0:CHANS], wide[1][:, 0:CHANS]

    b_in, c_in = head(b_wide), head(c_wide)
    small = (
        jnp.concatenate([b_in[0], c_in[0]], axis=0),
        jnp.concatenate([b_in[1], c_in[1]], axis=0),
    )
    lead_b = cdot(small, csplit(top_b))
    lead_c = cdot(small, csplit(top_c))
    bb, cb = [v[0:CHANS] for v in lead_b], [v[CHANS:] for v in lead_b]
    bc, cc = [v[0:CHANS] for v in lead_c], [v[CHANS:] for v in lead_c]
    two = shift_tab[1, 0:1, :]
    mean = shift_tab[1, 0:1, 0:1]
    zero = [bb[c] + mean * (bc[c] + cb[c]) + two * cc[c] for c in range(2)]
    by_b = cdot(tuple(zero), tb_parts)
    by_c = cdot(tuple(jnp.concatenate([bb[c], cb[c]], axis=0) for c in range(2)), tc_parts)

    def scaled(which):
        return split(tc_full[0] * shift_tab[which]), split(tc_full[1] * shift_tab[which])

    pair = cdot(tuple(bc), scaled(0))
    triple = cdot(tuple(cc), scaled(1))
    line = []
    for c in range(2):
        third = by_b[c] + mean * by_c[c][0:CHANS] + two * by_c[c][CHANS:] + pair[c] + triple[c]
        line.append(third - (bb[c] + mean * (cb[c] + bc[c]) + two * cc[c]))
    m_cos = dot_exact(jnp.concatenate(line, axis=0), tab.wave_cos)
    m_sin = dot_exact(jnp.concatenate(line, axis=0), tab.wave_sin)
    m_r = m_cos[:CHANS] - m_sin[CHANS:] + b_wide[0] + mean * c_wide[0]
    m_i = m_sin[:CHANS] + m_cos[CHANS:] + b_wide[1] + mean * c_wide[1]
    d = cdot(cdot(x, block_diag_c((m_r, m_i), tab)), x_parts)
    return -d[0], -d[1]


def correction_stage(d, square, e, kmap, tab):
    onehot = ((iota((WIDE, LANES), 0) >> 4) == kmap[...]).astype(F32).astype(BF16)
    keep = tab.row_block == tab.col_in

    def spread(panel):
        high, low = split(panel)

        def one(part):
            full = jnp.where(keep, tile_rows(part.astype(F32), CHANS), 0.0)
            return dot(full.astype(BF16), onehot)

        return one(high) + one(low)

    dr, di = spread(d[0]), spread(d[1])
    sr, si = square[e, 0].reshape(WIDE, LANES), square[e, 1].reshape(WIDE, LANES)
    re = jnp.sum(dr * sr - di * si, axis=0, keepdims=True)
    im = jnp.sum(dr * si + di * sr, axis=0, keepdims=True)
    return re, im


def coarse_out(x, tab, store):
    fold = (tab.col_block == tab.row_in)
    pick = (iota((WIDE, MOMS), 0) >> 4 == iota((WIDE, MOMS), 1)).astype(F32).astype(BF16)
    high = x.astype(BF16)
    rest = x - high.astype(F32)
    mid = rest.astype(BF16)
    low = (rest - mid.astype(F32)).astype(BF16)
    total = None
    for part in (low, mid, high):
        wide = jnp.broadcast_to(part.astype(F32)[:, None, :], (CHANS, CHANS, WIDE))
        wide = jnp.where(tab.same_in, wide.reshape(WIDE, WIDE), 0.0).astype(BF16)
        piece = dot(wide, pick)
        total = piece if total is None else total + piece
    store(total.reshape(CHANS, CHANS, MOMS))


def gathered_panel(tiles, at):
    top = jnp.concatenate([tiles[at], tiles[at + 1]], axis=1)
    low = jnp.concatenate([tiles[at + 2], tiles[at + 3]], axis=1)
    return jnp.concatenate([top, low], axis=0)


def offsets(outer, inner, torus):
    def hops(step):
        first = min(step[0], outer - step[0])
        return first + (min(step[1], inner - step[1]) if torus else 0.5 * (step[1] > 0))

    steps = [(a, b) for a in range(outer) for b in range(inner) if a or b]
    return sorted(steps, key=lambda step: (-hops(step), step))


class Group:
    def __init__(self, axis, inner, torus):
        self.axis, self.inner = axis, inner
        self.count = lax.axis_size(axis)
        self.outer = self.count // inner
        self.steps = offsets(self.outer, inner, torus)
        self.me = lax.axis_index(axis)

    def peer(self, step):
        first = lax.rem(self.me // self.inner + step[0], self.outer)
        return first * self.inner + lax.rem(lax.rem(self.me, self.inner) + step[1], self.inner)

    def greet(self, barrier):
        for step in self.steps:
            pl.semaphore_signal(
                barrier, inc=1, device_id={self.axis: self.peer(step)}, device_id_type=MESH
            )


class Exchange:
    def __init__(self, group, slots, send, recv):
        self.group, self.slots, self.send, self.recv = group, slots, send, recv

    def copy(self, src, at, number, peer):
        return pltpu.make_async_remote_copy(
            src_ref=src, dst_ref=self.slots.at[at], send_sem=self.send.at[number],
            recv_sem=self.recv.at[at], device_id={self.group.axis: peer}, device_id_type=MESH,
        )

    def start(self, source):
        for number, step in enumerate(self.group.steps):
            peer = self.group.peer(step)
            self.copy(source(peer), self.group.me, number, peer).start()

    def wait(self, source):
        for number, step in enumerate(self.group.steps[::-1]):
            peer = self.group.peer(step)
            self.copy(source(self.group.me), peer, number, peer).wait_recv()

    def drain(self, source):
        for number, step in enumerate(self.group.steps):
            peer = self.group.peer(step)
            self.copy(source(self.group.me), self.group.me, number, peer).wait_send()


def kernel(
    per_moment, n_ka, n_cfg,
    structure_hbm, medium_hbm, kmap_hbm, occupation_hbm, weight, shift_a_hbm, shift_b_hbm,
    coarse_hbm, slots, correction_hbm,
    structure, medium, kmap, occupation, shift_a, shift_b,
    spread, factor, inner, square, panels, rows_tab, shift_tab,
    row, own_rows, outgoing, first, part, total, block, coarse, correction,
    load_sem, out_sem, row_send, row_recv, first_send, first_recv, part_send, part_recv,
    total_send, total_recv, slot_send, slot_recv,
):
    pairs = (
        (kmap_hbm, kmap), (medium_hbm, medium), (structure_hbm, structure),
        (occupation_hbm, occupation), (shift_a_hbm, shift_a), (shift_b_hbm, shift_b),
    )
    loads = [
        pltpu.make_async_copy(source, to, load_sem.at[at]) for at, (source, to) in enumerate(pairs)
    ]
    for load in loads[:3]:
        load.start()
    barrier = pltpu.get_barrier_semaphore()
    by_ka, by_cfg = Group("ka", 4, True), Group("cfg", 2, False)
    by_ka.greet(barrier)
    by_cfg.greet(barrier)
    for load in loads[3:]:
        load.start()
    energies = range(ENERGIES)
    rows_x = Exchange(by_cfg, own_rows, row_send, row_recv)
    first_x = Exchange(by_cfg, first, first_send, first_recv)
    part_x = Exchange(by_ka, part, part_send, part_recv)
    total_x = Exchange(by_cfg, total, total_send, total_recv)
    slot_x = Exchange(by_ka, slots, slot_send, slot_recv)
    ka, cfg = lax.axis_index("ka"), lax.axis_index("cfg")

    def own_row(to):
        return row

    def own_sums(to):
        return outgoing.at[to]

    def own_part(to):
        return part.at[ka]

    def own_total(to):
        return total.at[cfg]

    def own_block(to):
        return block

    loads[0].wait()
    onehot = momentum_matrix(kmap)
    loads[1].wait()
    spread_medium(medium, kmap, spread)
    loads[2].wait()
    for e in energies:
        kpoint_factor(structure, spread, factor, e)
        kpoint_inner(structure, factor, inner, e)

        def write(at, value, e=e):
            outgoing[at, e] = value

        kpoint_sums(inner, onehot, e, write)
    for load in loads[3:]:
        load.wait()
    config_row(occupation, weight, row)
    pl.semaphore_wait(barrier, n_ka + n_cfg - 2)
    first_x.start(own_sums)
    first[cfg] = outgoing[cfg]
    rows_x.start(own_row)
    own_rows[cfg] = row[...]
    kpoint_squares(spread, factor, inner, square, 0)
    rows_x.wait(own_row)
    line = iota((8, LANES), 0)
    group = jnp.zeros((8, LANES), F32)
    for at in range(n_cfg):
        group = group + jnp.where(line == at, own_rows[at], 0.0)
    first_x.wait(own_sums)
    for e in energies:
        value = first[0, e]
        for at in range(1, n_cfg):
            value = value + first[at, e]
        part[ka, e] = value
    part[ka, ENERGIES] = group
    part_x.start(own_part)
    tab = Tables()
    y = [medium_panels(medium, tab, e) for e in energies]
    wide = [shift_panels(shift_a, shift_b, tab, e) for e in energies]
    y_b = [cdot(y[e], block_diag_c(wide[e][0], tab)) for e in energies]
    y_c = [cdot(y[e], block_diag_c(wide[e][1], tab)) for e in energies]
    y_all = [
        (block_diag_c(y[e], tab), block_diag_c(y_b[e], tab), block_diag_c(y_c[e], tab))
        for e in energies
    ]
    kpoint_squares(spread, factor, inner, square, 1)
    phases = site_phases(cfg * 2)
    known = []
    for e in energies:
        lines = []
        for at, panel in enumerate((y[e], y_b[e], y_c[e])):
            panels[e, at, 0] = panel[0]
            panels[e, at, 1] = panel[1]
            lines.append(
                (panels[e, at, 0, pl.ds(ka, 1), :], panels[e, at, 1, pl.ds(ka, 1), :])
            )
        known.append(first_rows((y[e], y_b[e], y_c[e]), lines, tab, phases))
    matrices = [[site_matrix(parts, tab) for parts in y_all[0]]]
    part_x.wait(own_part)
    for e in energies:
        value = part[0, e]
        for at in range(1, n_ka):
            value = value + part[at, e]
        total[cfg, e] = value
    total_x.start(own_total)
    configs = jnp.concatenate([part[at, ENERGIES] for at in range(n_ka)], axis=0)
    moment_tables(configs, tab, rows_tab, shift_tab)
    matrices.append([site_matrix(parts, tab) for parts in y_all[1]])
    total_x.wait(own_total)
    lefts = []
    for e in energies:
        tiles = [total[at, e] for at in range(n_cfg)]
        sum_t = (gathered_panel(tiles, 0), gathered_panel(tiles, 4))
        lefts.append(left_panel(y[e], sum_t, tab, per_moment))
    rows = []
    for e in energies:
        panels[e, 0, 0] = lefts[e][0]
        panels[e, 0, 1] = lefts[e][1]
        line_e = (panels[e, 0, 0, pl.ds(ka, 1), :], panels[e, 0, 1, pl.ds(ka, 1), :])
        rows.append(more_rows(known[e], lefts[e], line_e, phases, matrices[e]))
    t_all = [translated_c(rows[e][0][0])[1] for e in energies]
    tb_all = [translated_c(rows[e][1][0])[1] for e in energies]
    tc_all = [translated_c(rows[e][2][0]) for e in energies]
    averages = [
        rows_stage(
            rows[e][0][1], rows[e][1][1], rows[e][2][1], t_all[e], tb_all[e], tc_all[e][1], rows_tab
        )
        for e in energies
    ]
    for e in energies:
        out = jnp.zeros((8, LANES), F32)
        for c in range(2):
            for site in range(2):
                for side in range(2):
                    at = c * 4 + site * 2 + side
                    lanes = averages[e][c][
                        site * 8 : site * 8 + 8, side * LANES : side * LANES + LANES
                    ]
                    out = jnp.where(line == at, lanes, out)
        block[e] = out
    slot_x.start(own_block)
    own = pltpu.make_async_copy(block, slots.at[ka], out_sem.at[0])
    own.start()
    found = []
    for e in energies:
        step = cdot(lefts[e], y_all[e][0])
        found.append((y[e][0] + step[0], y[e][1] + step[1]))
    moments = [
        moment_stage(
            rows[e][1][0], rows[e][2][0], tc_all[e][0], tb_all[e], tc_all[e][1], found[e],
            block_diag_c(found[e], tab), wide[e][0], wide[e][1], shift_tab, tab,
        )
        for e in energies
    ]
    for e in energies:
        re, im = correction_stage(moments[e], square, e, kmap, tab)
        correction[e, 0:1, :] = re
        correction[e, 1:2, :] = im
        for c in range(2):

            def store(value, e=e, c=c):
                coarse[e, c] = value

            coarse_out(found[e][c], tab, store)
    leave = [
        pltpu.make_async_copy(coarse, coarse_hbm, out_sem.at[1]),
        pltpu.make_async_copy(correction, correction_hbm, out_sem.at[2]),
    ]
    for copy in leave:
        copy.start()
    slot_x.wait(own_block)
    rows_x.drain(own_row)
    first_x.drain(own_sums)
    part_x.drain(own_part)
    total_x.drain(own_total)
    slot_x.drain(own_block)
    own.wait()
    for copy in leave:
        copy.wait()


def output_kernel(coarse, slots, correction, coarse_to, average, correction_to):
    coarse_to[...] = coarse[...]
    correction_to[...] = correction[...]
    for e in range(ENERGIES):
        for at in range(slots.shape[0]):
            for c in range(2):
                for site in range(2):
                    for side in range(2):
                        of = c * 4 + site * 2 + side
                        to = site * CHANS + at
                        average[e, c, to : to + 1, side * LANES : side * LANES + LANES] = slots[
                            at, e, of : of + 1, :
                        ]


def shape(*dims):
    return jax.ShapeDtypeStruct(dims, F32)


VMEM_SPEC = pl.BlockSpec(memory_space=pltpu.VMEM)
SMEM_SPEC = pl.BlockSpec(memory_space=pltpu.SMEM)


def per_device(medium_t, structure, kmap, occupation, cfg_weight, shift_a, shift_b):
    n_ka, n_cfg = lax.axis_size("ka"), lax.axis_size("cfg")
    per_moment = kmap.shape[0] * n_ka * n_cfg // MOMS
    kmap = kmap.reshape(1, LANES)
    kdims = (ENERGIES, 2, CHANS, CHANS, LANES)
    dma = pltpu.SemaphoreType.DMA

    def vmem(*dims):
        return pltpu.VMEM(dims, F32)

    any_spec = pl.BlockSpec(memory_space=pl.ANY)
    shapes = (
        shape(ENERGIES, 2, CHANS, CHANS, MOMS),
        shape(ENERGIES, 2, 2 * CHANS, WIDE),
        shape(ENERGIES, 2, LANES),
    )
    results = pl.pallas_call(
        functools.partial(kernel, per_moment, n_ka, n_cfg),
        out_shape=(shapes[0], shape(n_ka, ENERGIES, 8, LANES), shapes[2]),
        in_specs=[any_spec] * 4 + [SMEM_SPEC] + [any_spec] * 2,
        out_specs=(any_spec,) * 3,
        scratch_shapes=[
            vmem(*kdims), vmem(ENERGIES, 2, CHANS, CHANS, MOMS),
            pltpu.VMEM((1, LANES), jnp.int32), pltpu.VMEM((1, SITES), jnp.int32),
            vmem(ENERGIES, 2, CHANS, CHANS), vmem(ENERGIES, 2, CHANS, CHANS),
            vmem(*kdims), vmem(*kdims), vmem(*kdims), vmem(*kdims),
            vmem(ENERGIES, 3, 2, CHANS, WIDE),
            vmem(SITES + 1, ALPHA, WIDE + LANES),
            vmem(2, WIDE, WIDE),
            vmem(8, LANES), vmem(n_cfg, 8, LANES),
            vmem(n_cfg, ENERGIES, 8, LANES), vmem(n_cfg, ENERGIES, 8, LANES),
            vmem(n_ka, ENERGIES + 1, 8, LANES),
            vmem(n_cfg, ENERGIES, 8, LANES),
            vmem(ENERGIES, 8, LANES),
            vmem(ENERGIES, 2, CHANS, CHANS, MOMS), vmem(ENERGIES, 2, LANES),
            dma((6,)), dma((3,)),
            dma((n_cfg,)), dma((n_cfg,)),
            dma((n_cfg,)), dma((n_cfg,)),
            dma((n_ka,)), dma((n_ka,)),
            dma((n_cfg,)), dma((n_cfg,)),
            dma((n_ka,)), dma((n_ka,)),
        ],
        compiler_params=pltpu.CompilerParams(
            collective_id=0, has_side_effects=True, vmem_limit_bytes=56 * 1024 * 1024
        ),
    )(structure, medium_t, kmap, occupation, cfg_weight, shift_a, shift_b)
    return pl.pallas_call(
        output_kernel,
        out_shape=shapes,
        in_specs=[VMEM_SPEC] * 3,
        out_specs=(VMEM_SPEC,) * 3,
    )(*results)


def solution(mesh):
    placed = (
        P(),
        P(None, None, None, None, ("ka", "cfg")),
        P(("ka", "cfg")),
        P(("ka", "cfg"), None),
        P(("ka", "cfg")),
        P(),
        P(),
    )
    return jax.shard_map(
        per_device,
        mesh=mesh,
        in_specs=placed,
        out_specs=(P(), P(None, None, "cfg", None), P(None, None, ("ka", "cfg"))),
        check_vma=False,
    )
```

```python
import functools

import jax
import jax.numpy as jnp
from jax import lax
from jax.experimental import pallas as pl
from jax.experimental.pallas import tpu as pltpu
from jax.sharding import PartitionSpec as P

MESH = pl.DeviceIdType.MESH
F32 = jnp.float32
BF16 = jnp.bfloat16
NN = (((1,), (0,)), ((), ()))
NT = (((1,), (1,)), ((), ()))

ENERGIES = 2
SITES = 16
CHANS = 16
MOMS = 16
WIDE = SITES * CHANS
LANES = 128
ALPHA = 24


def split(x):
    high = x.astype(BF16)
    return high, (x - high.astype(F32)).astype(BF16)


def dot(left, right, dims=NN):
    return lax.dot_general(left, right, dims, preferred_element_type=F32)


def dot_exact(x, right, dims=NN):
    high, low = split(x)
    rows = x.shape[0]
    both = dot(jnp.concatenate([high, low], axis=0), right, dims)
    return both[:rows] + both[rows:]


def dot3(x, right, dims=NN):
    high, low = split(x)
    rows = x.shape[0]
    both = dot(jnp.concatenate([high, low], axis=0), right[0], dims)
    return both[:rows] + (both[rows:] + dot(high, right[1], dims))


def cdot(x, right, dims=NN):
    rows = x[0].shape[0]
    both = jnp.concatenate([x[0], x[1]], axis=0)
    by_re = dot3(both, right[0], dims)
    by_im = dot3(both, right[1], dims)
    return by_re[:rows] - by_im[rows:], by_im[:rows] + by_re[rows:]


def csplit(x):
    return split(x[0]), split(x[1])


def iota(shape, axis):
    return lax.broadcasted_iota(jnp.int32, shape, axis)


def tile_rows(x, times):
    return jnp.concatenate([x] * times, axis=0)


def quarter_turns(mom, site):
    half = site >> 3
    x = 2 * ((site >> 2) & 1) + half
    y = 2 * ((site >> 1) & 1) + half
    z = 2 * (site & 1) + half
    return ((mom >> 2) * x + ((mom >> 1) & 1) * y + (mom & 1) * z) & 3


def cos_sin(turns):
    sign = (1 - (turns & 2)).astype(F32)
    odd = (turns & 1) == 1
    return jnp.where(odd, 0.0, sign), jnp.where(odd, sign, 0.0)


def site_sum(first, second):
    carry = (first & second) >> 3
    return (first ^ second) ^ (7 * carry)


class Tables:
    def __init__(self):
        rows, cols = iota((WIDE, WIDE), 0), iota((WIDE, WIDE), 1)
        self.row_block, self.col_block = rows >> 4, cols >> 4
        self.row_in, self.col_in = rows & 15, cols & 15
        self.same_block = self.row_block == self.col_block
        self.same_in = self.row_in == self.col_in
        self.cos, self.sin = cos_sin(quarter_turns(self.col_block, self.row_block))
        self.wave_cos = jnp.where(self.same_in, self.cos, 0.0).astype(BF16)
        self.wave_sin = jnp.where(self.same_in, self.sin, 0.0).astype(BF16)
        small_r, small_c = iota((SITES, WIDE), 0), iota((SITES, WIDE), 1)
        self.pick_in = (small_r == (small_c & 15)).astype(F32).astype(BF16)
        self.pick_block = (small_r == (small_c >> 4)).astype(F32).astype(BF16)


def block_diag(panel, tab):
    def spread(part):
        return jnp.where(tab.same_block, tile_rows(part.astype(F32), SITES), 0.0).astype(BF16)

    high, low = split(panel)
    return spread(high), spread(low)


def block_diag_c(panel, tab):
    return block_diag(panel[0], tab), block_diag(panel[1], tab)


HELD_ROWS = 8


def kpoint_mul(store, left, right):
    def body(step, carry):
        start = step * HELD_ROWS
        zero = jnp.zeros((CHANS, LANES), F32)
        p, q, t = [zero] * HELD_ROWS, [zero] * HELD_ROWS, [zero] * HELD_ROWS
        for b in range(CHANS):
            rr, ri = right[0, b], right[1, b]
            less, more = ri - rr, rr + ri
            for j in range(HELD_ROWS):
                lr = left[0, start + j, pl.ds(b, 1), :]
                li = left[1, start + j, pl.ds(b, 1), :]
                p[j] = p[j] + (lr + li) * rr
                q[j] = q[j] + lr * less
                t[j] = t[j] + li * more
        for j in range(HELD_ROWS):
            store(start + j, p[j] - t[j], p[j] + q[j])
        return carry

    lax.fori_loop(0, CHANS // HELD_ROWS, body, 0)


def spread_medium(medium, kmap, spread):
    onehot = (iota((MOMS, LANES), 0) == kmap[...]).astype(F32).astype(BF16)
    for e in range(ENERGIES):
        for c in range(2):
            flat = medium[e, c].reshape(WIDE, MOMS)
            spread[e, c] = dot_exact(flat, onehot).reshape(CHANS, CHANS, LANES)


def kpoint_factor(structure, spread, factor, e):
    f = factor.at[e]

    def put(a, re, im):
        f[0, a] = re
        f[1, a] = im

    kpoint_mul(put, spread.at[e], structure.at[e])


def kpoint_inner(structure, factor, inner, e):
    g, h = structure.at[e], inner.at[e]

    def put(a, re, im):
        h[0, a] = g[0, a] + re
        h[1, a] = g[1, a] + im

    kpoint_mul(put, g, factor.at[e])


def momentum_matrix(kmap):
    onehot = jnp.transpose(((iota((WIDE, LANES), 0) >> 4) == kmap[...]).astype(F32)).astype(BF16)
    return jnp.concatenate([onehot, onehot], axis=0)


def kpoint_sums(inner, onehot, e, write_tile):
    keep = (iota((WIDE, WIDE), 0) >> 4) == (iota((WIDE, WIDE), 1) & 15)
    for c in range(2):
        flat = inner[e, c].reshape(WIDE, LANES)
        parts = jnp.concatenate(split(flat), axis=1)
        by_mom = jnp.where(keep, dot(parts, onehot), 0.0)
        panel = jnp.sum(by_mom.reshape(CHANS, CHANS, WIDE), axis=0)
        for half in range(2):
            for side in range(2):
                write_tile(
                    c * 4 + half * 2 + side,
                    panel[half * 8 : half * 8 + 8, side * LANES : side * LANES + LANES],
                )


def kpoint_tau(spread, factor, tau, work, e):
    y, f, t, s = spread.at[e], factor.at[e], tau.at[e], work.at[e]

    def put_q(a, re, im):
        s[0, a] = f[0, a] + re
        s[1, a] = f[1, a] + im

    def put_t(a, re, im):
        t[0, a] = y[0, a] + re
        t[1, a] = y[1, a] + im

    kpoint_mul(put_q, f, f)
    kpoint_mul(put_t, s, y)


def kpoint_square(tau, square, e):
    t, s = tau.at[e], square.at[e]

    def put(a, re, im):
        s[0, a] = re
        s[1, a] = im

    kpoint_mul(put, t, t)


def config_row(occupation, weight, row):
    lane = iota((8, LANES), 1)
    row[...] = jnp.where(lane == SITES, 1.0, 0.0) + jnp.where(
        lane == SITES + 1, weight[0], 0.0
    )
    row[:, 0:SITES] = jnp.broadcast_to(occupation[...].astype(F32), (8, SITES))


def moment_tables(configs, tab, rows_tab, shift_tab):
    turned = jnp.transpose(configs)
    count = turned[0:ALPHA]
    weight = turned[SITES + 1 : SITES + 2]
    weight = weight / jnp.sum(weight, axis=1, keepdims=True)
    live = iota((ALPHA, LANES), 0) <= SITES
    count = jnp.where(live, count, 0.0)
    weighted = count * weight
    flat = configs.astype(BF16)
    lane_r, lane_c = iota((LANES, WIDE), 0), iota((LANES, WIDE), 1)
    pick = (lane_r == (lane_c >> 4)).astype(F32).astype(BF16)
    wide = dot(flat, pick).astype(BF16)
    ones = jnp.ones((LANES, LANES), BF16)
    for s in range(SITES + 1):
        product = weighted * count[s : s + 1]
        rows_tab[s, :, 0:WIDE] = dot_exact(product, wide)
        rows_tab[s, :, WIDE : WIDE + LANES] = dot_exact(product, ones)
    r, c = iota((WIDE, LANES), 0), iota((WIDE, LANES), 1)
    move = (site_sum(r >> 4, r & 15) == c).astype(F32).astype(BF16)
    moved = dot(move, flat, NT)
    moved_b = moved.astype(BF16)
    own = dot(((r >> 4) == c).astype(F32).astype(BF16), flat, NT)
    base = moved * (weight * (1.0 / SITES))
    fold = (tab.row_in == tab.col_block).astype(F32).astype(BF16)
    for which, left in ((0, base), (1, base * own)):
        full = dot_exact(left, moved_b, NT)
        kept = jnp.where(tab.same_block, full, 0.0)
        small = jnp.sum(kept.reshape(SITES, SITES, WIDE), axis=0)
        lanes = dot_exact(small, fold)
        shift_tab[which] = jnp.broadcast_to(
            lanes[:, None, :], (SITES, CHANS, WIDE)
        ).reshape(WIDE, WIDE)


def medium_panels(medium, tab, e):
    out = []
    for c in range(2):
        flat = medium[e, c].reshape(WIDE, MOMS)
        pick = ((iota((MOMS, WIDE), 1) >> 4) == iota((MOMS, WIDE), 0)).astype(F32).astype(BF16)
        by_mom = jnp.where(tab.same_in, dot_exact(flat, pick), 0.0)
        out.append(jnp.sum(by_mom.reshape(CHANS, CHANS, WIDE), axis=1))
    return tuple(out)


def shift_panels(shift_a, shift_b, tab, e):
    def wide(x):
        return dot_exact(x, tab.pick_in)

    b = (wide(shift_b[e, 0]), wide(shift_b[e, 1]))
    c = (
        wide(shift_a[e, 0] - shift_b[e, 0]),
        wide(shift_a[e, 1] - shift_b[e, 1]),
    )
    return b, c


def left_panel(y, sum_t, tab, per_moment):
    left = cdot(y, block_diag_c(sum_t, tab), NT)
    return left[0] * (1.0 / per_moment), left[1] * (1.0 / per_moment)


def site_matrix(parts, tab):
    both = jnp.concatenate([parts[0][0], parts[0][1], parts[1][0], parts[1][1]], axis=0)

    def fold(full):
        return full[:WIDE] + full[WIDE : 2 * WIDE], full[2 * WIDE : 3 * WIDE] + full[3 * WIDE :]

    re_cos, im_cos = fold(dot(both, tab.wave_cos, NT))
    re_sin, im_sin = fold(dot(both, tab.wave_sin, NT))
    scale = 1.0 / SITES
    return csplit(((re_cos + im_sin) * scale, (im_cos - re_sin) * scale))


def site_phases(site0):
    mom = iota((16, WIDE), 1) >> 4
    return cos_sin(quarter_turns(mom, site0 + (iota((16, WIDE), 0) >> 3)))


def more_rows(known, left, line, phases, matrices):
    cos, sin = phases
    lr, li = jnp.broadcast_to(line[0], (16, WIDE)), jnp.broadcast_to(line[1], (16, WIDE))
    both = (
        jnp.concatenate([left[0], lr * cos - li * sin], axis=0),
        jnp.concatenate([left[1], lr * sin + li * cos], axis=0),
    )
    out = []
    for (top, own), matrix in zip(known, matrices):
        step = cdot(both, matrix)
        out.append(
            (
                (top[0] + step[0][:16], top[1] + step[1][:16]),
                (own[0] + step[0][16:], own[1] + step[1][16:]),
            )
        )
    return out


def first_rows(panels, lines, tab, phases):
    cos, sin = phases
    left_r, left_i = [], []
    for panel, line in zip(panels, lines):
        lr, li = jnp.broadcast_to(line[0], (16, WIDE)), jnp.broadcast_to(line[1], (16, WIDE))
        left_r += [panel[0], lr * cos - li * sin]
        left_i += [panel[1], lr * sin + li * cos]
    rows = 32 * len(panels)
    both = jnp.concatenate(left_r + left_i, axis=0) * (1.0 / SITES)
    by_cos = dot_exact(both, tab.wave_cos, NT)
    by_sin = dot_exact(both, tab.wave_sin, NT)
    real = by_cos[:rows] + by_sin[rows:]
    imag = by_cos[rows:] - by_sin[:rows]
    out = []
    for at in range(0, rows, 32):
        out.append(
            (
                (real[at : at + 16], imag[at : at + 16]),
                (real[at + 16 : at + 32], imag[at + 16 : at + 32]),
            )
        )
    return out


def swap_blocks(x, bit):
    step = 16 * bit
    up = pltpu.roll(x, LANES - step, axis=1)
    if bit == 4:
        return up
    down = pltpu.roll(x, step, axis=1)
    high = ((iota(x.shape, 1) >> 4) & bit) != 0
    return jnp.where(high, down, up)


def all_swaps(x):
    out = {0: x}
    out[4] = swap_blocks(x, 4)
    for at in (0, 4):
        out[at | 2] = swap_blocks(out[at], 2)
    for at in (0, 2, 4, 6):
        out[at | 1] = swap_blocks(out[at], 1)
    return out


def translated(panel):
    low = all_swaps(panel[:, 0:LANES])
    top = all_swaps(panel[:, LANES:WIDE])

    def whole(a, b):
        rows = [jnp.concatenate([a[q], b[q]], axis=1) for q in range(8)]
        rows += [jnp.concatenate([b[q ^ 7], a[q]], axis=1) for q in range(8)]
        return jnp.concatenate(rows, axis=0)

    low_parts = {q: split(v) for q, v in low.items()}
    top_parts = {q: split(v) for q, v in top.items()}
    parts = tuple(
        whole({q: v[p] for q, v in low_parts.items()}, {q: v[p] for q, v in top_parts.items()})
        for p in range(2)
    )
    return whole(low, top), parts


def translated_c(panel):
    real, imag = translated(panel[0]), translated(panel[1])
    return (real[0], imag[0]), (real[1], imag[1])


def rows_stage(start, with_b, with_c, t_parts, tb_parts, tc_parts, rows_tab):
    row = iota((ALPHA, WIDE), 0)
    block = iota((ALPHA, WIDE), 1) >> 4

    def opened(c):
        out = []
        for at in (0, 8):
            ub = jnp.broadcast_to(with_b[c][at : at + 1], (ALPHA, WIDE))
            uc = jnp.broadcast_to(with_c[c][at : at + 1], (ALPHA, WIDE))
            out.append(jnp.where(row == block, uc, jnp.where(row == SITES, ub, 0.0)))
        return jnp.concatenate(out, axis=0)

    begin = (opened(0), opened(1))
    hop_b = cdot(begin, tb_parts)
    hop_c = cdot(begin, tc_parts)
    inner = []
    for c in range(2):
        out = []
        for site in range(2):
            g = jnp.zeros((ALPHA, WIDE), F32)
            for s in range(SITES + 1):
                at = site * ALPHA + s
                pair = rows_tab[s, :, WIDE : WIDE + LANES]
                g = g + jnp.concatenate([pair, pair], axis=1) * hop_b[c][at : at + 1]
                g = g + rows_tab[s, :, 0:WIDE] * hop_c[c][at : at + 1]
            out.append(g)
        inner.append(jnp.concatenate(out, axis=0))
    mean = rows_tab[SITES, SITES : SITES + 1, 0:WIDE]

    def eight(parts):
        return jnp.concatenate([jnp.broadcast_to(p, (8, WIDE)) for p in parts], axis=0)

    ends = tuple(
        eight([inner[c][site * ALPHA + SITES : site * ALPHA + SITES + 1] for site in range(2)])
        for c in range(2)
    )
    by_b = cdot(ends, tb_parts)
    by_c = cdot(tuple(inner), tc_parts)
    z = []
    for c in range(2):
        picked = []
        for site in range(2):
            lines = by_c[c][site * ALPHA : site * ALPHA + ALPHA]
            picked.append(jnp.sum(jnp.where(row == block, lines, 0.0), axis=0, keepdims=True))
        z.append(with_b[c] + with_c[c] * mean - ends[c] + by_b[c] + eight(picked))
    last = cdot(tuple(z), t_parts)
    return start[0] - last[0], start[1] - last[1]


def moment_stage(top_b, top_c, tc_full, tb_parts, tc_parts, x, x_parts, b_wide, c_wide, shift_tab, tab):
    def head(wide):
        return wide[0][:, 0:CHANS], wide[1][:, 0:CHANS]

    b_in, c_in = head(b_wide), head(c_wide)
    small = (
        jnp.concatenate([b_in[0], c_in[0]], axis=0),
        jnp.concatenate([b_in[1], c_in[1]], axis=0),
    )
    lead_b = cdot(small, csplit(top_b))
    lead_c = cdot(small, csplit(top_c))
    bb, cb = [v[0:CHANS] for v in lead_b], [v[CHANS:] for v in lead_b]
    bc, cc = [v[0:CHANS] for v in lead_c], [v[CHANS:] for v in lead_c]
    two = shift_tab[1, 0:1, :]
    mean = shift_tab[1, 0:1, 0:1]
    zero = [bb[c] + mean * (bc[c] + cb[c]) + two * cc[c] for c in range(2)]
    by_b = cdot(tuple(zero), tb_parts)
    by_c = cdot(tuple(jnp.concatenate([bb[c], cb[c]], axis=0) for c in range(2)), tc_parts)

    def scaled(which):
        return split(tc_full[0] * shift_tab[which]), split(tc_full[1] * shift_tab[which])

    pair = cdot(tuple(bc), scaled(0))
    triple = cdot(tuple(cc), scaled(1))
    line = []
    for c in range(2):
        third = by_b[c] + mean * by_c[c][0:CHANS] + two * by_c[c][CHANS:] + pair[c] + triple[c]
        line.append(third - (bb[c] + mean * (cb[c] + bc[c]) + two * cc[c]))
    m_cos = dot_exact(jnp.concatenate(line, axis=0), tab.wave_cos)
    m_sin = dot_exact(jnp.concatenate(line, axis=0), tab.wave_sin)
    m_r = m_cos[:CHANS] - m_sin[CHANS:] + b_wide[0] + mean * c_wide[0]
    m_i = m_sin[:CHANS] + m_cos[CHANS:] + b_wide[1] + mean * c_wide[1]
    d = cdot(cdot(x, block_diag_c((m_r, m_i), tab)), x_parts)
    return -d[0], -d[1]


def correction_stage(d, square, e, kmap, tab):
    onehot = ((iota((WIDE, LANES), 0) >> 4) == kmap[...]).astype(F32).astype(BF16)
    keep = tab.row_block == tab.col_in

    def spread(panel):
        high, low = split(panel)

        def one(part):
            full = jnp.where(keep, tile_rows(part.astype(F32), CHANS), 0.0)
            return dot(full.astype(BF16), onehot)

        return one(high) + one(low)

    dr, di = spread(d[0]), spread(d[1])
    sr, si = square[e, 0].reshape(WIDE, LANES), square[e, 1].reshape(WIDE, LANES)
    re = jnp.sum(dr * sr - di * si, axis=0, keepdims=True)
    im = jnp.sum(dr * si + di * sr, axis=0, keepdims=True)
    return re, im


def coarse_out(x, tab, store):
    fold = (tab.col_block == tab.row_in)
    pick = (iota((WIDE, MOMS), 0) >> 4 == iota((WIDE, MOMS), 1)).astype(F32).astype(BF16)
    high = x.astype(BF16)
    rest = x - high.astype(F32)
    mid = rest.astype(BF16)
    low = (rest - mid.astype(F32)).astype(BF16)
    total = None
    for part in (low, mid, high):
        wide = jnp.broadcast_to(part.astype(F32)[:, None, :], (CHANS, CHANS, WIDE))
        wide = jnp.where(tab.same_in, wide.reshape(WIDE, WIDE), 0.0).astype(BF16)
        piece = dot(wide, pick)
        total = piece if total is None else total + piece
    store(total.reshape(CHANS, CHANS, MOMS))


def gathered_panel(tiles, at):
    top = jnp.concatenate([tiles[at], tiles[at + 1]], axis=1)
    low = jnp.concatenate([tiles[at + 2], tiles[at + 3]], axis=1)
    return jnp.concatenate([top, low], axis=0)


def offsets(outer, inner, torus):
    def hops(step):
        first = min(step[0], outer - step[0])
        return first + (min(step[1], inner - step[1]) if torus else 0.5 * (step[1] > 0))

    steps = [(a, b) for a in range(outer) for b in range(inner) if a or b]
    return sorted(steps, key=lambda step: (-hops(step), step))


class Group:
    def __init__(self, axis, inner, torus):
        self.axis, self.inner = axis, inner
        self.count = lax.axis_size(axis)
        self.outer = self.count // inner
        self.steps = offsets(self.outer, inner, torus)
        self.me = lax.axis_index(axis)

    def peer(self, step):
        first = lax.rem(self.me // self.inner + step[0], self.outer)
        return first * self.inner + lax.rem(lax.rem(self.me, self.inner) + step[1], self.inner)

    def greet(self, barrier):
        for step in self.steps:
            pl.semaphore_signal(
                barrier, inc=1, device_id={self.axis: self.peer(step)}, device_id_type=MESH
            )


class Exchange:
    def __init__(self, group, slots, send, recv):
        self.group, self.slots, self.send, self.recv = group, slots, send, recv

    def copy(self, src, at, number, peer):
        return pltpu.make_async_remote_copy(
            src_ref=src, dst_ref=self.slots.at[at], send_sem=self.send.at[number],
            recv_sem=self.recv.at[at], device_id={self.group.axis: peer}, device_id_type=MESH,
        )

    def start(self, source):
        for number, step in enumerate(self.group.steps):
            peer = self.group.peer(step)
            self.copy(source(peer), self.group.me, number, peer).start()

    def wait(self, source):
        for number, step in enumerate(self.group.steps[::-1]):
            peer = self.group.peer(step)
            self.copy(source(self.group.me), peer, number, peer).wait_recv()

    def drain(self, source):
        for number, step in enumerate(self.group.steps):
            peer = self.group.peer(step)
            self.copy(source(self.group.me), self.group.me, number, peer).wait_send()


def kernel(
    per_moment, n_ka, n_cfg,
    structure_hbm, medium_hbm, kmap_hbm, occupation_hbm, weight, shift_a_hbm, shift_b_hbm,
    coarse_hbm, slots, correction_hbm,
    structure, medium, kmap, occupation, shift_a, shift_b,
    spread, factor, inner, square, panels, rows_tab, shift_tab,
    row, own_rows, outgoing, first, part, total, block, coarse, correction,
    load_sem, out_sem, row_send, row_recv, first_send, first_recv, part_send, part_recv,
    total_send, total_recv, slot_send, slot_recv,
):
    pairs = (
        (kmap_hbm, kmap), (medium_hbm, medium), (structure_hbm, structure),
        (occupation_hbm, occupation), (shift_a_hbm, shift_a), (shift_b_hbm, shift_b),
    )
    loads = [
        pltpu.make_async_copy(source, to, load_sem.at[at]) for at, (source, to) in enumerate(pairs)
    ]
    for load in loads[:3]:
        load.start()
    barrier = pltpu.get_barrier_semaphore()
    by_ka, by_cfg = Group("ka", 4, True), Group("cfg", 2, False)
    by_ka.greet(barrier)
    by_cfg.greet(barrier)
    for load in loads[3:]:
        load.start()
    energies = range(ENERGIES)
    rows_x = Exchange(by_cfg, own_rows, row_send, row_recv)
    first_x = Exchange(by_cfg, first, first_send, first_recv)
    part_x = Exchange(by_ka, part, part_send, part_recv)
    total_x = Exchange(by_cfg, total, total_send, total_recv)
    slot_x = Exchange(by_ka, slots, slot_send, slot_recv)
    ka, cfg = lax.axis_index("ka"), lax.axis_index("cfg")

    def own_row(to):
        return row

    def own_sums(to):
        return outgoing.at[to]

    def own_part(to):
        return part.at[ka]

    def own_total(to):
        return total.at[cfg]

    def own_block(to):
        return block

    loads[0].wait()
    onehot = momentum_matrix(kmap)
    loads[1].wait()
    spread_medium(medium, kmap, spread)
    loads[2].wait()
    for e in energies:
        kpoint_factor(structure, spread, factor, e)
        kpoint_inner(structure, factor, inner, e)

        def write(at, value, e=e):
            outgoing[at, e] = value

        kpoint_sums(inner, onehot, e, write)
    for load in loads[3:]:
        load.wait()
    config_row(occupation, weight, row)
    pl.semaphore_wait(barrier, n_ka + n_cfg - 2)
    first_x.start(own_sums)
    first[cfg] = outgoing[cfg]
    rows_x.start(own_row)
    own_rows[cfg] = row[...]
    kpoint_tau(spread, factor, inner, square, 0)
    kpoint_square(inner, square, 0)
    tab = Tables()
    y = [medium_panels(medium, tab, e) for e in energies]
    wide = [shift_panels(shift_a, shift_b, tab, e) for e in energies]
    rows_x.wait(own_row)
    line = iota((8, LANES), 0)
    group = jnp.zeros((8, LANES), F32)
    for at in range(n_cfg):
        group = group + jnp.where(line == at, own_rows[at], 0.0)
    first_x.wait(own_sums)
    for e in energies:
        value = first[0, e]
        for at in range(1, n_cfg):
            value = value + first[at, e]
        part[ka, e] = value
    part[ka, ENERGIES] = group
    part_x.start(own_part)
    y_b = [cdot(y[e], block_diag_c(wide[e][0], tab)) for e in energies]
    y_c = [cdot(y[e], block_diag_c(wide[e][1], tab)) for e in energies]
    y_all = [
        (block_diag_c(y[e], tab), block_diag_c(y_b[e], tab), block_diag_c(y_c[e], tab))
        for e in energies
    ]
    kpoint_tau(spread, factor, inner, square, 1)
    phases = site_phases(cfg * 2)
    known = []
    for e in energies:
        lines = []
        for at, panel in enumerate((y[e], y_b[e], y_c[e])):
            panels[e, at, 0] = panel[0]
            panels[e, at, 1] = panel[1]
            lines.append(
                (panels[e, at, 0, pl.ds(ka, 1), :], panels[e, at, 1, pl.ds(ka, 1), :])
            )
        known.append(first_rows((y[e], y_b[e], y_c[e]), lines, tab, phases))
    matrices = [[site_matrix(parts, tab) for parts in y_all[0]]]
    part_x.wait(own_part)
    for e in energies:
        value = part[0, e]
        for at in range(1, n_ka):
            value = value + part[at, e]
        total[cfg, e] = value
    total_x.start(own_total)
    configs = jnp.concatenate([part[at, ENERGIES] for at in range(n_ka)], axis=0)
    moment_tables(configs, tab, rows_tab, shift_tab)
    matrices.append([site_matrix(parts, tab) for parts in y_all[1]])
    kpoint_square(inner, square, 1)
    total_x.wait(own_total)
    lefts = []
    for e in energies:
        tiles = [total[at, e] for at in range(n_cfg)]
        sum_t = (gathered_panel(tiles, 0), gathered_panel(tiles, 4))
        lefts.append(left_panel(y[e], sum_t, tab, per_moment))
    rows = []
    for e in energies:
        panels[e, 0, 0] = lefts[e][0]
        panels[e, 0, 1] = lefts[e][1]
        line_e = (panels[e, 0, 0, pl.ds(ka, 1), :], panels[e, 0, 1, pl.ds(ka, 1), :])
        rows.append(more_rows(known[e], lefts[e], line_e, phases, matrices[e]))
    t_all = [translated_c(rows[e][0][0])[1] for e in energies]
    tb_all = [translated_c(rows[e][1][0])[1] for e in energies]
    tc_all = [translated_c(rows[e][2][0]) for e in energies]
    averages = [
        rows_stage(
            rows[e][0][1], rows[e][1][1], rows[e][2][1], t_all[e], tb_all[e], tc_all[e][1], rows_tab
        )
        for e in energies
    ]
    for e in energies:
        out = jnp.zeros((8, LANES), F32)
        for c in range(2):
            for site in range(2):
                for side in range(2):
                    at = c * 4 + site * 2 + side
                    lanes = averages[e][c][
                        site * 8 : site * 8 + 8, side * LANES : side * LANES + LANES
                    ]
                    out = jnp.where(line == at, lanes, out)
        block[e] = out
    slot_x.start(own_block)
    own = pltpu.make_async_copy(block, slots.at[ka], out_sem.at[0])
    own.start()
    found = []
    for e in energies:
        step = cdot(lefts[e], y_all[e][0])
        found.append((y[e][0] + step[0], y[e][1] + step[1]))
    moments = [
        moment_stage(
            rows[e][1][0], rows[e][2][0], tc_all[e][0], tb_all[e], tc_all[e][1], found[e],
            block_diag_c(found[e], tab), wide[e][0], wide[e][1], shift_tab, tab,
        )
        for e in energies
    ]
    for e in energies:
        re, im = correction_stage(moments[e], square, e, kmap, tab)
        correction[e, 0:1, :] = re
        correction[e, 1:2, :] = im
        for c in range(2):

            def store(value, e=e, c=c):
                coarse[e, c] = value

            coarse_out(found[e][c], tab, store)
    leave = [
        pltpu.make_async_copy(coarse, coarse_hbm, out_sem.at[1]),
        pltpu.make_async_copy(correction, correction_hbm, out_sem.at[2]),
    ]
    for copy in leave:
        copy.start()
    slot_x.wait(own_block)
    rows_x.drain(own_row)
    first_x.drain(own_sums)
    part_x.drain(own_part)
    total_x.drain(own_total)
    slot_x.drain(own_block)
    own.wait()
    for copy in leave:
        copy.wait()


def output_kernel(coarse, slots, correction, coarse_to, average, correction_to):
    coarse_to[...] = coarse[...]
    correction_to[...] = correction[...]
    for e in range(ENERGIES):
        for at in range(slots.shape[0]):
            for c in range(2):
                for site in range(2):
                    for side in range(2):
                        of = c * 4 + site * 2 + side
                        to = site * CHANS + at
                        average[e, c, to : to + 1, side * LANES : side * LANES + LANES] = slots[
                            at, e, of : of + 1, :
                        ]


def shape(*dims):
    return jax.ShapeDtypeStruct(dims, F32)


VMEM_SPEC = pl.BlockSpec(memory_space=pltpu.VMEM)
SMEM_SPEC = pl.BlockSpec(memory_space=pltpu.SMEM)


def per_device(medium_t, structure, kmap, occupation, cfg_weight, shift_a, shift_b):
    n_ka, n_cfg = lax.axis_size("ka"), lax.axis_size("cfg")
    per_moment = kmap.shape[0] * n_ka * n_cfg // MOMS
    kmap = kmap.reshape(1, LANES)
    kdims = (ENERGIES, 2, CHANS, CHANS, LANES)
    dma = pltpu.SemaphoreType.DMA

    def vmem(*dims):
        return pltpu.VMEM(dims, F32)

    any_spec = pl.BlockSpec(memory_space=pl.ANY)
    shapes = (
        shape(ENERGIES, 2, CHANS, CHANS, MOMS),
        shape(ENERGIES, 2, 2 * CHANS, WIDE),
        shape(ENERGIES, 2, LANES),
    )
    results = pl.pallas_call(
        functools.partial(kernel, per_moment, n_ka, n_cfg),
        out_shape=(shapes[0], shape(n_ka, ENERGIES, 8, LANES), shapes[2]),
        in_specs=[any_spec] * 4 + [SMEM_SPEC] + [any_spec] * 2,
        out_specs=(any_spec,) * 3,
        scratch_shapes=[
            vmem(*kdims), vmem(ENERGIES, 2, CHANS, CHANS, MOMS),
            pltpu.VMEM((1, LANES), jnp.int32), pltpu.VMEM((1, SITES), jnp.int32),
            vmem(ENERGIES, 2, CHANS, CHANS), vmem(ENERGIES, 2, CHANS, CHANS),
            vmem(*kdims), vmem(*kdims), vmem(*kdims), vmem(*kdims),
            vmem(ENERGIES, 3, 2, CHANS, WIDE),
            vmem(SITES + 1, ALPHA, WIDE + LANES),
            vmem(2, WIDE, WIDE),
            vmem(8, LANES), vmem(n_cfg, 8, LANES),
            vmem(n_cfg, ENERGIES, 8, LANES), vmem(n_cfg, ENERGIES, 8, LANES),
            vmem(n_ka, ENERGIES + 1, 8, LANES),
            vmem(n_cfg, ENERGIES, 8, LANES),
            vmem(ENERGIES, 8, LANES),
            vmem(ENERGIES, 2, CHANS, CHANS, MOMS), vmem(ENERGIES, 2, LANES),
            dma((6,)), dma((3,)),
            dma((n_cfg,)), dma((n_cfg,)),
            dma((n_cfg,)), dma((n_cfg,)),
            dma((n_ka,)), dma((n_ka,)),
            dma((n_cfg,)), dma((n_cfg,)),
            dma((n_ka,)), dma((n_ka,)),
        ],
        compiler_params=pltpu.CompilerParams(
            collective_id=0, has_side_effects=True, vmem_limit_bytes=56 * 1024 * 1024
        ),
    )(structure, medium_t, kmap, occupation, cfg_weight, shift_a, shift_b)
    return pl.pallas_call(
        output_kernel,
        out_shape=shapes,
        in_specs=[VMEM_SPEC] * 3,
        out_specs=(VMEM_SPEC,) * 3,
    )(*results)


def solution(mesh):
    placed = (
        P(),
        P(None, None, None, None, ("ka", "cfg")),
        P(("ka", "cfg")),
        P(("ka", "cfg"), None),
        P(("ka", "cfg")),
        P(),
        P(),
    )
    return jax.shard_map(
        per_device,
        mesh=mesh,
        in_specs=placed,
        out_specs=(P(), P(None, None, "cfg", None), P(None, None, ("ka", "cfg"))),
        check_vma=False,
    )
```

```python
import functools

import jax
import jax.numpy as jnp
from jax import lax
from jax.experimental import pallas as pl
from jax.experimental.pallas import tpu as pltpu
from jax.sharding import PartitionSpec as P

MESH = pl.DeviceIdType.MESH
F32 = jnp.float32
BF16 = jnp.bfloat16
NN = (((1,), (0,)), ((), ()))
NT = (((1,), (1,)), ((), ()))

ENERGIES = 2
SITES = 16
CHANS = 16
MOMS = 16
WIDE = SITES * CHANS
LANES = 128
ALPHA = 24


def split(x):
    high = x.astype(BF16)
    return high, (x - high.astype(F32)).astype(BF16)


def dot(left, right, dims=NN):
    return lax.dot_general(left, right, dims, preferred_element_type=F32)


def dot_exact(x, right, dims=NN):
    high, low = split(x)
    rows = x.shape[0]
    both = dot(jnp.concatenate([high, low], axis=0), right, dims)
    return both[:rows] + both[rows:]


def dot3(x, right, dims=NN):
    high, low = split(x)
    rows = x.shape[0]
    both = dot(jnp.concatenate([high, low], axis=0), right[0], dims)
    return both[:rows] + (both[rows:] + dot(high, right[1], dims))


def cdot(x, right, dims=NN):
    rows = x[0].shape[0]
    both = jnp.concatenate([x[0], x[1]], axis=0)
    by_re = dot3(both, right[0], dims)
    by_im = dot3(both, right[1], dims)
    return by_re[:rows] - by_im[rows:], by_im[:rows] + by_re[rows:]


def csplit(x):
    return split(x[0]), split(x[1])


def iota(shape, axis):
    return lax.broadcasted_iota(jnp.int32, shape, axis)


def tile_rows(x, times):
    return jnp.concatenate([x] * times, axis=0)


def quarter_turns(mom, site):
    half = site >> 3
    x = 2 * ((site >> 2) & 1) + half
    y = 2 * ((site >> 1) & 1) + half
    z = 2 * (site & 1) + half
    return ((mom >> 2) * x + ((mom >> 1) & 1) * y + (mom & 1) * z) & 3


def cos_sin(turns):
    sign = (1 - (turns & 2)).astype(F32)
    odd = (turns & 1) == 1
    return jnp.where(odd, 0.0, sign), jnp.where(odd, sign, 0.0)


def site_sum(first, second):
    carry = (first & second) >> 3
    return (first ^ second) ^ (7 * carry)


class Tables:
    def __init__(self):
        rows, cols = iota((WIDE, WIDE), 0), iota((WIDE, WIDE), 1)
        self.row_block, self.col_block = rows >> 4, cols >> 4
        self.row_in, self.col_in = rows & 15, cols & 15
        self.same_block = self.row_block == self.col_block
        self.same_in = self.row_in == self.col_in
        self.cos, self.sin = cos_sin(quarter_turns(self.col_block, self.row_block))
        self.wave_cos = jnp.where(self.same_in, self.cos, 0.0).astype(BF16)
        self.wave_sin = jnp.where(self.same_in, self.sin, 0.0).astype(BF16)
        small_r, small_c = iota((SITES, WIDE), 0), iota((SITES, WIDE), 1)
        self.pick_in = (small_r == (small_c & 15)).astype(F32).astype(BF16)
        self.pick_block = (small_r == (small_c >> 4)).astype(F32).astype(BF16)


def block_diag(panel, tab):
    def spread(part):
        return jnp.where(tab.same_block, tile_rows(part.astype(F32), SITES), 0.0).astype(BF16)

    high, low = split(panel)
    return spread(high), spread(low)


def block_diag_c(panel, tab):
    return block_diag(panel[0], tab), block_diag(panel[1], tab)


HELD_ROWS = 8


def kpoint_mul(store, left, right):
    def body(step, carry):
        start = step * HELD_ROWS
        zero = jnp.zeros((CHANS, LANES), F32)
        p, q, t = [zero] * HELD_ROWS, [zero] * HELD_ROWS, [zero] * HELD_ROWS
        for b in range(CHANS):
            rr, ri = right[0, b], right[1, b]
            less, more = ri - rr, rr + ri
            for j in range(HELD_ROWS):
                lr = left[0, start + j, pl.ds(b, 1), :]
                li = left[1, start + j, pl.ds(b, 1), :]
                p[j] = p[j] + (lr + li) * rr
                q[j] = q[j] + lr * less
                t[j] = t[j] + li * more
        for j in range(HELD_ROWS):
            store(start + j, p[j] - t[j], p[j] + q[j])
        return carry

    lax.fori_loop(0, CHANS // HELD_ROWS, body, 0)


def spread_medium(medium, kmap, spread):
    onehot = (iota((MOMS, LANES), 0) == kmap[...]).astype(F32).astype(BF16)
    for e in range(ENERGIES):
        for c in range(2):
            flat = medium[e, c].reshape(WIDE, MOMS)
            spread[e, c] = dot_exact(flat, onehot).reshape(CHANS, CHANS, LANES)


def kpoint_factor(structure, spread, factor, e):
    f = factor.at[e]

    def put(a, re, im):
        f[0, a] = re
        f[1, a] = im

    kpoint_mul(put, spread.at[e], structure.at[e])


def kpoint_inner(structure, factor, inner, e):
    g, h = structure.at[e], inner.at[e]

    def put(a, re, im):
        h[0, a] = g[0, a] + re
        h[1, a] = g[1, a] + im

    kpoint_mul(put, g, factor.at[e])


def momentum_matrix(kmap):
    onehot = jnp.transpose(((iota((WIDE, LANES), 0) >> 4) == kmap[...]).astype(F32)).astype(BF16)
    return jnp.concatenate([onehot, onehot], axis=0)


def kpoint_sums(inner, onehot, e, write_tile):
    keep = (iota((WIDE, WIDE), 0) >> 4) == (iota((WIDE, WIDE), 1) & 15)
    for c in range(2):
        flat = inner[e, c].reshape(WIDE, LANES)
        parts = jnp.concatenate(split(flat), axis=1)
        by_mom = jnp.where(keep, dot(parts, onehot), 0.0)
        panel = jnp.sum(by_mom.reshape(CHANS, CHANS, WIDE), axis=0)
        for half in range(2):
            for side in range(2):
                write_tile(
                    c * 4 + half * 2 + side,
                    panel[half * 8 : half * 8 + 8, side * LANES : side * LANES + LANES],
                )


def kpoint_tau(spread, factor, tau, work, e):
    y, f, t, s = spread.at[e], factor.at[e], tau.at[e], work.at[e]

    def put_q(a, re, im):
        s[0, a] = f[0, a] + re
        s[1, a] = f[1, a] + im

    def put_t(a, re, im):
        t[0, a] = y[0, a] + re
        t[1, a] = y[1, a] + im

    kpoint_mul(put_q, f, f)
    kpoint_mul(put_t, s, y)


def kpoint_square(tau, square, e):
    t, s = tau.at[e], square.at[e]

    def put(a, re, im):
        s[0, a] = re
        s[1, a] = im

    kpoint_mul(put, t, t)


def config_row(occupation, weight, row):
    lane = iota((8, LANES), 1)
    row[...] = jnp.where(lane == SITES, 1.0, 0.0) + jnp.where(
        lane == SITES + 1, weight[0], 0.0
    )
    row[:, 0:SITES] = jnp.broadcast_to(occupation[...].astype(F32), (8, SITES))


def moment_tables(configs, tab, rows_tab, shift_tab):
    turned = jnp.transpose(configs)
    count = turned[0:ALPHA]
    weight = turned[SITES + 1 : SITES + 2]
    weight = weight / jnp.sum(weight, axis=1, keepdims=True)
    live = iota((ALPHA, LANES), 0) <= SITES
    count = jnp.where(live, count, 0.0)
    weighted = count * weight
    flat = configs.astype(BF16)
    lane_r, lane_c = iota((LANES, WIDE), 0), iota((LANES, WIDE), 1)
    pick = (lane_r == (lane_c >> 4)).astype(F32).astype(BF16)
    wide = dot(flat, pick).astype(BF16)
    ones = jnp.ones((LANES, LANES), BF16)
    for s in range(SITES + 1):
        product = weighted * count[s : s + 1]
        rows_tab[s, :, 0:WIDE] = dot_exact(product, wide)
        rows_tab[s, :, WIDE : WIDE + LANES] = dot_exact(product, ones)
    r, c = iota((WIDE, LANES), 0), iota((WIDE, LANES), 1)
    move = (site_sum(r >> 4, r & 15) == c).astype(F32).astype(BF16)
    moved = dot(move, flat, NT)
    moved_b = moved.astype(BF16)
    own = dot(((r >> 4) == c).astype(F32).astype(BF16), flat, NT)
    base = moved * (weight * (1.0 / SITES))
    fold = (tab.row_in == tab.col_block).astype(F32).astype(BF16)
    for which, left in ((0, base), (1, base * own)):
        full = dot_exact(left, moved_b, NT)
        kept = jnp.where(tab.same_block, full, 0.0)
        small = jnp.sum(kept.reshape(SITES, SITES, WIDE), axis=0)
        lanes = dot_exact(small, fold)
        shift_tab[which] = jnp.broadcast_to(
            lanes[:, None, :], (SITES, CHANS, WIDE)
        ).reshape(WIDE, WIDE)


def medium_panels(medium, tab, e):
    out = []
    for c in range(2):
        flat = medium[e, c].reshape(WIDE, MOMS)
        pick = ((iota((MOMS, WIDE), 1) >> 4) == iota((MOMS, WIDE), 0)).astype(F32).astype(BF16)
        by_mom = jnp.where(tab.same_in, dot_exact(flat, pick), 0.0)
        out.append(jnp.sum(by_mom.reshape(CHANS, CHANS, WIDE), axis=1))
    return tuple(out)


def shift_panels(shift_a, shift_b, tab, e):
    def wide(x):
        return dot_exact(x, tab.pick_in)

    b = (wide(shift_b[e, 0]), wide(shift_b[e, 1]))
    c = (
        wide(shift_a[e, 0] - shift_b[e, 0]),
        wide(shift_a[e, 1] - shift_b[e, 1]),
    )
    return b, c


def left_panel(y, sum_t, tab, per_moment):
    left = cdot(y, block_diag_c(sum_t, tab), NT)
    return left[0] * (1.0 / per_moment), left[1] * (1.0 / per_moment)


def site_matrix(parts, tab):
    both = jnp.concatenate([parts[0][0], parts[0][1], parts[1][0], parts[1][1]], axis=0)

    def fold(full):
        return full[:WIDE] + full[WIDE : 2 * WIDE], full[2 * WIDE : 3 * WIDE] + full[3 * WIDE :]

    re_cos, im_cos = fold(dot(both, tab.wave_cos, NT))
    re_sin, im_sin = fold(dot(both, tab.wave_sin, NT))
    scale = 1.0 / SITES
    return csplit(((re_cos + im_sin) * scale, (im_cos - re_sin) * scale))


def site_phases(site0):
    mom = iota((16, WIDE), 1) >> 4
    return cos_sin(quarter_turns(mom, site0 + (iota((16, WIDE), 0) >> 3)))


def more_rows(known, left, line, phases, matrices):
    cos, sin = phases
    lr, li = jnp.broadcast_to(line[0], (16, WIDE)), jnp.broadcast_to(line[1], (16, WIDE))
    both = (
        jnp.concatenate([left[0], lr * cos - li * sin], axis=0),
        jnp.concatenate([left[1], lr * sin + li * cos], axis=0),
    )
    out = []
    for (top, own), matrix in zip(known, matrices):
        step = cdot(both, matrix)
        out.append(
            (
                (top[0] + step[0][:16], top[1] + step[1][:16]),
                (own[0] + step[0][16:], own[1] + step[1][16:]),
            )
        )
    return out


def first_rows(panels, lines, tab, phases):
    cos, sin = phases
    left_r, left_i = [], []
    for panel, line in zip(panels, lines):
        lr, li = jnp.broadcast_to(line[0], (16, WIDE)), jnp.broadcast_to(line[1], (16, WIDE))
        left_r += [panel[0], lr * cos - li * sin]
        left_i += [panel[1], lr * sin + li * cos]
    rows = 32 * len(panels)
    both = jnp.concatenate(left_r + left_i, axis=0) * (1.0 / SITES)
    by_cos = dot_exact(both, tab.wave_cos, NT)
    by_sin = dot_exact(both, tab.wave_sin, NT)
    real = by_cos[:rows] + by_sin[rows:]
    imag = by_cos[rows:] - by_sin[:rows]
    out = []
    for at in range(0, rows, 32):
        out.append(
            (
                (real[at : at + 16], imag[at : at + 16]),
                (real[at + 16 : at + 32], imag[at + 16 : at + 32]),
            )
        )
    return out


def swap_blocks(x, bit):
    step = 16 * bit
    up = pltpu.roll(x, LANES - step, axis=1)
    if bit == 4:
        return up
    down = pltpu.roll(x, step, axis=1)
    high = ((iota(x.shape, 1) >> 4) & bit) != 0
    return jnp.where(high, down, up)


def all_swaps(x):
    out = {0: x}
    out[4] = swap_blocks(x, 4)
    for at in (0, 4):
        out[at | 2] = swap_blocks(out[at], 2)
    for at in (0, 2, 4, 6):
        out[at | 1] = swap_blocks(out[at], 1)
    return out


def translated(panel):
    low = all_swaps(panel[:, 0:LANES])
    top = all_swaps(panel[:, LANES:WIDE])

    def whole(a, b):
        rows = [jnp.concatenate([a[q], b[q]], axis=1) for q in range(8)]
        rows += [jnp.concatenate([b[q ^ 7], a[q]], axis=1) for q in range(8)]
        return jnp.concatenate(rows, axis=0)

    low_parts = {q: split(v) for q, v in low.items()}
    top_parts = {q: split(v) for q, v in top.items()}
    parts = tuple(
        whole({q: v[p] for q, v in low_parts.items()}, {q: v[p] for q, v in top_parts.items()})
        for p in range(2)
    )
    return whole(low, top), parts


def translated_c(panel):
    real, imag = translated(panel[0]), translated(panel[1])
    return (real[0], imag[0]), (real[1], imag[1])


def rows_stage(start, with_b, with_c, t_parts, tb_parts, tc_parts, rows_tab):
    row = iota((ALPHA, WIDE), 0)
    block = iota((ALPHA, WIDE), 1) >> 4

    def opened(c):
        out = []
        for at in (0, 8):
            ub = jnp.broadcast_to(with_b[c][at : at + 1], (ALPHA, WIDE))
            uc = jnp.broadcast_to(with_c[c][at : at + 1], (ALPHA, WIDE))
            out.append(jnp.where(row == block, uc, jnp.where(row == SITES, ub, 0.0)))
        return jnp.concatenate(out, axis=0)

    begin = (opened(0), opened(1))
    hop_b = cdot(begin, tb_parts)
    hop_c = cdot(begin, tc_parts)
    inner = []
    for c in range(2):
        out = []
        for site in range(2):
            g = jnp.zeros((ALPHA, WIDE), F32)
            for s in range(SITES + 1):
                at = site * ALPHA + s
                pair = rows_tab[s, :, WIDE : WIDE + LANES]
                g = g + jnp.concatenate([pair, pair], axis=1) * hop_b[c][at : at + 1]
                g = g + rows_tab[s, :, 0:WIDE] * hop_c[c][at : at + 1]
            out.append(g)
        inner.append(jnp.concatenate(out, axis=0))
    mean = rows_tab[SITES, SITES : SITES + 1, 0:WIDE]

    def eight(parts):
        return jnp.concatenate([jnp.broadcast_to(p, (8, WIDE)) for p in parts], axis=0)

    ends = tuple(
        eight([inner[c][site * ALPHA + SITES : site * ALPHA + SITES + 1] for site in range(2)])
        for c in range(2)
    )
    by_b = cdot(ends, tb_parts)
    by_c = cdot(tuple(inner), tc_parts)
    z = []
    for c in range(2):
        picked = []
        for site in range(2):
            lines = by_c[c][site * ALPHA : site * ALPHA + ALPHA]
            picked.append(jnp.sum(jnp.where(row == block, lines, 0.0), axis=0, keepdims=True))
        z.append(with_b[c] + with_c[c] * mean - ends[c] + by_b[c] + eight(picked))
    last = cdot(tuple(z), t_parts)
    return start[0] - last[0], start[1] - last[1]


def moment_stage(top_b, top_c, tc_full, tb_parts, tc_parts, x, x_parts, b_wide, c_wide, shift_tab, tab):
    def head(wide):
        return wide[0][:, 0:CHANS], wide[1][:, 0:CHANS]

    b_in, c_in = head(b_wide), head(c_wide)
    small = (
        jnp.concatenate([b_in[0], c_in[0]], axis=0),
        jnp.concatenate([b_in[1], c_in[1]], axis=0),
    )
    lead_b = cdot(small, csplit(top_b))
    lead_c = cdot(small, csplit(top_c))
    bb, cb = [v[0:CHANS] for v in lead_b], [v[CHANS:] for v in lead_b]
    bc, cc = [v[0:CHANS] for v in lead_c], [v[CHANS:] for v in lead_c]
    two = shift_tab[1, 0:1, :]
    mean = shift_tab[1, 0:1, 0:1]
    zero = [bb[c] + mean * (bc[c] + cb[c]) + two * cc[c] for c in range(2)]
    by_b = cdot(tuple(zero), tb_parts)
    by_c = cdot(tuple(jnp.concatenate([bb[c], cb[c]], axis=0) for c in range(2)), tc_parts)

    def scaled(which):
        return split(tc_full[0] * shift_tab[which]), split(tc_full[1] * shift_tab[which])

    pair = cdot(tuple(bc), scaled(0))
    triple = cdot(tuple(cc), scaled(1))
    line = []
    for c in range(2):
        third = by_b[c] + mean * by_c[c][0:CHANS] + two * by_c[c][CHANS:] + pair[c] + triple[c]
        line.append(third - (bb[c] + mean * (cb[c] + bc[c]) + two * cc[c]))
    m_cos = dot_exact(jnp.concatenate(line, axis=0), tab.wave_cos)
    m_sin = dot_exact(jnp.concatenate(line, axis=0), tab.wave_sin)
    m_r = m_cos[:CHANS] - m_sin[CHANS:] + b_wide[0] + mean * c_wide[0]
    m_i = m_sin[:CHANS] + m_cos[CHANS:] + b_wide[1] + mean * c_wide[1]
    d = cdot(cdot(x, block_diag_c((m_r, m_i), tab)), x_parts)
    return -d[0], -d[1]


def correction_stage(d, square, e, kmap, tab):
    onehot = ((iota((WIDE, LANES), 0) >> 4) == kmap[...]).astype(F32).astype(BF16)
    keep = tab.row_block == tab.col_in

    def spread(panel):
        high, low = split(panel)

        def one(part):
            full = jnp.where(keep, tile_rows(part.astype(F32), CHANS), 0.0)
            return dot(full.astype(BF16), onehot)

        return one(high) + one(low)

    dr, di = spread(d[0]), spread(d[1])
    sr, si = square[e, 0].reshape(WIDE, LANES), square[e, 1].reshape(WIDE, LANES)
    re = jnp.sum(dr * sr - di * si, axis=0, keepdims=True)
    im = jnp.sum(dr * si + di * sr, axis=0, keepdims=True)
    return re, im


def coarse_out(x, tab, store):
    fold = (tab.col_block == tab.row_in)
    pick = (iota((WIDE, MOMS), 0) >> 4 == iota((WIDE, MOMS), 1)).astype(F32).astype(BF16)
    high = x.astype(BF16)
    rest = x - high.astype(F32)
    mid = rest.astype(BF16)
    low = (rest - mid.astype(F32)).astype(BF16)
    total = None
    for part in (low, mid, high):
        wide = jnp.broadcast_to(part.astype(F32)[:, None, :], (CHANS, CHANS, WIDE))
        wide = jnp.where(tab.same_in, wide.reshape(WIDE, WIDE), 0.0).astype(BF16)
        piece = dot(wide, pick)
        total = piece if total is None else total + piece
    store(total.reshape(CHANS, CHANS, MOMS))


def gathered_panel(tiles, at):
    top = jnp.concatenate([tiles[at], tiles[at + 1]], axis=1)
    low = jnp.concatenate([tiles[at + 2], tiles[at + 3]], axis=1)
    return jnp.concatenate([top, low], axis=0)


def offsets(outer, inner, torus):
    def hops(step):
        first = min(step[0], outer - step[0])
        return first + (min(step[1], inner - step[1]) if torus else 0.5 * (step[1] > 0))

    steps = [(a, b) for a in range(outer) for b in range(inner) if a or b]
    return sorted(steps, key=lambda step: (-hops(step), step))


class Group:
    def __init__(self, axis, inner, torus):
        self.axis, self.inner = axis, inner
        self.count = lax.axis_size(axis)
        self.outer = self.count // inner
        self.steps = offsets(self.outer, inner, torus)
        self.me = lax.axis_index(axis)

    def peer(self, step):
        first = lax.rem(self.me // self.inner + step[0], self.outer)
        return first * self.inner + lax.rem(lax.rem(self.me, self.inner) + step[1], self.inner)

    def greet(self, barrier):
        for step in self.steps:
            pl.semaphore_signal(
                barrier, inc=1, device_id={self.axis: self.peer(step)}, device_id_type=MESH
            )


class Exchange:
    def __init__(self, group, slots, send, recv):
        self.group, self.slots, self.send, self.recv = group, slots, send, recv

    def copy(self, src, at, number, peer):
        return pltpu.make_async_remote_copy(
            src_ref=src, dst_ref=self.slots.at[at], send_sem=self.send.at[number],
            recv_sem=self.recv.at[at], device_id={self.group.axis: peer}, device_id_type=MESH,
        )

    def start(self, source):
        for number, step in enumerate(self.group.steps):
            peer = self.group.peer(step)
            self.copy(source(peer), self.group.me, number, peer).start()

    def wait(self, source):
        for number, step in enumerate(self.group.steps[::-1]):
            peer = self.group.peer(step)
            self.copy(source(self.group.me), peer, number, peer).wait_recv()

    def drain(self, source):
        for number, step in enumerate(self.group.steps):
            peer = self.group.peer(step)
            self.copy(source(self.group.me), self.group.me, number, peer).wait_send()


def kernel(
    per_moment, n_ka, n_cfg,
    structure_hbm, medium_hbm, kmap_hbm, occupation_hbm, weight, shift_a_hbm, shift_b_hbm,
    coarse_hbm, slots, correction_hbm,
    structure, medium, kmap, occupation, shift_a, shift_b,
    spread, factor, inner, square, panels, rows_tab, shift_tab,
    row, own_rows, outgoing, first, part, total, block, coarse, correction,
    load_sem, out_sem, row_send, row_recv, first_send, first_recv, part_send, part_recv,
    total_send, total_recv, slot_send, slot_recv,
):
    pairs = (
        (kmap_hbm, kmap), (medium_hbm, medium), (structure_hbm, structure),
        (occupation_hbm, occupation), (shift_a_hbm, shift_a), (shift_b_hbm, shift_b),
    )
    loads = [
        pltpu.make_async_copy(source, to, load_sem.at[at]) for at, (source, to) in enumerate(pairs)
    ]
    for load in loads[:3]:
        load.start()
    barrier = pltpu.get_barrier_semaphore()
    by_ka, by_cfg = Group("ka", 4, True), Group("cfg", 2, False)
    by_ka.greet(barrier)
    by_cfg.greet(barrier)
    for load in loads[3:]:
        load.start()
    energies = range(ENERGIES)
    rows_x = Exchange(by_cfg, own_rows, row_send, row_recv)
    first_x = Exchange(by_cfg, first, first_send, first_recv)
    part_x = Exchange(by_ka, part, part_send, part_recv)
    total_x = Exchange(by_cfg, total, total_send, total_recv)
    slot_x = Exchange(by_ka, slots, slot_send, slot_recv)
    ka, cfg = lax.axis_index("ka"), lax.axis_index("cfg")

    def own_row(to):
        return row

    def own_sums(to):
        return outgoing.at[to]

    def own_part(to):
        return part.at[ka]

    def own_total(to):
        return total.at[cfg]

    def own_block(to):
        return block

    loads[0].wait()
    onehot = momentum_matrix(kmap)
    loads[1].wait()
    spread_medium(medium, kmap, spread)
    loads[2].wait()
    for e in energies:
        kpoint_factor(structure, spread, factor, e)
        kpoint_inner(structure, factor, inner, e)

        def write(at, value, e=e):
            outgoing[at, e] = value

        kpoint_sums(inner, onehot, e, write)
    for load in loads[3:]:
        load.wait()
    config_row(occupation, weight, row)
    pl.semaphore_wait(barrier, n_ka + n_cfg - 2)
    first_x.start(own_sums)
    first[cfg] = outgoing[cfg]
    rows_x.start(own_row)
    own_rows[cfg] = row[...]
    kpoint_tau(spread, factor, inner, square, 0)
    kpoint_square(inner, square, 0)
    tab = Tables()
    y = [medium_panels(medium, tab, e) for e in energies]
    wide = [shift_panels(shift_a, shift_b, tab, e) for e in energies]
    rows_x.wait(own_row)
    line = iota((8, LANES), 0)
    group = jnp.zeros((8, LANES), F32)
    for at in range(n_cfg):
        group = group + jnp.where(line == at, own_rows[at], 0.0)
    first_x.wait(own_sums)
    for e in energies:
        value = first[0, e]
        for at in range(1, n_cfg):
            value = value + first[at, e]
        part[ka, e] = value
    part[ka, ENERGIES] = group
    part_x.start(own_part)
    y_b = [cdot(y[e], block_diag_c(wide[e][0], tab)) for e in energies]
    y_c = [cdot(y[e], block_diag_c(wide[e][1], tab)) for e in energies]
    y_all = [
        (block_diag_c(y[e], tab), block_diag_c(y_b[e], tab), block_diag_c(y_c[e], tab))
        for e in energies
    ]
    kpoint_tau(spread, factor, inner, square, 1)
    phases = site_phases(cfg * 2)
    known = []
    for e in energies:
        lines = []
        for at, panel in enumerate((y[e], y_b[e], y_c[e])):
            panels[e, at, 0] = panel[0]
            panels[e, at, 1] = panel[1]
            lines.append(
                (panels[e, at, 0, pl.ds(ka, 1), :], panels[e, at, 1, pl.ds(ka, 1), :])
            )
        known.append(first_rows((y[e], y_b[e], y_c[e]), lines, tab, phases))
    matrices = [[site_matrix(parts, tab) for parts in y_all[0]]]
    part_x.wait(own_part)
    for e in energies:
        value = part[0, e]
        for at in range(1, n_ka):
            value = value + part[at, e]
        total[cfg, e] = value
    total_x.start(own_total)
    configs = jnp.concatenate([part[at, ENERGIES] for at in range(n_ka)], axis=0)
    moment_tables(configs, tab, rows_tab, shift_tab)
    matrices.append([site_matrix(parts, tab) for parts in y_all[1]])
    kpoint_square(inner, square, 1)
    total_x.wait(own_total)
    lefts = []
    for e in energies:
        tiles = [total[at, e] for at in range(n_cfg)]
        sum_t = (gathered_panel(tiles, 0), gathered_panel(tiles, 4))
        lefts.append(left_panel(y[e], sum_t, tab, per_moment))
    rows = []
    for e in energies:
        panels[e, 0, 0] = lefts[e][0]
        panels[e, 0, 1] = lefts[e][1]
        line_e = (panels[e, 0, 0, pl.ds(ka, 1), :], panels[e, 0, 1, pl.ds(ka, 1), :])
        rows.append(more_rows(known[e], lefts[e], line_e, phases, matrices[e]))
    t_all = [translated_c(rows[e][0][0])[1] for e in energies]
    tb_all = [translated_c(rows[e][1][0])[1] for e in energies]
    tc_all = [translated_c(rows[e][2][0]) for e in energies]
    averages = [
        rows_stage(
            rows[e][0][1], rows[e][1][1], rows[e][2][1], t_all[e], tb_all[e], tc_all[e][1], rows_tab
        )
        for e in energies
    ]
    for e in energies:
        out = jnp.zeros((8, LANES), F32)
        for c in range(2):
            for site in range(2):
                for side in range(2):
                    at = c * 4 + site * 2 + side
                    lanes = averages[e][c][
                        site * 8 : site * 8 + 8, side * LANES : side * LANES + LANES
                    ]
                    out = jnp.where(line == at, lanes, out)
        block[e] = out
    slot_x.start(own_block)
    own = pltpu.make_async_copy(block, slots.at[ka], out_sem.at[0])
    own.start()
    found = []
    for e in energies:
        step = cdot(lefts[e], y_all[e][0])
        found.append((y[e][0] + step[0], y[e][1] + step[1]))
    moments = [
        moment_stage(
            rows[e][1][0], rows[e][2][0], tc_all[e][0], tb_all[e], tc_all[e][1], found[e],
            block_diag_c(found[e], tab), wide[e][0], wide[e][1], shift_tab, tab,
        )
        for e in energies
    ]
    for e in energies:
        re, im = correction_stage(moments[e], square, e, kmap, tab)
        correction[e, 0:1, :] = re
        correction[e, 1:2, :] = im
        for c in range(2):

            def store(value, e=e, c=c):
                coarse[e, c] = value

            coarse_out(found[e][c], tab, store)
    leave = [
        pltpu.make_async_copy(coarse, coarse_hbm, out_sem.at[1]),
        pltpu.make_async_copy(correction, correction_hbm, out_sem.at[2]),
    ]
    for copy in leave:
        copy.start()
    slot_x.wait(own_block)
    rows_x.drain(own_row)
    first_x.drain(own_sums)
    part_x.drain(own_part)
    total_x.drain(own_total)
    slot_x.drain(own_block)
    own.wait()
    for copy in leave:
        copy.wait()


def output_kernel(
    coarse_from, slots_from, correction_from, coarse_to, average_to, correction_to,
    coarse, slots, correction, average, sem,
):
    loads = [
        pltpu.make_async_copy(slots_from, slots, sem.at[0]),
        pltpu.make_async_copy(coarse_from, coarse, sem.at[1]),
        pltpu.make_async_copy(correction_from, correction, sem.at[2]),
    ]
    stores = [
        pltpu.make_async_copy(average, average_to, sem.at[3]),
        pltpu.make_async_copy(coarse, coarse_to, sem.at[4]),
        pltpu.make_async_copy(correction, correction_to, sem.at[5]),
    ]
    for load in loads:
        load.start()
    loads[0].wait()
    for e in range(ENERGIES):
        for at in range(slots.shape[0]):
            for c in range(2):
                for site in range(2):
                    for side in range(2):
                        of = c * 4 + site * 2 + side
                        to = site * CHANS + at
                        average[e, c, to : to + 1, side * LANES : side * LANES + LANES] = slots[
                            at, e, of : of + 1, :
                        ]
    stores[0].start()
    for load, store in zip(loads[1:], stores[1:]):
        load.wait()
        store.start()
    for store in stores:
        store.wait()


def shape(*dims):
    return jax.ShapeDtypeStruct(dims, F32)


VMEM_SPEC = pl.BlockSpec(memory_space=pltpu.VMEM)
SMEM_SPEC = pl.BlockSpec(memory_space=pltpu.SMEM)


def per_device(medium_t, structure, kmap, occupation, cfg_weight, shift_a, shift_b):
    n_ka, n_cfg = lax.axis_size("ka"), lax.axis_size("cfg")
    per_moment = kmap.shape[0] * n_ka * n_cfg // MOMS
    kmap = kmap.reshape(1, LANES)
    kdims = (ENERGIES, 2, CHANS, CHANS, LANES)
    dma = pltpu.SemaphoreType.DMA

    def vmem(*dims):
        return pltpu.VMEM(dims, F32)

    any_spec = pl.BlockSpec(memory_space=pl.ANY)
    shapes = (
        shape(ENERGIES, 2, CHANS, CHANS, MOMS),
        shape(ENERGIES, 2, 2 * CHANS, WIDE),
        shape(ENERGIES, 2, LANES),
    )
    results = pl.pallas_call(
        functools.partial(kernel, per_moment, n_ka, n_cfg),
        out_shape=(shapes[0], shape(n_ka, ENERGIES, 8, LANES), shapes[2]),
        in_specs=[any_spec] * 4 + [SMEM_SPEC] + [any_spec] * 2,
        out_specs=(any_spec,) * 3,
        scratch_shapes=[
            vmem(*kdims), vmem(ENERGIES, 2, CHANS, CHANS, MOMS),
            pltpu.VMEM((1, LANES), jnp.int32), pltpu.VMEM((1, SITES), jnp.int32),
            vmem(ENERGIES, 2, CHANS, CHANS), vmem(ENERGIES, 2, CHANS, CHANS),
            vmem(*kdims), vmem(*kdims), vmem(*kdims), vmem(*kdims),
            vmem(ENERGIES, 3, 2, CHANS, WIDE),
            vmem(SITES + 1, ALPHA, WIDE + LANES),
            vmem(2, WIDE, WIDE),
            vmem(8, LANES), vmem(n_cfg, 8, LANES),
            vmem(n_cfg, ENERGIES, 8, LANES), vmem(n_cfg, ENERGIES, 8, LANES),
            vmem(n_ka, ENERGIES + 1, 8, LANES),
            vmem(n_cfg, ENERGIES, 8, LANES),
            vmem(ENERGIES, 8, LANES),
            vmem(ENERGIES, 2, CHANS, CHANS, MOMS), vmem(ENERGIES, 2, LANES),
            dma((6,)), dma((3,)),
            dma((n_cfg,)), dma((n_cfg,)),
            dma((n_cfg,)), dma((n_cfg,)),
            dma((n_ka,)), dma((n_ka,)),
            dma((n_cfg,)), dma((n_cfg,)),
            dma((n_ka,)), dma((n_ka,)),
        ],
        compiler_params=pltpu.CompilerParams(
            collective_id=0, has_side_effects=True, vmem_limit_bytes=56 * 1024 * 1024
        ),
    )(structure, medium_t, kmap, occupation, cfg_weight, shift_a, shift_b)
    return pl.pallas_call(
        output_kernel,
        out_shape=shapes,
        in_specs=[any_spec] * 3,
        out_specs=(any_spec,) * 3,
        scratch_shapes=[
            vmem(ENERGIES, 2, CHANS, CHANS, MOMS), vmem(n_ka, ENERGIES, 8, LANES),
            vmem(ENERGIES, 2, LANES), vmem(ENERGIES, 2, 2 * CHANS, WIDE), dma((6,)),
        ],
        compiler_params=pltpu.CompilerParams(vmem_limit_bytes=56 * 1024 * 1024),
    )(*results)


def solution(mesh):
    placed = (
        P(),
        P(None, None, None, None, ("ka", "cfg")),
        P(("ka", "cfg")),
        P(("ka", "cfg"), None),
        P(("ka", "cfg")),
        P(),
        P(),
    )
    return jax.shard_map(
        per_device,
        mesh=mesh,
        in_specs=placed,
        out_specs=(P(), P(None, None, "cfg", None), P(None, None, ("ka", "cfg"))),
        check_vma=False,
    )
```
